256 devices in a mesh: sec: 2 (over z_hi), tile: 32 (over x, z_lo, core), tp: 4 (over y).
Axes of the slice: x: 4, y: 4, z: 8 (z_hi: 2, z_lo: 4; z = z_hi * 4 + z_lo), core: 2. Of those that a mesh axis runs over, the one named last changes fastest.
Arguments:
- global_state: bfloat16 [32768, 1024], P(('sec', 'tile')), may hold values from -60 to 60
- band_codes: int32 [64], P(('sec', 'tile')), may hold values from 0 to 999999
- norm_gain: bfloat16 [1024], replicated, may hold values from 0.5 to 1.5
- w_query: bfloat16 [1024, 1024], P(None, 'tp'), may hold values from -32 to 32
- w_key: bfloat16 [1024, 1024], P(None, 'tp'), may hold values from -1 to 1
- w_value: bfloat16 [1024, 1024], P(None, 'tp'), may hold values from -0.1875 to 0.1875
- w_out: bfloat16 [1024, 1024], P('tp'), may hold values from -2.390625 to 2.390625
- reg_state: bfloat16 [2048, 16, 512], P(('sec', 'tile', 'tp')), may hold values from -6 to 6
- src_band: int32 [2048, 16, 1], P(('sec', 'tile', 'tp')), may hold values from 0 to 63; in each aligned block of 128 rows (0 to 127, 128 to 255, ..., all dimensions but the last counted through in order) at most 4 rows name the same one
- src_tok: int32 [2048, 16], P(('sec', 'tile', 'tp')), may hold values from 0 to 127
- w_bound: bfloat16 [1024, 512], replicated, may hold values from -0.1875 to 0.1875
- conv_w: bfloat16 [9, 512, 512], replicated, may hold values from -0.09375 to 0.09375
Outputs:
- global_out: bfloat16 [3, 32768, 1024], P(None, ('sec', 'tile', 'tp'))
- regional_out: bfloat16 [3, 2048, 16, 512], P(None, ('sec', 'tile', 'tp'))
The draws below stay inside these ranges and needn't reach their ends.
Inputs may be any that keep to these rules, and one draw needn't show every extreme that they name: `src_band`: among the cells of one device (aligned blocks of 128 cells in the order column, then row), no band is named by more than 4 cells.
All inputs are finite; a program needn't handle non-finite values.
Results may differ from the reference program's by a relative error of at most 0.02.
Values may be sent and summed in bfloat16 or wider, within the bound.
No kernel may reach another device: no remote copies, remote signals or barrier semaphores. Data moves between devices by JAX's collectives and lax.ppermute only.
A program may use at most 128 MiB of HBM per device.

```python
import math
import jax
import jax.numpy as jnp
import numpy as np
from jax import lax

D = 1024
HEADS = 16
C = 512
GT = 512
RY = 16
CC = 8
HD = 64
NB = 64
NTOK = 32768
HALO = 256
NCOLS = 2048
NCELL = 128
MOST = 4
N_TP = 4


def draw_global_state(key, part):
    first, second, third = jax.random.split(key, 3)
    col_scale = jnp.exp(jax.random.uniform(second, (1, D), jnp.float32) * math.log(10.0))
    row_scale = jnp.exp(jax.random.uniform(third, (NTOK, 1), jnp.float32) * math.log(10.0))
    basis = jnp.clip(jax.random.normal(first, (NTOK, D), jnp.float32), -6.0, 6.0)
    return (basis * col_scale * row_scale / 10.0).astype(jnp.bfloat16)


def key_basis(key):
    return jnp.clip(jax.random.normal(jax.random.fold_in(key, 11), (D, D), jnp.float32), -6.0, 6.0) / math.sqrt(D)


def draw_w_key(key, part):
    return key_basis(key).astype(jnp.bfloat16)


def draw_w_query(key, part):
    return (jnp.clip(jax.random.normal(jax.random.fold_in(key, 13), (D, D), jnp.float32), -6.0, 6.0) / math.sqrt(D)).astype(jnp.bfloat16)


def place_ends(entries, rng, least, top_value):
    extent = entries.shape
    index_at = [jax.random.randint(jax.random.fold_in(rng, axis), (), 0, extent[axis]) for axis in range(len(extent))]
    entries = entries.at[tuple(index_at)].set(least)
    longest = extent.index(max(extent))
    index_at[longest] = (index_at[longest] + 1) % extent[longest]
    return entries.at[tuple(index_at)].set(top_value)


def steps_of(own_key, shape, cuts, smallest, high):
    gain = 1.0
    for axis_at, blocks in cuts:
        steps = jax.random.uniform(jax.random.fold_in(jax.random.fold_in(own_key, 6), axis_at), (blocks,), jnp.float32, smallest / len(cuts), high / len(cuts))
        gain = gain * jnp.repeat(jnp.exp(steps), shape[axis_at] // blocks).reshape((-1,) + (1,) * (len(shape) - 1 - axis_at))
    return gain


def assign_block(own_key, own, number, rows, amount, top, most, lean):
    ranking = jax.random.permutation(own_key, amount)
    crowded, ordinary = load_shares(amount, rows * top, most, lean, True), load_shares(amount, rows * top, most, lean, False)
    places = jnp.arange(amount)

    def named(lengths, turn):
        used = int((lengths > 0).sum())
        fixed = max(1, used // 4)
        moved = fixed + (places - fixed + turn * (used - fixed)) % max(1, amount - fixed)
        return jnp.zeros((amount,), jnp.int32).at[ranking[jnp.where(places < fixed, places, moved)]].set(jnp.asarray(lengths, jnp.int32))

    lengths = jnp.where(number % 4 == 0, named(crowded, number // 4), named(ordinary, number - number // 4 - 1))
    mixed = jax.random.permutation(jax.random.fold_in(own, 3), amount)
    giver, taker = mixed[0:amount // 2 * 2:2], mixed[1:amount // 2 * 2:2]
    margin = jnp.minimum(lengths[giver] - 1, most - lengths[taker]) // 2
    margin = jnp.where((giver == ranking[0]) | (taker == ranking[0]) | (lengths[taker] == 0), 0, jnp.maximum(margin, 0))
    moved = jax.random.randint(jax.random.fold_in(own, 4), (amount // 2,), 0, 1 << 20) % (margin + 1)
    lengths = lengths.at[giver].add(-moved).at[taker].add(moved)
    items = jnp.searchsorted(jnp.cumsum(lengths), jnp.arange(rows * top), side="right").astype(jnp.int32)
    table = items.reshape(top, rows).T
    table = table[jax.random.permutation(jax.random.fold_in(own, 1), rows)]
    turn = jax.random.randint(jax.random.fold_in(own, 2), (rows, 1), 0, top)
    return jnp.take_along_axis(table, (jnp.arange(top)[None, :] + turn) % top, axis=1)


def load_shares(number_of, total, limit, slope, full):
    loads = [(1 << 20) // math.isqrt(rank ** slope) + 1 for rank in range(1, number_of + 1)]
    largest = limit if full else min(limit, max(-(-total // number_of), total * loads[0] // sum(loads)))
    least = 1 if total - largest >= number_of - 1 else 0
    counts, spare = [largest] + [least] * (number_of - 1), total - largest - least * (number_of - 1)
    while spare > 0:
        candidates = [i for i in range(1, number_of) if counts[i] < largest] or [i for i in range(1, number_of) if counts[i] < limit]
        pool, left = sum([loads[i] for i in candidates]), spare
        for i in candidates:
            addition = min(limit - counts[i], max(1, left * loads[i] // pool), spare)
            counts[i] = counts[i] + addition
            spare = spare - addition
    return np.array(counts)


def centred(own_key, extent, deviation, reach, shards=(), kind=jnp.bfloat16):
    drawn = jax.random.normal(own_key, extent, jnp.float32) * deviation
    if len(shards) > 0:
        drawn = steps_of(own_key, extent, shards, -0.22, 0.18) * drawn
    return jnp.clip(drawn, min=-reach, max=reach).astype(kind)


def setup_inputs(seed: int = 0) -> dict:
    keys = jax.random.split(jax.random.key(seed), 13)
    global_state = draw_global_state(jax.random.fold_in(keys[12], 71), 0)
    band_codes = place_ends(jax.random.randint(keys[1], (NB,), 0, 1000000), jax.random.fold_in(keys[1], 1), 0, 999999).astype(jnp.int32)
    norm_gain = jnp.clip(1.0 + 0.1 * jax.random.normal(keys[2], (D,), jnp.float32), 0.5, 1.5).astype(jnp.bfloat16)
    w_query = draw_w_query(jax.random.fold_in(keys[12], 71), 0)
    w_key = draw_w_key(jax.random.fold_in(keys[12], 71), 0)
    w_value = centred(keys[5], (D, D), D ** -0.5, 0.1875, ((1, 4),))
    w_out = centred(keys[6], (D, D), 0.4, 2.390625, ((0, 4),))
    reg_state = centred(keys[7], (NCOLS, RY, C), 1.0, 6.0, ((0, 256),))
    src_band_keys = jax.random.split(jax.random.fold_in(keys[8], 1), NCOLS * RY // NCELL)
    src_band_turns = jax.random.permutation(jax.random.fold_in(keys[8], 3), NCOLS * RY // NCELL)
    src_band = jax.vmap(lambda own, number: assign_block(jax.random.fold_in(keys[8], 2), own, number, NCELL, NB, 1, MOST, 2))(src_band_keys, src_band_turns).reshape((NCOLS, RY, 1))
    src_tok = place_ends(jax.random.randint(keys[9], (NCOLS, RY), 0, GT // N_TP), jax.random.fold_in(keys[9], 1), 0, (GT // N_TP) - 1).astype(jnp.int32)
    w_bound = centred(keys[10], (D, C), D ** -0.5, 0.1875)
    conv_w = centred(keys[11], (9, C, C), (9 * C) ** -0.5, 0.09375)
    return {"global_state": global_state, "band_codes": band_codes, "norm_gain": norm_gain, "w_query": w_query, "w_key": w_key, "w_value": w_value, "w_out": w_out, "reg_state": reg_state, "src_band": src_band, "src_tok": src_tok, "w_bound": w_bound, "conv_w": conv_w}


mix_band = 73856093
mix_token = 19349663
mix_feature = 83492791
mix_again = 668265261

def wiggle(band_code, token, feature):
    mixed = band_code * mix_band + token * mix_token + feature * mix_feature
    mixed = jnp.bitwise_xor(mixed, jnp.right_shift(mixed, 15))
    mixed = mixed * mix_again
    mixed = jnp.bitwise_xor(mixed, jnp.right_shift(mixed, 13))
    level = jnp.bitwise_and(mixed, 1023).astype(jnp.float32)
    return (level - 511.5) * (0.5 / 295.6)

def reference(global_state, band_codes, norm_gain, w_query, w_key, w_value, w_out, reg_state, src_band, src_tok, w_bound, conv_w):
    sign_set = jnp.array([0.0, 1.0, -1.0], jnp.float32)
    tok_ids = jnp.arange(GT, dtype=jnp.int32)[:, None]
    feat_ids = jnp.arange(D, dtype=jnp.int32)[None, :]
    band_x = global_state.reshape(NB, GT, D)

    def states_of(slab, band_code):
        return slab.astype(jnp.float32)[None] + sign_set[:, None, None] * wiggle(band_code, tok_ids, feat_ids)[None]

    def project_band(operands):
        slab, band_code = operands
        states = states_of(slab, band_code)
        inv_rms = lax.rsqrt(lax.optimization_barrier(jnp.mean(states * states, -1, keepdims=True)) + 1e-06)
        normed = (states * inv_rms * norm_gain.astype(jnp.float32)).astype(jnp.bfloat16).reshape(3 * GT, D)
        queries = jnp.dot(normed, w_query, preferred_element_type=jnp.float32).astype(jnp.bfloat16).reshape(3, GT, D)
        key_rows = jnp.dot(normed, w_key, preferred_element_type=jnp.float32).astype(jnp.bfloat16).reshape(3, GT, D)
        value_rows = jnp.dot(normed, w_value, preferred_element_type=jnp.float32).astype(jnp.bfloat16).reshape(3, GT, D)
        return (queries, key_rows, value_rows)
    queries, key_rows, value_rows = lax.map(project_band, (band_x, band_codes))
    key_pad = jnp.pad(jnp.transpose(key_rows, (1, 0, 2, 3)).reshape(3, NTOK, D), ((0, 0), (HALO, HALO), (0, 0)))
    value_pad = jnp.pad(jnp.transpose(value_rows, (1, 0, 2, 3)).reshape(3, NTOK, D), ((0, 0), (HALO, HALO), (0, 0)))
    key_span = GT + 2 * HALO
    head_cols = D // N_TP

    def attend(operands):
        band_index, band_q, slab, band_code = operands
        start = band_index * GT
        key_part = lax.dynamic_slice_in_dim(key_pad, start, key_span, 1).astype(jnp.float32).reshape(3, key_span, HEADS, HD)
        value_part = lax.dynamic_slice_in_dim(value_pad, start, key_span, 1).astype(jnp.float32).reshape(3, key_span, HEADS, HD)
        key_pos = start - HALO + jnp.arange(key_span, dtype=jnp.int32)
        key_valid = (key_pos >= 0) & (key_pos < NTOK)
        query_part = band_q.astype(jnp.float32).reshape(3, GT, HEADS, HD)
        scores = jnp.einsum('pqhd,pkhd->phqk', query_part, key_part) * HD ** (-0.5)
        scores = jnp.where(key_valid[None, None, None, :], scores, -1e+30)
        row_max = lax.optimization_barrier(jnp.max(scores, -1, keepdims=True))
        expon = jnp.exp(scores - row_max)
        weights = (expon / lax.optimization_barrier(jnp.sum(expon, -1, keepdims=True))).astype(jnp.bfloat16)
        attended = jnp.einsum('phqk,pkhd->pqhd', weights.astype(jnp.float32), value_part).astype(jnp.bfloat16)
        attended = attended.reshape(3 * GT, N_TP, head_cols).astype(jnp.float32)
        parts = jnp.einsum('rgk,gkn->grn', attended, w_out.reshape(N_TP, head_cols, D).astype(jnp.float32))
        parts = lax.optimization_barrier(parts.astype(jnp.bfloat16)).astype(jnp.float32)
        summed = lax.optimization_barrier(jnp.sum(parts, 0)).reshape(3, GT, D)
        return (states_of(slab, band_code) + summed).astype(jnp.bfloat16)
    band_out = lax.map(attend, (jnp.arange(NB, dtype=jnp.int32), queries, band_x, band_codes))
    global_out = jnp.transpose(band_out, (1, 0, 2, 3)).reshape(3, NTOK, D)
    col_ids = jnp.arange(NCOLS, dtype=jnp.int32)[:, None]
    source = src_band[:, :, 0] * GT + col_ids // CC % N_TP * (GT // N_TP) + src_tok
    gathered = global_out[:, source]
    forcing = jnp.dot(gathered.reshape(-1, D), w_bound, preferred_element_type=jnp.float32).astype(jnp.bfloat16).reshape(3, NCOLS, RY, C)
    inputs = (reg_state.astype(jnp.float32)[None] + forcing.astype(jnp.float32)).astype(jnp.bfloat16)
    padded = jnp.pad(inputs, ((0, 0), (1, 1), (1, 1), (0, 0)))
    conv_sum = jnp.zeros((3 * NCOLS * RY, C), jnp.float32)
    for shift_col in range(3):
        for shift_row in range(3):
            window = padded[:, shift_col:shift_col + NCOLS, shift_row:shift_row + RY].reshape(-1, C)
            conv_sum = conv_sum + jnp.dot(window, conv_w[3 * shift_col + shift_row], preferred_element_type=jnp.float32)
    result = inputs.astype(jnp.float32) + jax.nn.silu(conv_sum.reshape(3, NCOLS, RY, C))
    return (global_out, result.astype(jnp.bfloat16))
```

```python
import functools

import jax
import jax.numpy as jnp
from jax import lax
from jax.experimental import pallas as pl
from jax.experimental.pallas import tpu as pltpu
from jax.sharding import PartitionSpec as P

HD = 64
SIGNS = (0.0, 1.0, -1.0)
BANDS = ("sec", "tile")
CELLS = ("sec", "tile", "tp")
LOG2E = 1.4426950408889634
VMEM_LIMIT = 56 * 1024 * 1024

mix_band = 73856093
mix_token = 19349663
mix_feature = 83492791
mix_again = 668265261


def iota(shape, dim):
    return lax.broadcasted_iota(jnp.int32, shape, dim)


def dot(a, b):
    return jnp.dot(a, b, preferred_element_type=jnp.float32)


def dot_t(a, b):
    return lax.dot_general(a, b, (((1,), (1,)), ((), ())), preferred_element_type=jnp.float32)


def wiggle(code, first_token, rows, features):
    by_row = code * mix_band + (first_token + iota((rows, 1), 0)) * mix_token
    mixed = by_row + iota((1, features), 1) * mix_feature
    mixed = lax.bitwise_xor(mixed, lax.shift_right_arithmetic(mixed, jnp.full_like(mixed, 15)))
    mixed = mixed * mix_again
    mixed = lax.bitwise_xor(mixed, lax.shift_right_arithmetic(mixed, jnp.full_like(mixed, 13)))
    level = lax.bitwise_and(mixed, 1023).astype(jnp.float32)
    return (level - 511.5) * (0.5 / 295.6)


def project_kernel(band_ref, *refs, halo):
    if halo:
        step = pl.program_id(0)
        before_ref, after_ref, gain_ref, *refs = refs
        rows = before_ref.shape[0] - 16
        came = jnp.where(step == 0, before_ref[...], after_ref[...]).astype(jnp.float32)
        x = came[:rows]
        first = (1 - step) * rows
        digits = came[rows : rows + 1, 0:128]
        lane = iota((1, 128), 1)
        place = jnp.where(lane == 0, 65536.0, jnp.where(lane == 1, 256.0, 1.0))
        code = jnp.sum(jnp.where(lane < 3, digits * place, 0.0), -1, keepdims=True)
        code = code.astype(jnp.int32)
    else:
        x_ref, gain_ref, *refs = refs
        rows = x_ref.shape[0]
        x = x_ref[...].astype(jnp.float32)
        first = pl.program_id(0) * rows
        code = jnp.full((1, 1), band_ref[2], jnp.int32)
    weights, outs = refs[: len(refs) // 2], refs[len(refs) // 2 :]
    features = x.shape[1]
    p = wiggle(code, first, rows, features)
    gain = gain_ref[...].astype(jnp.float32)
    x_scaled = (x * gain).astype(jnp.bfloat16)
    p_scaled = (p * gain).astype(jnp.bfloat16)
    inv = []
    for sign in SIGNS:
        state = x if sign == 0.0 else (x + p if sign > 0 else x - p)
        inv.append(lax.rsqrt(jnp.sum(state * state, -1, keepdims=True) / features + 1e-06))
    for index, (w_ref, out_ref) in enumerate(zip(weights, outs)):
        scale = HD**-0.5 * LOG2E if (index == 0 and not halo) else 1.0
        base = dot(x_scaled, w_ref[...])
        diff = dot(p_scaled, w_ref[...])
        for s, sign in enumerate(SIGNS):
            out_ref[s] = ((base + sign * diff) * (inv[s] * scale)).astype(jnp.bfloat16)


def project(band, arrays, gain, weights, halo):
    features = gain.shape[1]
    cols = weights[0].shape[1]
    whole = lambda i, b: (0, 0)
    if halo:
        tokens = 2 * (arrays[0].shape[0] - 16)
        specs = [pl.BlockSpec(a.shape, whole) for a in arrays]
    else:
        tokens = arrays[0].shape[0]
        specs = [pl.BlockSpec((tokens // 2, features), lambda i, b: (i, 0))]
    rows = tokens // 2
    return pl.pallas_call(
        functools.partial(project_kernel, halo=halo),
        out_shape=[jax.ShapeDtypeStruct((3, tokens, cols), jnp.bfloat16) for _ in weights],
        grid_spec=pltpu.PrefetchScalarGridSpec(
            num_scalar_prefetch=1,
            grid=(2,),
            in_specs=specs
            + [pl.BlockSpec(gain.shape, whole)]
            + [pl.BlockSpec(w.shape, whole) for w in weights],
            out_specs=[pl.BlockSpec((3, rows, cols), lambda i, b: (0, i, 0)) for _ in weights],
        ),
        compiler_params=pltpu.CompilerParams(vmem_limit_bytes=VMEM_LIMIT),
        name="project_halo" if halo else "project_own",
    )(band, *arrays, gain, *weights)


def attend_kernel(band_ref, q_ref, k_ref, v_ref, k_halo_ref, v_halo_ref, out_ref, *, bands):
    tokens, cols = q_ref.shape[1:]
    half = tokens // 2
    left = band_ref[0] > 0
    right = band_ref[0] < bands - 1
    head_of = iota((1, cols), 1) // HD
    k = k_ref[0]
    v = v_ref[0]
    row = iota((tokens, 1), 0)
    there = jnp.where(row < half, left.astype(jnp.int32), right.astype(jnp.int32)) > 0
    k_halo = jnp.where(there, k_halo_ref[0], k)
    v_halo = v_halo_ref[0]
    one = there.astype(jnp.bfloat16)
    v_halo = v_halo * one
    result = [None] * 4
    block = half
    for part in range(tokens // block):
        q = q_ref[0, part * block : (part + 1) * block, :]
        gathered = jnp.zeros((block, cols), jnp.float32)
        for head in range(cols // HD):
            mine = head_of == head
            q_head = jnp.where(mine, q, jnp.zeros_like(q))
            own = dot_t(q_head, k)
            far = dot_t(q_head, k_halo)
            top = jnp.maximum(
                jnp.max(own, -1, keepdims=True), jnp.max(far, -1, keepdims=True)
            )
            own = jnp.exp2(own - top).astype(jnp.bfloat16)
            far = jnp.exp2(far - top).astype(jnp.bfloat16)
            v_own = jnp.where(mine, v, jnp.ones_like(v))
            v_far = jnp.where(mine, v_halo, jnp.broadcast_to(one, v.shape))
            acc = dot(own, v_own) + dot(far, v_far)
            total = pltpu.roll(acc, cols // 2, 1)
            gathered = jnp.where(mine, acc / total, gathered)
        gathered = gathered.astype(jnp.bfloat16)
        quarter = out_ref.shape[2]
        for piece in range(block // quarter):
            out_ref[part * (block // quarter) + piece, 0] = gathered[
                piece * quarter : (piece + 1) * quarter
            ]


def attend(band, q, k, v, k_halo, v_halo, ranks, bands):
    forwards, tokens, cols = q.shape
    spec = pl.BlockSpec((1, tokens, cols), lambda i, b: (i, 0, 0))
    quarter = tokens // ranks
    return pl.pallas_call(
        functools.partial(attend_kernel, bands=bands),
        out_shape=jax.ShapeDtypeStruct((ranks, forwards, quarter, cols), jnp.bfloat16),
        grid_spec=pltpu.PrefetchScalarGridSpec(
            num_scalar_prefetch=1,
            grid=(forwards,),
            in_specs=[spec] * 5,
            out_specs=pl.BlockSpec((ranks, 1, quarter, cols), lambda i, b: (0, i, 0, 0)),
        ),
        compiler_params=pltpu.CompilerParams(vmem_limit_bytes=VMEM_LIMIT),
        name="attend",
    )(band, q, k, v, k_halo, v_halo)


def ask_kernel(row_ref, col_ref, ask_ref, take_ref):
    bands = ask_ref.shape[0]
    cells = row_ref.shape[1]
    named = row_ref[...]
    band_row = lax.shift_right_arithmetic(named, jnp.full_like(named, 7))
    token = lax.bitwise_and(named, 127).astype(jnp.float32)
    match = (band_row == iota((bands, cells), 0)).astype(jnp.float32)
    before = (iota((cells, cells), 0) < iota((cells, cells), 1)).astype(jnp.float32)
    slot = dot(match.astype(jnp.bfloat16), before.astype(jnp.bfloat16))
    lanes = iota((bands, cells), 1)
    asked = jnp.zeros((bands, cells), jnp.float32)
    for s in range(4):
        hit = jnp.where(slot == s, match, 0.0)
        token_s = jnp.sum(hit * (token + 1.0), -1, keepdims=True) - 1.0
        asked = jnp.where(lanes == s, token_s, asked)
    ask_ref[...] = asked[:, :4].astype(jnp.int32)

    named = col_ref[...]
    band_col = lax.shift_right_arithmetic(named, jnp.full_like(named, 7))
    earlier = (band_col == band_row) & (iota((cells, cells), 1) < iota((cells, cells), 0))
    slot_col = jnp.sum(earlier.astype(jnp.float32), -1, keepdims=True).astype(jnp.int32)
    target = band_col * 16 + slot_col * 4
    rows = take_ref.shape[1]
    for part in range(4):
        take_ref[part * cells : (part + 1) * cells, :] = (
            (iota((cells, rows), 1) == target + part).astype(jnp.float32).astype(jnp.bfloat16)
        )


def ask(row, col, bands):
    cells = row.shape[1]
    return pl.pallas_call(
        ask_kernel,
        out_shape=[
            jax.ShapeDtypeStruct((bands, 4), jnp.int32),
            jax.ShapeDtypeStruct((4 * cells, bands * 16), jnp.bfloat16),
        ],
        compiler_params=pltpu.CompilerParams(vmem_limit_bytes=VMEM_LIMIT),
        name="ask",
    )(row, col)


def pick_rows(asked, rows, cells):
    bands = asked.shape[0]
    spread = (iota((rows, bands), 0) // 16 == iota((rows, bands), 1)).astype(jnp.float32)
    per_row = dot(spread.astype(jnp.bfloat16), asked.astype(jnp.float32).astype(jnp.bfloat16))
    r = iota((rows, 1), 0)
    mine = iota((rows, 4), 1) == (r // 4) % 4
    token_r = jnp.sum(jnp.where(mine, per_row, 0.0), -1, keepdims=True).astype(jnp.int32)
    target = jnp.where(token_r >= 0, (r % 4) * cells + token_r, -1)
    return (iota((rows, 4 * cells), 1) == target).astype(jnp.float32).astype(jnp.bfloat16)


def combine_kernel(where_ref, att_ref, w_out_ref, x_ref, w_bound_ref, asked_ref, out_ref, send_ref):
    ranks, _, cols = att_ref.shape
    quarter, features = x_ref.shape
    code = jnp.full((1, 1), where_ref[2], jnp.int32)
    x = x_ref[...].astype(jnp.float32)
    p = wiggle(code, where_ref[1] * quarter, quarter, features)
    rows = []
    for s, sign in enumerate(SIGNS):
        part = x + sign * p
        for g in range(ranks):
            part = part + dot(
                att_ref[g, s * quarter : (s + 1) * quarter, :],
                w_out_ref[g * cols : (g + 1) * cols, :],
            )
        part = part.astype(jnp.bfloat16)
        out_ref[s] = part
        rows.append(dot(part, w_bound_ref[...]).astype(jnp.bfloat16))
    parts = rows[0].shape[1] // 128
    table = jnp.concatenate(
        [
            jnp.concatenate([f[:, c * 128 : (c + 1) * 128] for f in rows], 1)
            for c in range(parts)
        ],
        0,
    )
    pick = pick_rows(asked_ref[...], send_ref.shape[0] * 16, quarter)
    picked = dot(pick, table).astype(jnp.bfloat16)
    send_ref[...] = picked.reshape(send_ref.shape)


def combine(where, att, w_out, x, w_bound, asked):
    ranks = att.shape[0]
    quarter = x.shape[0] // ranks
    features = x.shape[1]
    shapes = [(3, quarter, features), (asked.shape[0], 16, 384)]
    whole2 = lambda i, b: (0, 0)
    whole3 = lambda i, b: (0, 0, 0)
    return pl.pallas_call(
        combine_kernel,
        out_shape=[jax.ShapeDtypeStruct(s, jnp.bfloat16) for s in shapes],
        grid_spec=pltpu.PrefetchScalarGridSpec(
            num_scalar_prefetch=1,
            grid=(1,),
            in_specs=[
                pl.BlockSpec(att.shape, whole3),
                pl.BlockSpec(w_out.shape, whole2),
                pl.BlockSpec((quarter, features), lambda i, b: (b[1], 0)),
                pl.BlockSpec(w_bound.shape, whole2),
                pl.BlockSpec(asked.shape, whole2),
            ],
            out_specs=[pl.BlockSpec(s, whole3) for s in shapes],
        ),
        compiler_params=pltpu.CompilerParams(vmem_limit_bytes=VMEM_LIMIT),
        name="combine",
    )(where, att, w_out, x, w_bound, asked)


def inputs_kernel(arrived_ref, take_ref, reg_ref, out_ref, first_ref, last_ref):
    cols, rows, channels = reg_ref.shape
    cells = cols * rows
    table = arrived_ref[...].reshape(take_ref.shape[1], 384)
    taken = dot(take_ref[...], table)
    for part in range(channels // 128):
        lanes = slice(part * 128, (part + 1) * 128)
        reg = reg_ref[:, :, lanes].astype(jnp.float32)
        for s in range(3):
            forced = taken[part * cells : (part + 1) * cells, s * 128 : (s + 1) * 128]
            made = (reg + forced.reshape(cols, rows, 128)).astype(jnp.bfloat16)
            out_ref[:, s * rows : (s + 1) * rows, lanes] = made
            first_ref[s * rows : (s + 1) * rows, lanes] = made[0]
            last_ref[s * rows : (s + 1) * rows, lanes] = made[cols - 1]


def make_inputs(arrived, take, reg):
    cols, rows, channels = reg.shape
    shapes = [(cols, 3 * rows, channels), (3 * rows, channels), (3 * rows, channels)]
    return pl.pallas_call(
        inputs_kernel,
        out_shape=[jax.ShapeDtypeStruct(s, jnp.bfloat16) for s in shapes],
        compiler_params=pltpu.CompilerParams(vmem_limit_bytes=VMEM_LIMIT),
        name="inputs",
    )(arrived, take, reg)


def conv_kernel(x_ref, before_ref, after_ref, w_ref, out_ref):
    cols, slab, channels = x_ref.shape
    rows = slab // 3
    x = x_ref[...].reshape(cols * slab, channels)
    padded = jnp.concatenate([before_ref[...], x, after_ref[...]], 0)
    wide = padded.astype(jnp.float32)
    total = padded.shape[0]
    row = iota((total, 1), 0) % rows
    shifted = [
        jnp.where(row > 0, pltpu.roll(wide, 1, 0), 0.0).astype(jnp.bfloat16),
        padded,
        jnp.where(row < rows - 1, pltpu.roll(wide, total - 1, 0), 0.0).astype(jnp.bfloat16),
    ]
    conv = None
    for a in range(3):
        for b in range(3):
            piece = dot(shifted[b][a * slab : a * slab + cols * slab], w_ref[3 * a + b])
            conv = piece if conv is None else conv + piece
    result = x.astype(jnp.float32) + conv / (1.0 + jnp.exp(-conv))
    result = result.astype(jnp.bfloat16).reshape(cols, slab, channels)
    for s in range(3):
        out_ref[s] = result[:, s * rows : (s + 1) * rows, :]


def convolve(x, before, after, conv_w):
    cols, slab, channels = x.shape
    return pl.pallas_call(
        conv_kernel,
        out_shape=jax.ShapeDtypeStruct((3, cols, slab // 3, channels), jnp.bfloat16),
        compiler_params=pltpu.CompilerParams(vmem_limit_bytes=VMEM_LIMIT),
        name="convolve",
    )(x, before, after, conv_w)


def neighbours(last, first, axis):
    count = lax.axis_size(axis)
    up = [(i, i + 1) for i in range(count - 1)]
    down = [(j, i) for i, j in up]
    return lax.ppermute(last, axis, up), lax.ppermute(first, axis, down)


def per_device(
    global_state,
    band_codes,
    norm_gain,
    w_query,
    w_key,
    w_value,
    w_out,
    reg_state,
    src_band,
    src_tok,
    w_bound,
    conv_w,
):
    ranks = lax.axis_size("tp")
    bands = lax.axis_size(BANDS)
    rank = lax.axis_index("tp")
    band = lax.axis_index(BANDS)
    tokens = global_state.shape[0]
    half = tokens // 2
    cells = src_tok.size
    gain = norm_gain[None, :]

    named = src_band.reshape(cells) * 128 + src_tok.reshape(cells)
    asked, take = ask(named[None, :], named[:, None], bands)
    w_out_all = lax.all_gather(w_out, "tp", axis=0, tiled=True)
    code = band_codes[0]
    digits = jnp.stack([code // 65536, (code // 256) % 256, code % 256]).astype(jnp.bfloat16)
    digits = jnp.pad(digits[None], ((0, 15), (0, global_state.shape[1] - 3)))
    before, after = neighbours(
        jnp.concatenate([global_state[half:], digits]),
        jnp.concatenate([global_state[:half], digits]),
        BANDS,
    )
    asked = lax.all_to_all(asked[:, None, :], BANDS, 0, 0, tiled=True)[:, 0, :]

    where = jnp.stack([band, rank, code])
    q, k, v = project(where, [global_state], gain, [w_query, w_key, w_value], False)
    k_halo, v_halo = project(where, [before, after], gain, [w_key, w_value], True)
    attended = attend(where, q, k, v, k_halo, v_halo, ranks, bands)
    attended = lax.all_to_all(
        attended.reshape(ranks, -1, attended.shape[-1]), "tp", 0, 0, tiled=True
    )
    global_out, send = combine(where, attended, w_out_all, global_state, w_bound, asked)
    arrived = lax.all_to_all(send, BANDS, 0, 0, tiled=True)
    inputs, first, last = make_inputs(arrived, take, reg_state)
    before, after = neighbours(last, first, CELLS)
    return global_out, convolve(inputs, before, after, conv_w)


def solution(mesh):
    placed = (
        P(("sec", "tile"), None),
        P(("sec", "tile")),
        P(),
        P(None, "tp"),
        P(None, "tp"),
        P(None, "tp"),
        P("tp", None),
        P(("sec", "tile", "tp"), None, None),
        P(("sec", "tile", "tp"), None, None),
        P(("sec", "tile", "tp"), None),
        P(),
        P(),
    )
    return jax.shard_map(
        per_device,
        mesh=mesh,
        in_specs=placed,
        out_specs=(
            P(None, ("sec", "tile", "tp"), None),
            P(None, ("sec", "tile", "tp"), None, None),
        ),
        check_vma=False,
    )
```

```python
import functools

import jax
import jax.numpy as jnp
from jax import lax
from jax.experimental import pallas as pl
from jax.experimental.pallas import tpu as pltpu
from jax.sharding import PartitionSpec as P

HD = 64
SIGNS = (0.0, 1.0, -1.0)
BANDS = ("sec", "tile")
CELLS = ("sec", "tile", "tp")
LOG2E = 1.4426950408889634
MIB = 1024 * 1024
ON_CHIP = pl.BlockSpec(memory_space=pltpu.VMEM)
SCALARS = pl.BlockSpec(memory_space=pltpu.SMEM)

mix_band = 73856093
mix_token = 19349663
mix_feature = 83492791
mix_again = 668265261


def iota(shape, dim):
    return lax.broadcasted_iota(jnp.int32, shape, dim)


def dot(a, b):
    return jnp.dot(a, b, preferred_element_type=jnp.float32)


def dot_t(a, b):
    return lax.dot_general(a, b, (((1,), (1,)), ((), ())), preferred_element_type=jnp.float32)


def wiggle(code, first_token, rows, features):
    by_row = code * mix_band + (first_token + iota((rows, 1), 0)) * mix_token
    mixed = by_row + iota((1, features), 1) * mix_feature
    mixed = lax.bitwise_xor(mixed, lax.shift_right_arithmetic(mixed, jnp.full_like(mixed, 15)))
    mixed = mixed * mix_again
    mixed = lax.bitwise_xor(mixed, lax.shift_right_arithmetic(mixed, jnp.full_like(mixed, 13)))
    level = lax.bitwise_and(mixed, 1023).astype(jnp.float32)
    return (level - 511.5) * (0.5 / 295.6)


def project_kernel(code_ref, *refs, halo):
    step = pl.program_id(0)
    both_ref, inv_ref = refs[-2:]
    if halo:
        before_ref, after_ref, gain_ref, *refs = refs[:-2]
        rows = before_ref.shape[0] - 16
        first = (1 - step) * rows
        digits = jnp.where(
            step == 0, before_ref[rows : rows + 16, 0:128], after_ref[rows : rows + 16, 0:128]
        ).astype(jnp.float32)[0:1]
        lane = iota((1, 128), 1)
        place = jnp.where(lane == 0, 65536.0, jnp.where(lane == 1, 256.0, 1.0))
        code = jnp.sum(jnp.where(lane < 3, digits * place, 0.0), -1, keepdims=True)
        code = code.astype(jnp.int32)
    else:
        x_ref, gain_ref, *refs = refs[:-2]
        rows = x_ref.shape[0]
        first = step * rows
        code = jnp.full((1, 1), code_ref[0], jnp.int32)
    weights, outs = refs[: len(refs) // 2], refs[len(refs) // 2 :]
    features = gain_ref.shape[1]
    gain = gain_ref[...].astype(jnp.float32)
    chunk, block = 16, 128
    for at in range(0, rows, block):
        for r in range(at, at + block, chunk):
            if halo:
                x = jnp.where(step == 0, before_ref[r : r + chunk], after_ref[r : r + chunk])
            else:
                x = x_ref[r : r + chunk]
            x = x.astype(jnp.float32)
            p = wiggle(code, first + r, chunk, features)
            place = 2 * at + (r - at)
            both_ref[place : place + chunk] = (x * gain).astype(jnp.bfloat16)
            both_ref[place + block : place + block + chunk] = (p * gain).astype(jnp.bfloat16)
            for s, sign in enumerate(SIGNS):
                state = x if sign == 0.0 else (x + p if sign > 0 else x - p)
                mean = jnp.sum(state * state, -1, keepdims=True) * (1.0 / features)
                inv_ref[s, r : r + chunk] = lax.rsqrt(mean + 1e-06)
        here = slice(at, at + block)
        for index, (w_ref, out_ref) in enumerate(zip(weights, outs)):
            scale = HD**-0.5 * LOG2E if (index == 0 and not halo) else 1.0
            made = dot(both_ref[2 * at : 2 * at + 2 * block], w_ref[...])
            base, diff = made[:block], made[block:]
            for s, sign in enumerate(SIGNS):
                full = base if sign == 0.0 else (base + diff if sign > 0 else base - diff)
                out_ref[s, here] = (full * (inv_ref[s, here] * scale)).astype(jnp.bfloat16)


def project(code, arrays, gain, weights, halo):
    features = gain.shape[1]
    cols = weights[0].shape[1]
    whole = lambda i: (0, 0)
    if halo:
        tokens = 2 * (arrays[0].shape[0] - 16)
        specs = [ON_CHIP for a in arrays]
    else:
        tokens = arrays[0].shape[0]
        specs = [pl.BlockSpec((tokens // 2, features), lambda i: (i, 0))]
    rows = tokens // 2
    return pl.pallas_call(
        functools.partial(project_kernel, halo=halo),
        out_shape=[jax.ShapeDtypeStruct((3, tokens, cols), jnp.bfloat16) for _ in weights],
        grid=(2,),
        in_specs=[SCALARS]
        + specs
        + [pl.BlockSpec(gain.shape, whole)]
        + [pl.BlockSpec(w.shape, whole) for w in weights],
        out_specs=[pl.BlockSpec((3, rows, cols), lambda i: (0, i, 0)) for _ in weights],
        scratch_shapes=[
            pltpu.VMEM((2 * rows, features), jnp.bfloat16),
            pltpu.VMEM((3, rows, 1), jnp.float32),
        ],
        compiler_params=pltpu.CompilerParams(vmem_limit_bytes=20 * MIB),
        name="project_halo" if halo else "project_own",
    )(code, *arrays, gain, *weights)


def attend_kernel(q_ref, k_ref, v_ref, k_halo_ref, v_halo_ref, out_ref, *, bands):
    tokens, cols = q_ref.shape[1:]
    half = tokens // 2
    band = lax.axis_index(BANDS)
    left = band > 0
    right = band < bands - 1
    head_of = iota((1, cols), 1) // HD
    k = k_ref[0]
    v = v_ref[0]
    row = iota((tokens, 1), 0)
    there = jnp.where(row < half, left.astype(jnp.int32), right.astype(jnp.int32)) > 0
    k_halo = jnp.where(there, k_halo_ref[0], k)
    v_halo = v_halo_ref[0]
    one = there.astype(jnp.bfloat16)
    v_halo = v_halo * one
    result = [None] * 4
    block = half
    for part in range(tokens // block):
        q = q_ref[0, part * block : (part + 1) * block, :]
        gathered = jnp.zeros((block, cols), jnp.float32)
        for head in range(cols // HD):
            mine = head_of == head
            q_head = jnp.where(mine, q, jnp.zeros_like(q))
            own = dot_t(q_head, k)
            far = dot_t(q_head, k_halo)
            top = jnp.maximum(
                jnp.max(own, -1, keepdims=True), jnp.max(far, -1, keepdims=True)
            )
            own = jnp.exp2(own - top).astype(jnp.bfloat16)
            far = jnp.exp2(far - top).astype(jnp.bfloat16)
            v_own = jnp.where(mine, v, jnp.ones_like(v))
            v_far = jnp.where(mine, v_halo, jnp.broadcast_to(one, v.shape))
            acc = dot(own, v_own) + dot(far, v_far)
            total = pltpu.roll(acc, cols // 2, 1)
            gathered = jnp.where(mine, acc / total, gathered)
        gathered = gathered.astype(jnp.bfloat16)
        quarter = out_ref.shape[2]
        for piece in range(block // quarter):
            out_ref[part * (block // quarter) + piece, 0] = gathered[
                piece * quarter : (piece + 1) * quarter
            ]


def attend(q, k, v, k_halo, v_halo, ranks, bands):
    forwards, tokens, cols = q.shape
    spec = pl.BlockSpec((1, tokens, cols), lambda i: (i, 0, 0))
    quarter = tokens // ranks
    return pl.pallas_call(
        functools.partial(attend_kernel, bands=bands),
        out_shape=jax.ShapeDtypeStruct((ranks, forwards, quarter, cols), jnp.bfloat16),
        grid=(forwards,),
        in_specs=[spec] * 5,
        out_specs=pl.BlockSpec((ranks, 1, quarter, cols), lambda i: (0, i, 0, 0)),
        compiler_params=pltpu.CompilerParams(vmem_limit_bytes=24 * MIB),
        name="attend",
    )(q, k, v, k_halo, v_halo)


def cells_row(x):
    cols, rows = x.shape
    cells = cols * rows
    spread = (iota((rows, cells), 1) % rows == iota((rows, cells), 0)).astype(jnp.float32)
    wide = dot(x.astype(jnp.float32).astype(jnp.bfloat16), spread.astype(jnp.bfloat16))
    mine = iota((cols, cells), 1) // rows == iota((cols, cells), 0)
    return jnp.sum(jnp.where(mine, wide, 0.0), 0, keepdims=True)


def ask_kernel(band_ref, tok_ref, ask_ref):
    bands = ask_ref.shape[0]
    named = cells_row(band_ref[...])
    token = cells_row(tok_ref[...])
    cells = named.shape[1]
    match = (named.astype(jnp.int32) == iota((bands, cells), 0)).astype(jnp.float32)
    before = (iota((cells, cells), 0) < iota((cells, cells), 1)).astype(jnp.float32)
    slot = dot(match.astype(jnp.bfloat16), before.astype(jnp.bfloat16))
    lanes = iota((bands, cells), 1)
    asked = jnp.zeros((bands, cells), jnp.float32)
    for s in range(4):
        hit = jnp.where(slot == s, match, 0.0)
        token_s = jnp.sum(hit * (token + 1.0), -1, keepdims=True) - 1.0
        asked = jnp.where(lanes == s, token_s, asked)
    ask_ref[...] = asked[:, :4].astype(jnp.int32)


def ask(band, tok, bands):
    return pl.pallas_call(
        ask_kernel,
        out_shape=jax.ShapeDtypeStruct((bands, 4), jnp.int32),
        in_specs=[ON_CHIP] * 2,
        out_specs=ON_CHIP,
        compiler_params=pltpu.CompilerParams(vmem_limit_bytes=4 * MIB),
        name="ask",
    )(band, tok)


def take_kernel(band_ref, take_ref):
    band_row = cells_row(band_ref[...])
    cells = band_row.shape[1]
    rows = take_ref.shape[1]
    r, c = iota((cells, cells), 0), iota((cells, cells), 1)
    band_col = jnp.sum(jnp.where(r == c, band_row, 0.0), -1, keepdims=True)
    earlier = (band_col == band_row) & (c < r)
    slot = jnp.sum(jnp.where(earlier, 1.0, 0.0), -1, keepdims=True)
    target = (band_col * 16.0 + slot * 4.0).astype(jnp.int32)
    for part in range(4):
        take_ref[part * cells : (part + 1) * cells, :] = (
            (iota((cells, rows), 1) == target + part).astype(jnp.float32).astype(jnp.bfloat16)
        )


def make_take(band, bands):
    return pl.pallas_call(
        take_kernel,
        out_shape=jax.ShapeDtypeStruct((4 * band.size, bands * 16), jnp.bfloat16),
        in_specs=[ON_CHIP],
        out_specs=ON_CHIP,
        compiler_params=pltpu.CompilerParams(vmem_limit_bytes=8 * MIB),
        name="take",
    )(band)


def prepare_kernel(code_ref, asked_ref, pick_ref, p_ref):
    rows, wide = pick_ref.shape
    bands = asked_ref.shape[0]
    cells = wide // 4
    spread = (iota((rows, bands), 0) // 16 == iota((rows, bands), 1)).astype(jnp.float32)
    asked = asked_ref[...].astype(jnp.float32)
    per_row = dot(spread.astype(jnp.bfloat16), asked.astype(jnp.bfloat16))
    r = iota((rows, 1), 0)
    mine = iota((rows, 4), 1) == (r // 4) % 4
    token_r = jnp.sum(jnp.where(mine, per_row, 0.0), -1, keepdims=True).astype(jnp.int32)
    target = jnp.where(token_r >= 0, (r % 4) * cells + token_r, -1)
    pick_ref[...] = (iota((rows, wide), 1) == target).astype(jnp.float32).astype(jnp.bfloat16)
    quarter, features = p_ref.shape
    code = jnp.full((1, 1), code_ref[0], jnp.int32)
    p_ref[...] = wiggle(code, lax.axis_index("tp") * quarter, quarter, features)


def prepare(code, asked, quarter, features):
    return pl.pallas_call(
        prepare_kernel,
        out_shape=[
            jax.ShapeDtypeStruct((asked.shape[0] * 16, 4 * quarter), jnp.bfloat16),
            jax.ShapeDtypeStruct((quarter, features), jnp.float32),
        ],
        in_specs=[SCALARS, ON_CHIP],
        out_specs=[ON_CHIP] * 2,
        compiler_params=pltpu.CompilerParams(vmem_limit_bytes=12 * MIB),
        name="prepare",
    )(code, asked)


def combine_kernel(att_ref, w0_ref, w1_ref, w2_ref, w3_ref, x_ref, p_ref, w_bound_ref, pick_ref, out_ref, send_ref):
    ranks, _, cols = att_ref.shape
    quarter = p_ref.shape[0]
    rank = lax.axis_index("tp")
    x = x_ref[pl.ds(pl.multiple_of(rank * quarter, quarter), quarter), :].astype(jnp.float32)
    p = p_ref[...]
    total = None
    for d, w_ref in enumerate((w0_ref, w1_ref, w2_ref, w3_ref)):
        piece = dot(att_ref[lax.rem(rank + ranks - d, ranks)], w_ref[...])
        total = piece if total is None else total + piece
    made = []
    for s, sign in enumerate(SIGNS):
        part = x if sign == 0.0 else (x + p if sign > 0 else x - p)
        part = (part + total[s * quarter : (s + 1) * quarter]).astype(jnp.bfloat16)
        out_ref[s] = part
        made.append(part)
    forced = dot(jnp.concatenate(made, 0), w_bound_ref[...]).astype(jnp.bfloat16)
    rows = [forced[s * quarter : (s + 1) * quarter] for s in range(3)]
    parts = forced.shape[1] // 128
    table = jnp.concatenate(
        [
            jnp.concatenate([f[:, c * 128 : (c + 1) * 128] for f in rows], 1)
            for c in range(parts)
        ],
        0,
    )
    picked = dot(pick_ref[...], table).astype(jnp.bfloat16)
    send_ref[...] = picked.reshape(send_ref.shape)


def combine(att, w_outs, x, p, w_bound, pick):
    shapes = [(3, *p.shape), (pick.shape[0] // 16, 16, 384)]
    operands = [att, *w_outs, x, p, w_bound, pick]
    return pl.pallas_call(
        combine_kernel,
        out_shape=[jax.ShapeDtypeStruct(s, jnp.bfloat16) for s in shapes],
        in_specs=[ON_CHIP] * len(operands),
        out_specs=[ON_CHIP] * 2,
        compiler_params=pltpu.CompilerParams(vmem_limit_bytes=24 * MIB),
        name="combine",
    )(*operands)


def inputs_kernel(arrived_ref, take_ref, reg_ref, out_ref, first_ref, last_ref):
    cols, rows, channels = reg_ref.shape
    cells = cols * rows
    table = arrived_ref[...].reshape(take_ref.shape[1], 384)
    taken = dot(take_ref[...], table)
    for part in range(channels // 128):
        lanes = slice(part * 128, (part + 1) * 128)
        reg = reg_ref[:, :, lanes].astype(jnp.float32)
        for s in range(3):
            forced = taken[part * cells : (part + 1) * cells, s * 128 : (s + 1) * 128]
            made = (reg + forced.reshape(cols, rows, 128)).astype(jnp.bfloat16)
            out_ref[:, s * rows : (s + 1) * rows, lanes] = made
            first_ref[s * rows : (s + 1) * rows, lanes] = made[0]
            last_ref[s * rows : (s + 1) * rows, lanes] = made[cols - 1]


def make_inputs(arrived, take, reg):
    cols, rows, channels = reg.shape
    shapes = [(cols, 3 * rows, channels), (3 * rows, channels), (3 * rows, channels)]
    return pl.pallas_call(
        inputs_kernel,
        out_shape=[jax.ShapeDtypeStruct(s, jnp.bfloat16) for s in shapes],
        in_specs=[ON_CHIP] * 3,
        out_specs=[ON_CHIP] * 3,
        compiler_params=pltpu.CompilerParams(vmem_limit_bytes=12 * MIB),
        name="inputs",
    )(arrived, take, reg)


def conv_kernel(x_ref, before_ref, after_ref, w_ref, out_ref):
    cols, slab, channels = x_ref.shape
    rows = slab // 3
    x = x_ref[...].reshape(cols * slab, channels)
    padded = jnp.concatenate([before_ref[...], x, after_ref[...]], 0)
    wide = padded.astype(jnp.float32)
    total = padded.shape[0]
    row = iota((total, 1), 0) % rows
    shifted = [
        jnp.where(row > 0, pltpu.roll(wide, 1, 0), 0.0).astype(jnp.bfloat16),
        padded,
        jnp.where(row < rows - 1, pltpu.roll(wide, total - 1, 0), 0.0).astype(jnp.bfloat16),
    ]
    conv = None
    for a in range(3):
        for b in range(3):
            piece = dot(shifted[b][a * slab : a * slab + cols * slab], w_ref[3 * a + b])
            conv = piece if conv is None else conv + piece
    result = x.astype(jnp.float32) + conv / (1.0 + jnp.exp(-conv))
    result = result.astype(jnp.bfloat16).reshape(cols, slab, channels)
    for s in range(3):
        out_ref[s] = result[:, s * rows : (s + 1) * rows, :]


def convolve(x, before, after, conv_w):
    cols, slab, channels = x.shape
    return pl.pallas_call(
        conv_kernel,
        out_shape=jax.ShapeDtypeStruct((3, cols, slab // 3, channels), jnp.bfloat16),
        in_specs=[ON_CHIP] * 4,
        out_specs=ON_CHIP,
        compiler_params=pltpu.CompilerParams(vmem_limit_bytes=20 * MIB),
        name="convolve",
    )(x, before, after, conv_w)


def neighbours(last, first, axis):
    count = lax.axis_size(axis)
    up = [(i, i + 1) for i in range(count - 1)]
    down = [(j, i) for i, j in up]
    return lax.ppermute(last, axis, up), lax.ppermute(first, axis, down)


def per_device(
    global_state,
    band_codes,
    norm_gain,
    w_query,
    w_key,
    w_value,
    w_out,
    reg_state,
    src_band,
    src_tok,
    w_bound,
    conv_w,
):
    ranks = lax.axis_size("tp")
    bands = lax.axis_size(BANDS)
    tokens, features = global_state.shape
    half = tokens // 2
    gain = norm_gain[None, :]
    cell_band = src_band.reshape(src_tok.shape)

    code = band_codes[0]
    digits = jnp.stack([code // 65536, (code // 256) % 256, code % 256]).astype(jnp.bfloat16)
    digits = jnp.pad(digits[None], ((0, 15), (0, features - 3)))
    before, after = neighbours(
        jnp.concatenate([global_state[half:], digits]),
        jnp.concatenate([global_state[:half], digits]),
        BANDS,
    )
    asked = ask(cell_band, src_tok, bands)
    asked = lax.all_to_all(asked[:, None, :], BANDS, 0, 0, tiled=True)[:, 0, :]
    w_outs = [w_out] + [
        lax.ppermute(w_out, "tp", [(i, (i + d) % ranks) for i in range(ranks)])
        for d in range(1, ranks)
    ]

    q, k, v = project(band_codes, [global_state], gain, [w_query, w_key, w_value], False)
    k_halo, v_halo = project(band_codes, [before, after], gain, [w_key, w_value], True)
    attended = attend(q, k, v, k_halo, v_halo, ranks, bands)
    asked, attended = lax.optimization_barrier((asked, attended))
    pick, p = prepare(band_codes, asked, tokens // ranks, features)
    attended = lax.all_to_all(
        attended.reshape(ranks, -1, attended.shape[-1]), "tp", 0, 0, tiled=True
    )
    global_out, send = combine(attended, w_outs, global_state, p, w_bound, pick)
    cell_band, send = lax.optimization_barrier((cell_band, send))
    take = make_take(cell_band, bands)
    arrived = lax.all_to_all(send, BANDS, 0, 0, tiled=True)
    inputs, first, last = make_inputs(arrived, take, reg_state)
    before, after = neighbours(last, first, CELLS)
    return global_out, convolve(inputs, before, after, conv_w)


def solution(mesh):
    placed = (
        P(("sec", "tile"), None),
        P(("sec", "tile")),
        P(),
        P(None, "tp"),
        P(None, "tp"),
        P(None, "tp"),
        P("tp", None),
        P(("sec", "tile", "tp"), None, None),
        P(("sec", "tile", "tp"), None, None),
        P(("sec", "tile", "tp"), None),
        P(),
        P(),
    )
    return jax.shard_map(
        per_device,
        mesh=mesh,
        in_specs=placed,
        out_specs=(
            P(None, ("sec", "tile", "tp"), None),
            P(None, ("sec", "tile", "tp"), None, None),
        ),
        check_vma=False,
    )
```

```python
import functools

import jax
import jax.numpy as jnp
from jax import lax
from jax.experimental import pallas as pl
from jax.experimental.pallas import tpu as pltpu
from jax.sharding import PartitionSpec as P

HD = 64
SIGNS = (0.0, 1.0, -1.0)
BANDS = ("sec", "tile")
CELLS = ("sec", "tile", "tp")
LOG2E = 1.4426950408889634
MIB = 1024 * 1024
ON_CHIP = pl.BlockSpec(memory_space=pltpu.VMEM)
SCALARS = pl.BlockSpec(memory_space=pltpu.SMEM)

mix_band = 73856093
mix_token = 19349663
mix_feature = 83492791
mix_again = 668265261


def iota(shape, dim):
    return lax.broadcasted_iota(jnp.int32, shape, dim)


def in_hbm(x):
    return pltpu.with_memory_space_constraint(x, pltpu.HBM)


def dot(a, b):
    return jnp.dot(a, b, preferred_element_type=jnp.float32)


def dot_t(a, b):
    return lax.dot_general(a, b, (((1,), (1,)), ((), ())), preferred_element_type=jnp.float32)


def wiggle(code, first_token, rows, features):
    by_row = code * mix_band + (first_token + iota((rows, 1), 0)) * mix_token
    mixed = by_row + iota((1, features), 1) * mix_feature
    mixed = lax.bitwise_xor(mixed, lax.shift_right_arithmetic(mixed, jnp.full_like(mixed, 15)))
    mixed = mixed * mix_again
    mixed = lax.bitwise_xor(mixed, lax.shift_right_arithmetic(mixed, jnp.full_like(mixed, 13)))
    level = lax.bitwise_and(mixed, 1023).astype(jnp.float32)
    return (level - 511.5) * (0.5 / 295.6)


def edges_kernel(code_ref, x_ref, last_ref, first_ref, sems):
    half = x_ref.shape[0] // 2
    copies = [
        pltpu.make_async_copy(x_ref.at[pl.ds(half, half)], last_ref.at[pl.ds(0, half)], sems.at[0]),
        pltpu.make_async_copy(x_ref.at[pl.ds(0, half)], first_ref.at[pl.ds(0, half)], sems.at[1]),
    ]
    for copy in copies:
        copy.start()
    code = jnp.full((16, x_ref.shape[1]), code_ref[0], jnp.int32)
    lane = iota(code.shape, 1)
    shift = jnp.where(lane == 0, 16, jnp.where(lane == 1, 8, 0))
    digit = lax.bitwise_and(lax.shift_right_arithmetic(code, shift), 255)
    digit = digit.astype(jnp.float32).astype(jnp.bfloat16)
    last_ref[half:] = digit
    first_ref[half:] = digit
    for copy in copies:
        copy.wait()


def make_edges(code, x):
    tokens, features = x.shape
    shape = jax.ShapeDtypeStruct((tokens // 2 + 16, features), jnp.bfloat16)
    return pl.pallas_call(
        edges_kernel,
        out_shape=[shape, shape],
        in_specs=[SCALARS, pl.BlockSpec(memory_space=pltpu.HBM)],
        out_specs=[ON_CHIP] * 2,
        scratch_shapes=[pltpu.SemaphoreType.DMA((2,))],
        compiler_params=pltpu.CompilerParams(vmem_limit_bytes=4 * MIB),
        name="edges",
    )(code, x)


def project_kernel(code_ref, *refs, halo):
    step = pl.program_id(0)
    both_ref, inv_ref = refs[-2:]
    if halo:
        before_ref, after_ref, gain_ref, *refs = refs[:-2]
        rows = before_ref.shape[0] - 16
        first = (1 - step) * rows
        digits = jnp.where(
            step == 0, before_ref[rows : rows + 16, 0:128], after_ref[rows : rows + 16, 0:128]
        ).astype(jnp.float32)[0:1]
        lane = iota((1, 128), 1)
        place = jnp.where(lane == 0, 65536.0, jnp.where(lane == 1, 256.0, 1.0))
        code = jnp.sum(jnp.where(lane < 3, digits * place, 0.0), -1, keepdims=True)
        code = code.astype(jnp.int32)
    else:
        x_ref, gain_ref, *refs = refs[:-2]
        rows = x_ref.shape[0]
        first = step * rows
        code = jnp.full((1, 1), code_ref[0], jnp.int32)
    weights, outs = refs[: len(refs) // 2], refs[len(refs) // 2 :]
    features = gain_ref.shape[1]
    gain = gain_ref[...].astype(jnp.float32)
    chunk, block = 16, 128
    for at in range(0, rows, block):
        for r in range(at, at + block, chunk):
            if halo:
                x = jnp.where(step == 0, before_ref[r : r + chunk], after_ref[r : r + chunk])
            else:
                x = x_ref[r : r + chunk]
            x = x.astype(jnp.float32)
            p = wiggle(code, first + r, chunk, features)
            place = 2 * at + (r - at)
            both_ref[place : place + chunk] = (x * gain).astype(jnp.bfloat16)
            both_ref[place + block : place + block + chunk] = (p * gain).astype(jnp.bfloat16)
            for s, sign in enumerate(SIGNS):
                state = x if sign == 0.0 else (x + p if sign > 0 else x - p)
                mean = jnp.sum(state * state, -1, keepdims=True) * (1.0 / features)
                inv_ref[s, r : r + chunk] = lax.rsqrt(mean + 1e-06)
        here = slice(at, at + block)
        for index, (w_ref, out_ref) in enumerate(zip(weights, outs)):
            scale = HD**-0.5 * LOG2E if (index == 0 and not halo) else 1.0
            made = dot(both_ref[2 * at : 2 * at + 2 * block], w_ref[...])
            base, diff = made[:block], made[block:]
            for s, sign in enumerate(SIGNS):
                full = base if sign == 0.0 else (base + diff if sign > 0 else base - diff)
                out_ref[s, here] = (full * (inv_ref[s, here] * scale)).astype(jnp.bfloat16)


def project(code, arrays, gain, weights, halo):
    features = gain.shape[1]
    cols = weights[0].shape[1]
    whole = lambda i: (0, 0)
    if halo:
        tokens = 2 * (arrays[0].shape[0] - 16)
        specs = [ON_CHIP for a in arrays]
    else:
        tokens = arrays[0].shape[0]
        specs = [pl.BlockSpec((tokens // 2, features), lambda i: (i, 0))]
    rows = tokens // 2
    return pl.pallas_call(
        functools.partial(project_kernel, halo=halo),
        out_shape=[jax.ShapeDtypeStruct((3, tokens, cols), jnp.bfloat16) for _ in weights],
        grid=(2,),
        in_specs=[SCALARS]
        + specs
        + [pl.BlockSpec(gain.shape, whole)]
        + [pl.BlockSpec(w.shape, whole) for w in weights],
        out_specs=[pl.BlockSpec((3, rows, cols), lambda i: (0, i, 0)) for _ in weights],
        scratch_shapes=[
            pltpu.VMEM((2 * rows, features), jnp.bfloat16),
            pltpu.VMEM((3, rows, 1), jnp.float32),
        ],
        compiler_params=pltpu.CompilerParams(vmem_limit_bytes=12 * MIB),
        name="project_halo" if halo else "project_own",
    )(code, *arrays, gain, *weights)


def attend_kernel(q_ref, k_ref, v_ref, k_halo_ref, v_halo_ref, *refs, bands):
    *out_refs, held_ref = refs
    tokens, cols = q_ref.shape[1:]
    half = tokens // 2
    band = lax.axis_index(BANDS)
    left = band > 0
    right = band < bands - 1
    head_of = iota((1, cols), 1) // HD
    k = k_ref[0]
    v = v_ref[0]
    row = iota((tokens, 1), 0)
    there = jnp.where(row < half, left.astype(jnp.int32), right.astype(jnp.int32)) > 0
    k_halo = jnp.where(there, k_halo_ref[0], k)
    v_halo = v_halo_ref[0]
    one = there.astype(jnp.bfloat16)
    v_halo = v_halo * one
    block = half
    for part in range(tokens // block):
        q = q_ref[0, part * block : (part + 1) * block, :]
        gathered = jnp.zeros((block, cols), jnp.float32)
        for head in range(cols // HD):
            mine = head_of == head
            q_head = jnp.where(mine, q, jnp.zeros_like(q))
            own = dot_t(q_head, k)
            far = dot_t(q_head, k_halo)
            top = jnp.maximum(
                jnp.max(own, -1, keepdims=True), jnp.max(far, -1, keepdims=True)
            )
            own = jnp.exp2(own - top).astype(jnp.bfloat16)
            far = jnp.exp2(far - top).astype(jnp.bfloat16)
            v_own = jnp.where(mine, v, jnp.ones_like(v))
            v_far = jnp.where(mine, v_halo, jnp.broadcast_to(one, v.shape))
            acc = dot(own, v_own) + dot(far, v_far)
            total = pltpu.roll(acc, cols // 2, 1)
            gathered = jnp.where(mine, acc / total, gathered)
        held_ref[part * block : (part + 1) * block] = gathered.astype(jnp.bfloat16)
    ranks = len(out_refs)
    quarter = tokens // ranks
    rank = lax.axis_index("tp")
    for distance, out_ref in enumerate(out_refs):
        first = pl.multiple_of(lax.rem(rank + distance, ranks) * quarter, quarter)
        out_ref[...] = held_ref[pl.ds(first, quarter), :]


def attend(q, k, v, k_halo, v_halo, ranks, bands):
    forwards, tokens, cols = q.shape
    spec = pl.BlockSpec((1, tokens, cols), lambda i: (i, 0, 0))
    quarter = tokens // ranks
    return pl.pallas_call(
        functools.partial(attend_kernel, bands=bands),
        out_shape=[jax.ShapeDtypeStruct((forwards * quarter, cols), jnp.bfloat16)] * ranks,
        grid=(forwards,),
        in_specs=[spec] * 5,
        out_specs=[pl.BlockSpec((quarter, cols), lambda i: (i, 0))] * ranks,
        scratch_shapes=[pltpu.VMEM((tokens, cols), jnp.bfloat16)],
        compiler_params=pltpu.CompilerParams(vmem_limit_bytes=14 * MIB),
        name="attend",
    )(q, k, v, k_halo, v_halo)


def cells_row(x):
    cols, rows = x.shape
    cells = cols * rows
    spread = (iota((rows, cells), 1) % rows == iota((rows, cells), 0)).astype(jnp.float32)
    wide = dot(x.astype(jnp.float32).astype(jnp.bfloat16), spread.astype(jnp.bfloat16))
    mine = iota((cols, cells), 1) // rows == iota((cols, cells), 0)
    return jnp.sum(jnp.where(mine, wide, 0.0), 0, keepdims=True)


def ask_kernel(band_ref, tok_ref, ask_ref):
    bands = ask_ref.shape[0]
    named = cells_row(band_ref[...])
    token = cells_row(tok_ref[...])
    cells = named.shape[1]
    match = (named.astype(jnp.int32) == iota((bands, cells), 0)).astype(jnp.float32)
    before = (iota((cells, cells), 0) < iota((cells, cells), 1)).astype(jnp.float32)
    slot = dot(match.astype(jnp.bfloat16), before.astype(jnp.bfloat16))
    lanes = iota((bands, cells), 1)
    asked = jnp.zeros((bands, cells), jnp.float32)
    for s in range(4):
        hit = jnp.where(slot == s, match, 0.0)
        token_s = jnp.sum(hit * (token + 1.0), -1, keepdims=True) - 1.0
        asked = jnp.where(lanes == s, token_s, asked)
    ask_ref[...] = asked[:, :4].astype(jnp.int32)


def ask(band, tok, bands):
    return pl.pallas_call(
        ask_kernel,
        out_shape=jax.ShapeDtypeStruct((bands, 4), jnp.int32),
        in_specs=[ON_CHIP] * 2,
        out_specs=ON_CHIP,
        compiler_params=pltpu.CompilerParams(vmem_limit_bytes=4 * MIB),
        name="ask",
    )(band, tok)


def take_kernel(band_ref, take_ref):
    band_row = cells_row(band_ref[...])
    cells = band_row.shape[1]
    rows = take_ref.shape[1]
    r, c = iota((cells, cells), 0), iota((cells, cells), 1)
    band_col = jnp.sum(jnp.where(r == c, band_row, 0.0), -1, keepdims=True)
    earlier = (band_col == band_row) & (c < r)
    slot = jnp.sum(jnp.where(earlier, 1.0, 0.0), -1, keepdims=True)
    target = (band_col * 16.0 + slot * 4.0).astype(jnp.int32)
    for part in range(4):
        take_ref[part * cells : (part + 1) * cells, :] = (
            (iota((cells, rows), 1) == target + part).astype(jnp.float32).astype(jnp.bfloat16)
        )


def make_take(band, bands):
    return pl.pallas_call(
        take_kernel,
        out_shape=jax.ShapeDtypeStruct((4 * band.size, bands * 16), jnp.bfloat16),
        in_specs=[ON_CHIP],
        out_specs=ON_CHIP,
        compiler_params=pltpu.CompilerParams(vmem_limit_bytes=4 * MIB),
        name="take",
    )(band)


def pick_rows(asked, rows, cells):
    bands = asked.shape[0]
    spread = (iota((rows, bands), 0) // 16 == iota((rows, bands), 1)).astype(jnp.float32)
    per_row = dot(spread.astype(jnp.bfloat16), asked.astype(jnp.float32).astype(jnp.bfloat16))
    r = iota((rows, 1), 0)
    mine = iota((rows, 4), 1) == (r // 4) % 4
    token_r = jnp.sum(jnp.where(mine, per_row, 0.0), -1, keepdims=True).astype(jnp.int32)
    target = jnp.where(token_r >= 0, (r % 4) * cells + token_r, -1)
    return (iota((rows, 4 * cells), 1) == target).astype(jnp.float32).astype(jnp.bfloat16)


def combine_kernel(code_ref, att0_ref, att1_ref, att2_ref, att3_ref, w0_ref, w1_ref, w3_ref, top_ref, low_ref, x_ref, w_bound_ref, asked_ref, out_ref, send_ref):
    cols = att0_ref.shape[1]
    features = x_ref.shape[1]
    quarter = out_ref.shape[1]
    rank = lax.axis_index("tp")
    x = x_ref[pl.ds(pl.multiple_of(rank * quarter, quarter), quarter), :].astype(jnp.float32)
    code = jnp.full((1, 1), code_ref[0], jnp.int32)
    p = wiggle(code, rank * quarter, quarter, features)
    pick = pick_rows(asked_ref[...], send_ref.shape[0] * 16, quarter)
    total = dot(att0_ref[...], w0_ref[...]) + dot(att1_ref[...], w1_ref[...])
    total = total + dot(att3_ref[...], w3_ref[...])
    total = total + dot(att2_ref[:, : cols // 2], top_ref[...])
    total = total + dot(att2_ref[:, cols // 2 :], low_ref[...])
    made = []
    for s, sign in enumerate(SIGNS):
        part = x if sign == 0.0 else (x + p if sign > 0 else x - p)
        part = (part + total[s * quarter : (s + 1) * quarter]).astype(jnp.bfloat16)
        out_ref[s] = part
        made.append(part)
    forced = dot(jnp.concatenate(made, 0), w_bound_ref[...]).astype(jnp.bfloat16)
    rows = [forced[s * quarter : (s + 1) * quarter] for s in range(3)]
    parts = forced.shape[1] // 128
    table = jnp.concatenate(
        [
            jnp.concatenate([f[:, c * 128 : (c + 1) * 128] for f in rows], 1)
            for c in range(parts)
        ],
        0,
    )
    picked = dot(pick, table).astype(jnp.bfloat16)
    send_ref[...] = picked.reshape(send_ref.shape)


def combine(code, att, w_outs, x, w_bound, asked):
    shapes = [(3, att[0].shape[0] // 3, x.shape[1]), (asked.shape[0], 16, 384)]
    operands = [*att, *w_outs, x, w_bound, asked]
    whole = lambda: (0, 0, 0)
    return pl.pallas_call(
        combine_kernel,
        out_shape=[jax.ShapeDtypeStruct(s, jnp.bfloat16) for s in shapes],
        in_specs=[SCALARS] + [ON_CHIP] * len(operands),
        out_specs=[pl.BlockSpec(s, whole) for s in shapes],
        compiler_params=pltpu.CompilerParams(vmem_limit_bytes=16 * MIB),
        name="combine",
    )(code, *operands)


def inputs_kernel(arrived_ref, take_ref, reg_ref, out_ref, first_ref, last_ref):
    cols, rows, channels = reg_ref.shape
    cells = cols * rows
    table = arrived_ref[...].reshape(take_ref.shape[1], 384)
    taken = dot(take_ref[...], table)
    for part in range(channels // 128):
        lanes = slice(part * 128, (part + 1) * 128)
        reg = reg_ref[:, :, lanes].astype(jnp.float32)
        for s in range(3):
            forced = taken[part * cells : (part + 1) * cells, s * 128 : (s + 1) * 128]
            made = (reg + forced.reshape(cols, rows, 128)).astype(jnp.bfloat16)
            out_ref[:, s * rows : (s + 1) * rows, lanes] = made
            first_ref[s * rows : (s + 1) * rows, lanes] = made[0]
            last_ref[s * rows : (s + 1) * rows, lanes] = made[cols - 1]


def make_inputs(arrived, take, reg):
    cols, rows, channels = reg.shape
    shapes = [(cols, 3 * rows, channels), (3 * rows, channels), (3 * rows, channels)]
    return pl.pallas_call(
        inputs_kernel,
        out_shape=[jax.ShapeDtypeStruct(s, jnp.bfloat16) for s in shapes],
        in_specs=[ON_CHIP] * 3,
        out_specs=[ON_CHIP] * 3,
        compiler_params=pltpu.CompilerParams(vmem_limit_bytes=5 * MIB),
        name="inputs",
    )(arrived, take, reg)


def conv_kernel(x_ref, before_ref, after_ref, w_ref, out_ref, low_ref, mid_ref, high_ref, sum_ref):
    step = pl.program_id(0)
    cols, slab, channels = x_ref.shape
    cells = cols * slab
    rows = slab // 3

    @pl.when(step == 0)
    def _():
        x = x_ref[...].reshape(cells, channels)
        padded = jnp.concatenate([before_ref[...], x, after_ref[...]], 0)
        wide = padded.astype(jnp.float32)
        total = padded.shape[0]
        row = iota((total, 1), 0) % rows
        low_ref[...] = jnp.where(row > 0, pltpu.roll(wide, 1, 0), 0.0).astype(jnp.bfloat16)
        mid_ref[...] = padded
        high_ref[...] = jnp.where(
            row < rows - 1, pltpu.roll(wide, total - 1, 0), 0.0
        ).astype(jnp.bfloat16)

    here = pl.ds(pl.multiple_of(step * slab, slab), cells)
    part = dot(low_ref[here], w_ref[0]) + dot(mid_ref[here], w_ref[1]) + dot(high_ref[here], w_ref[2])

    @pl.when(step == 0)
    def _():
        sum_ref[...] = part

    @pl.when(step == 1)
    def _():
        sum_ref[...] += part

    @pl.when(step == 2)
    def _():
        conv = sum_ref[...] + part
        x = x_ref[...].reshape(cells, channels).astype(jnp.float32)
        result = (x + conv / (1.0 + jnp.exp(-conv))).astype(jnp.bfloat16)
        result = result.reshape(cols, slab, channels)
        for s in range(3):
            out_ref[s] = result[:, s * rows : (s + 1) * rows, :]


def convolve(x, before, after, conv_w):
    cols, slab, channels = x.shape
    shape = (3, cols, slab // 3, channels)
    padded = ((cols + 2) * slab, channels)
    return pl.pallas_call(
        conv_kernel,
        out_shape=jax.ShapeDtypeStruct(shape, jnp.bfloat16),
        grid=(3,),
        in_specs=[ON_CHIP] * 3 + [pl.BlockSpec((3, channels, channels), lambda i: (i, 0, 0))],
        out_specs=pl.BlockSpec(shape, lambda i: (0, 0, 0, 0)),
        scratch_shapes=[pltpu.VMEM(padded, jnp.bfloat16)] * 3
        + [pltpu.VMEM((cols * slab, channels), jnp.float32)],
        compiler_params=pltpu.CompilerParams(vmem_limit_bytes=16 * MIB),
        name="convolve",
    )(x, before, after, conv_w)


def neighbours(last, first, axis):
    count = lax.axis_size(axis)
    up = [(i, i + 1) for i in range(count - 1)]
    down = [(j, i) for i, j in up]
    return lax.ppermute(last, axis, up), lax.ppermute(first, axis, down)


def per_device(
    global_state,
    band_codes,
    norm_gain,
    w_query,
    w_key,
    w_value,
    w_out,
    reg_state,
    src_band,
    src_tok,
    w_bound,
    conv_w,
):
    ranks = lax.axis_size("tp")
    bands = lax.axis_size(BANDS)
    tokens, features = global_state.shape
    half = tokens // 2
    gain = norm_gain[None, :]
    cell_band = src_band.reshape(src_tok.shape)
    w_query, w_key, w_value = (in_hbm(w) for w in (w_query, w_key, w_value))

    up = [(i, (i + 1) % ranks) for i in range(ranks)]
    down = [(j, i) for i, j in up]
    before, after = neighbours(*make_edges(band_codes, in_hbm(global_state)), BANDS)
    w1, w3 = lax.ppermute(w_out, "tp", up), lax.ppermute(w_out, "tp", down)
    asked = ask(cell_band, src_tok, bands)

    q, k, v = project(band_codes, [in_hbm(global_state)], gain, [w_query, w_key, w_value], False)
    q, before, after = lax.optimization_barrier((q, before, after))
    k_halo, v_halo = project(band_codes, [before, after], gain, [w_key, w_value], True)
    k_halo, w1, w3 = lax.optimization_barrier((k_halo, w1, w3))
    middle = w_out.shape[0] // 2
    top, low = lax.ppermute(w1[:middle], "tp", up), lax.ppermute(w3[middle:], "tp", down)
    attended = attend(q, k, v, k_halo, v_halo, ranks, bands)
    attended, asked, top, low = lax.optimization_barrier((attended, asked, top, low))
    attended = [attended[0]] + [
        lax.ppermute(attended[d], "tp", [(i, (i + d) % ranks) for i in range(ranks)])
        for d in range(1, ranks)
    ]
    asked = lax.all_to_all(asked[:, None, :], BANDS, 0, 0, tiled=True)[:, 0, :]
    global_out, send = combine(
        band_codes, attended, [w_out, w1, w3, top, low], global_state, w_bound, asked
    )
    cell_band, send = lax.optimization_barrier((cell_band, send))
    take = make_take(cell_band, bands)
    arrived = lax.all_to_all(send, BANDS, 0, 0, tiled=True)
    inputs, first, last = make_inputs(arrived, take, reg_state)
    before, after = neighbours(last, first, CELLS)
    return global_out, convolve(inputs, before, after, in_hbm(conv_w))


def solution(mesh):
    placed = (
        P(("sec", "tile"), None),
        P(("sec", "tile")),
        P(),
        P(None, "tp"),
        P(None, "tp"),
        P(None, "tp"),
        P("tp", None),
        P(("sec", "tile", "tp"), None, None),
        P(("sec", "tile", "tp"), None, None),
        P(("sec", "tile", "tp"), None),
        P(),
        P(),
    )
    return jax.shard_map(
        per_device,
        mesh=mesh,
        in_specs=placed,
        out_specs=(
            P(None, ("sec", "tile", "tp"), None),
            P(None, ("sec", "tile", "tp"), None, None),
        ),
        check_vma=False,
    )
```

```python
import functools

import jax
import jax.numpy as jnp
from jax import lax
from jax.experimental import pallas as pl
from jax.experimental.pallas import tpu as pltpu
from jax.sharding import Mesh
from jax.sharding import PartitionSpec as P

HD = 64
SIGNS = (0.0, 1.0, -1.0)
BANDS = ("sec", "x", "z", "core")
CELLS = BANDS + ("tp",)
ALONG = ("sec", "z")
ACROSS = ("x", "core")
LOG2E = 1.4426950408889634
MIB = 1024 * 1024
ON_CHIP = pl.BlockSpec(memory_space=pltpu.VMEM)
SCALARS = pl.BlockSpec(memory_space=pltpu.SMEM)

mix_band = 73856093
mix_token = 19349663
mix_feature = 83492791
mix_again = 668265261


def iota(shape, dim):
    return lax.broadcasted_iota(jnp.int32, shape, dim)


def in_hbm(x):
    return pltpu.with_memory_space_constraint(x, pltpu.HBM)


def dot(a, b):
    return jnp.dot(a, b, preferred_element_type=jnp.float32)


def dot_t(a, b):
    return lax.dot_general(a, b, (((1,), (1,)), ((), ())), preferred_element_type=jnp.float32)


def wiggle(code, first_token, rows, features):
    by_row = code * mix_band + (first_token + iota((rows, 1), 0)) * mix_token
    mixed = by_row + iota((1, features), 1) * mix_feature
    mixed = lax.bitwise_xor(mixed, lax.shift_right_arithmetic(mixed, jnp.full_like(mixed, 15)))
    mixed = mixed * mix_again
    mixed = lax.bitwise_xor(mixed, lax.shift_right_arithmetic(mixed, jnp.full_like(mixed, 13)))
    level = lax.bitwise_and(mixed, 1023).astype(jnp.float32)
    return (level - 511.5) * (0.5 / 295.6)


def edges_kernel(code_ref, x_ref, last_ref, first_ref, sems):
    half = x_ref.shape[0] // 2
    copies = [
        pltpu.make_async_copy(x_ref.at[pl.ds(half, half)], last_ref.at[pl.ds(0, half)], sems.at[0]),
        pltpu.make_async_copy(x_ref.at[pl.ds(0, half)], first_ref.at[pl.ds(0, half)], sems.at[1]),
    ]
    for copy in copies:
        copy.start()
    code = jnp.full((16, x_ref.shape[1]), code_ref[0], jnp.int32)
    lane = iota(code.shape, 1)
    shift = jnp.where(lane == 0, 16, jnp.where(lane == 1, 8, 0))
    digit = lax.bitwise_and(lax.shift_right_arithmetic(code, shift), 255)
    digit = digit.astype(jnp.float32).astype(jnp.bfloat16)
    last_ref[half:] = digit
    first_ref[half:] = digit
    for copy in copies:
        copy.wait()


def make_edges(code, x):
    tokens, features = x.shape
    shape = jax.ShapeDtypeStruct((tokens // 2 + 16, features), jnp.bfloat16)
    return pl.pallas_call(
        edges_kernel,
        out_shape=[shape, shape],
        in_specs=[SCALARS, pl.BlockSpec(memory_space=pltpu.HBM)],
        out_specs=[ON_CHIP] * 2,
        scratch_shapes=[pltpu.SemaphoreType.DMA((2,))],
        compiler_params=pltpu.CompilerParams(vmem_limit_bytes=4 * MIB),
        name="edges",
    )(code, x)


def project_kernel(code_ref, *refs, halo):
    step = pl.program_id(0)
    both_ref, inv_ref, held_ref, sems = refs[-4:]
    if halo:
        before_ref, after_ref, gain_ref, *refs = refs[:-4]
        rows = before_ref.shape[0] - 16
        first = (1 - step) * rows
        digits = jnp.where(
            step == 0, before_ref[rows : rows + 16, 0:128], after_ref[rows : rows + 16, 0:128]
        ).astype(jnp.float32)[0:1]
        lane = iota((1, 128), 1)
        place = jnp.where(lane == 0, 65536.0, jnp.where(lane == 1, 256.0, 1.0))
        code = jnp.sum(jnp.where(lane < 3, digits * place, 0.0), -1, keepdims=True)
        code = code.astype(jnp.int32)
    else:
        x_ref, gain_ref, *refs = refs[:-4]
        rows = x_ref.shape[0]
        first = step * rows
        code = jnp.full((1, 1), code_ref[0], jnp.int32)
    weights, outs = refs[: len(refs) // 2], refs[len(refs) // 2 :]
    copies = [
        pltpu.make_async_copy(w_ref, held_ref.at[i], sems.at[i]) for i, w_ref in enumerate(weights)
    ]

    @pl.when(step == 0)
    def _():
        for copy in copies:
            copy.start()

    features = both_ref.shape[1]
    gain = gain_ref[...].astype(jnp.float32).reshape(1, features)
    chunk, block = 16, 128
    for at in range(0, rows, block):
        for r in range(at, at + block, chunk):
            if halo:
                x = jnp.where(step == 0, before_ref[r : r + chunk], after_ref[r : r + chunk])
            else:
                x = x_ref[r : r + chunk]
            x = x.astype(jnp.float32)
            p = wiggle(code, first + r, chunk, features)
            place = 2 * at + (r - at)
            both_ref[place : place + chunk] = (x * gain).astype(jnp.bfloat16)
            both_ref[place + block : place + block + chunk] = (p * gain).astype(jnp.bfloat16)
            for s, sign in enumerate(SIGNS):
                state = x if sign == 0.0 else (x + p if sign > 0 else x - p)
                mean = jnp.sum(state * state, -1, keepdims=True) * (1.0 / features)
                inv_ref[s, r : r + chunk] = lax.rsqrt(mean + 1e-06)
        if at == 0:

            @pl.when(step == 0)
            def _():
                for copy in copies:
                    copy.wait()

        here = slice(at, at + block)
        for index, out_ref in enumerate(outs):
            scale = HD**-0.5 * LOG2E if (index == 0 and not halo) else 1.0
            made = dot(both_ref[2 * at : 2 * at + 2 * block], held_ref[index])
            base, diff = made[:block], made[block:]
            for s, sign in enumerate(SIGNS):
                full = base if sign == 0.0 else (base + diff if sign > 0 else base - diff)
                out_ref[s, here] = (full * (inv_ref[s, here] * scale)).astype(jnp.bfloat16)


def project(code, arrays, gain, weights, halo):
    features = gain.shape[0]
    cols = weights[0].shape[1]
    if halo:
        tokens = 2 * (arrays[0].shape[0] - 16)
        specs = [ON_CHIP for a in arrays]
    else:
        tokens = arrays[0].shape[0]
        specs = [pl.BlockSpec((tokens // 2, features), lambda i: (i, 0))]
    rows = tokens // 2
    return pl.pallas_call(
        functools.partial(project_kernel, halo=halo),
        out_shape=[jax.ShapeDtypeStruct((3, tokens, cols), jnp.bfloat16) for _ in weights],
        grid=(2,),
        in_specs=[SCALARS]
        + specs
        + [pl.BlockSpec(gain.shape, lambda i: (0,))]
        + [pl.BlockSpec(memory_space=pltpu.HBM) for w in weights],
        out_specs=[pl.BlockSpec((3, rows, cols), lambda i: (0, i, 0)) for _ in weights],
        scratch_shapes=[
            pltpu.VMEM((2 * rows, features), jnp.bfloat16),
            pltpu.VMEM((3, rows, 1), jnp.float32),
            pltpu.VMEM((len(weights), features, cols), jnp.bfloat16),
            pltpu.SemaphoreType.DMA((len(weights),)),
        ],
        compiler_params=pltpu.CompilerParams(vmem_limit_bytes=12 * MIB),
        name="project_halo" if halo else "project_own",
    )(code, *arrays, gain, *weights)


def attend_kernel(q_ref, k_ref, v_ref, k_halo_ref, v_halo_ref, *refs, bands):
    *out_refs, held_ref = refs
    tokens, cols = q_ref.shape[1:]
    half = tokens // 2
    band = lax.axis_index(BANDS)
    left = band > 0
    right = band < bands - 1
    head_of = iota((1, cols), 1) // HD
    k = k_ref[0]
    v = v_ref[0]
    row = iota((tokens, 1), 0)
    there = jnp.where(row < half, left.astype(jnp.int32), right.astype(jnp.int32)) > 0
    k_halo = jnp.where(there, k_halo_ref[0], k)
    v_halo = v_halo_ref[0]
    one = there.astype(jnp.bfloat16)
    v_halo = v_halo * one
    block = half
    for part in range(tokens // block):
        q = q_ref[0, part * block : (part + 1) * block, :]
        gathered = jnp.zeros((block, cols), jnp.float32)
        for head in range(cols // HD):
            mine = head_of == head
            q_head = jnp.where(mine, q, jnp.zeros_like(q))
            own = dot_t(q_head, k)
            far = dot_t(q_head, k_halo)
            top = jnp.maximum(
                jnp.max(own, -1, keepdims=True), jnp.max(far, -1, keepdims=True)
            )
            own = jnp.exp2(own - top).astype(jnp.bfloat16)
            far = jnp.exp2(far - top).astype(jnp.bfloat16)
            v_own = jnp.where(mine, v, jnp.ones_like(v))
            v_far = jnp.where(mine, v_halo, jnp.broadcast_to(one, v.shape))
            acc = dot(own, v_own) + dot(far, v_far)
            total = pltpu.roll(acc, cols // 2, 1)
            gathered = jnp.where(mine, acc / total, gathered)
        held_ref[part * block : (part + 1) * block] = gathered.astype(jnp.bfloat16)
    ranks = len(out_refs)
    quarter = tokens // ranks
    rank = lax.axis_index("tp")
    for distance, out_ref in enumerate(out_refs):
        first = pl.multiple_of(lax.rem(rank + distance, ranks) * quarter, quarter)
        out_ref[...] = held_ref[pl.ds(first, quarter), :]


def attend(q, k, v, k_halo, v_halo, ranks, bands):
    forwards, tokens, cols = q.shape
    spec = pl.BlockSpec((1, tokens, cols), lambda i: (i, 0, 0))
    quarter = tokens // ranks
    return pl.pallas_call(
        functools.partial(attend_kernel, bands=bands),
        out_shape=[jax.ShapeDtypeStruct((forwards * quarter, cols), jnp.bfloat16)] * ranks,
        grid=(forwards,),
        in_specs=[spec] * 5,
        out_specs=[pl.BlockSpec((quarter, cols), lambda i: (i, 0))] * ranks,
        scratch_shapes=[pltpu.VMEM((tokens, cols), jnp.bfloat16)],
        compiler_params=pltpu.CompilerParams(vmem_limit_bytes=14 * MIB),
        name="attend",
    )(q, k, v, k_halo, v_halo)


def cells_row(x):
    cols, rows = x.shape
    cells = cols * rows
    spread = (iota((rows, cells), 1) % rows == iota((rows, cells), 0)).astype(jnp.float32)
    wide = dot(x.astype(jnp.float32).astype(jnp.bfloat16), spread.astype(jnp.bfloat16))
    mine = iota((cols, cells), 1) // rows == iota((cols, cells), 0)
    return jnp.sum(jnp.where(mine, wide, 0.0), 0, keepdims=True)


def place_of(band):
    return (band // 32) * 4 + (band // 2) % 4, ((band // 8) % 4) * 2 + band % 2


def ask_kernel(band_ref, tok_ref, ask_ref, *, bands):
    named = cells_row(band_ref[...])
    token = cells_row(tok_ref[...])
    cells = named.shape[1]
    match = (named.astype(jnp.int32) == iota((bands, cells), 0)).astype(jnp.float32)
    before = (iota((cells, cells), 0) < iota((cells, cells), 1)).astype(jnp.float32)
    slot = dot(match.astype(jnp.bfloat16), before.astype(jnp.bfloat16))
    lanes = iota((bands, cells), 1)
    asked = jnp.zeros((bands, cells), jnp.float32)
    for s in range(4):
        hit = jnp.where(slot == s, match, 0.0)
        token_s = jnp.sum(hit * (token + 1.0), -1, keepdims=True) - 1.0
        asked = jnp.where(lanes == s, token_s, asked)
    along, wide = ask_ref.shape
    lane = iota((4, wide), 1)
    four = (lane % 4 == iota((4, wide), 0)).astype(jnp.float32).astype(jnp.bfloat16)
    spread = dot(asked[:, :4].astype(jnp.bfloat16), four)
    _, xc = place_of(iota((bands, 1), 0))
    spread = jnp.where(iota((bands, wide), 1) // 4 == xc, spread, 0.0)
    z, _ = place_of(iota((1, bands), 1))
    rows = (iota((along, bands), 0) == z).astype(jnp.float32).astype(jnp.bfloat16)
    ask_ref[...] = dot(rows, spread.astype(jnp.bfloat16)).astype(jnp.int32)


def ask(band, tok, bands):
    along, across = lax.axis_size(ALONG), lax.axis_size(ACROSS)
    return pl.pallas_call(
        functools.partial(ask_kernel, bands=bands),
        out_shape=jax.ShapeDtypeStruct((along, across * 4), jnp.int32),
        in_specs=[ON_CHIP] * 2,
        out_specs=ON_CHIP,
        compiler_params=pltpu.CompilerParams(vmem_limit_bytes=4 * MIB),
        name="ask",
    )(band, tok)


def take_kernel(band_ref, conv_hbm_ref, take_ref, outer_ref, sems):
    copies = [
        pltpu.make_async_copy(
            conv_hbm_ref.at[pl.ds(6 * i, 3)], outer_ref.at[pl.ds(3 * i, 3)], sems.at[i]
        )
        for i in range(2)
    ]
    for copy in copies:
        copy.start()
    band_row = cells_row(band_ref[...])
    cells = band_row.shape[1]
    rows = take_ref.shape[1]
    r, c = iota((cells, cells), 0), iota((cells, cells), 1)
    band_col = jnp.sum(jnp.where(r == c, band_row, 0.0), -1, keepdims=True)
    earlier = (band_col == band_row) & (c < r)
    slot = jnp.sum(jnp.where(earlier, 1.0, 0.0), -1, keepdims=True)
    target = (band_col * 16.0 + slot * 4.0).astype(jnp.int32)
    for part in range(4):
        take_ref[part * cells : (part + 1) * cells, :] = (
            (iota((cells, rows), 1) == target + part).astype(jnp.float32).astype(jnp.bfloat16)
        )
    for copy in copies:
        copy.wait()


def make_take(band, bands, conv_w):
    return pl.pallas_call(
        take_kernel,
        out_shape=[
            jax.ShapeDtypeStruct((4 * band.size, bands * 16), jnp.bfloat16),
            jax.ShapeDtypeStruct((6, *conv_w.shape[1:]), conv_w.dtype),
        ],
        in_specs=[ON_CHIP, pl.BlockSpec(memory_space=pltpu.HBM)],
        out_specs=[ON_CHIP] * 2,
        scratch_shapes=[pltpu.SemaphoreType.DMA((2,))],
        compiler_params=pltpu.CompilerParams(vmem_limit_bytes=4 * MIB),
        name="take",
    )(band, conv_w)


def turn_kernel(x_ref, out_ref):
    count, wide = x_ref.shape
    others, width = out_ref.shape
    x = x_ref[...].astype(jnp.float32).astype(jnp.bfloat16)
    lane = iota((wide, width), 1)
    row = iota((wide, width), 0)
    for other in range(others):
        choose = (row == other * 4 + lane % 4).astype(jnp.float32).astype(jnp.bfloat16)
        spread = dot(x, choose)
        mine = iota((count, width), 1) // 4 == iota((count, width), 0)
        out_ref[other : other + 1] = jnp.sum(
            jnp.where(mine, spread, 0.0), 0, keepdims=True
        ).astype(jnp.int32)


def turn(x):
    count, wide = x.shape
    return pl.pallas_call(
        turn_kernel,
        out_shape=jax.ShapeDtypeStruct((wide // 4, 4 * count), jnp.int32),
        in_specs=[ON_CHIP],
        out_specs=ON_CHIP,
        compiler_params=pltpu.CompilerParams(vmem_limit_bytes=2 * MIB),
        name="turn",
    )(x)


def pick_rows(asked, rows, cells):
    across, wide = asked.shape
    r = iota((rows, 1), 0)
    z, xc = place_of(r // 16)
    spread = (iota((rows, across), 1) == xc).astype(jnp.float32).astype(jnp.bfloat16)
    per_row = dot(spread, asked.astype(jnp.float32).astype(jnp.bfloat16))
    mine = iota((rows, wide), 1) == z * 4 + (r // 4) % 4
    token_r = jnp.sum(jnp.where(mine, per_row, 0.0), -1, keepdims=True).astype(jnp.int32)
    target = jnp.where(token_r >= 0, (r % 4) * cells + token_r, -1)
    return (iota((rows, 4 * cells), 1) == target).astype(jnp.float32).astype(jnp.bfloat16)


def combine_kernel(code_ref, att0_ref, att1_ref, att2_ref, att3_ref, w0_ref, w1_ref, w3_ref, top_ref, low_ref, x_ref, w_bound_ref, asked_ref, out_ref, send_ref):
    cols = att0_ref.shape[1]
    features = x_ref.shape[1]
    quarter = out_ref.shape[1]
    rank = lax.axis_index("tp")
    x = x_ref[pl.ds(pl.multiple_of(rank * quarter, quarter), quarter), :].astype(jnp.float32)
    code = jnp.full((1, 1), code_ref[0], jnp.int32)
    p = wiggle(code, rank * quarter, quarter, features)
    pick = pick_rows(asked_ref[...], send_ref.shape[0] * 16, quarter)
    total = dot(att0_ref[...], w0_ref[...]) + dot(att1_ref[...], w1_ref[...])
    total = total + dot(att3_ref[...], w3_ref[...])
    total = total + dot(att2_ref[:, : cols // 2], top_ref[...])
    total = total + dot(att2_ref[:, cols // 2 :], low_ref[...])
    made = []
    for s, sign in enumerate(SIGNS):
        part = x if sign == 0.0 else (x + p if sign > 0 else x - p)
        part = (part + total[s * quarter : (s + 1) * quarter]).astype(jnp.bfloat16)
        out_ref[s] = part
        made.append(part)
    forced = dot(jnp.concatenate(made, 0), w_bound_ref[...]).astype(jnp.bfloat16)
    rows = [forced[s * quarter : (s + 1) * quarter] for s in range(3)]
    parts = forced.shape[1] // 128
    table = jnp.concatenate(
        [
            jnp.concatenate([f[:, c * 128 : (c + 1) * 128] for f in rows], 1)
            for c in range(parts)
        ],
        0,
    )
    picked = dot(pick, table).astype(jnp.bfloat16)
    send_ref[...] = picked.reshape(send_ref.shape)


def combine(code, att, w_outs, x, w_bound, asked, bands):
    shapes = [(3, att[0].shape[0] // 3, x.shape[1]), (bands, 16, 384)]
    operands = [*att, *w_outs, x, w_bound, asked]
    whole = lambda: (0, 0, 0)
    return pl.pallas_call(
        combine_kernel,
        out_shape=[jax.ShapeDtypeStruct(s, jnp.bfloat16) for s in shapes],
        in_specs=[SCALARS] + [ON_CHIP] * len(operands),
        out_specs=[pl.BlockSpec(s, whole) for s in shapes],
        compiler_params=pltpu.CompilerParams(vmem_limit_bytes=16 * MIB),
        name="combine",
    )(code, *operands)


def inputs_kernel(arrived_ref, take_ref, reg_ref, out_ref, first_ref, last_ref):
    cols, rows, channels = reg_ref.shape
    cells = cols * rows
    table = arrived_ref[...].reshape(take_ref.shape[1], 384)
    taken = dot(take_ref[...], table)
    for part in range(channels // 128):
        lanes = slice(part * 128, (part + 1) * 128)
        reg = reg_ref[:, :, lanes].astype(jnp.float32)
        for s in range(3):
            forced = taken[part * cells : (part + 1) * cells, s * 128 : (s + 1) * 128]
            made = (reg + forced.reshape(cols, rows, 128)).astype(jnp.bfloat16)
            out_ref[:, s * rows : (s + 1) * rows, lanes] = made
            first_ref[s * rows : (s + 1) * rows, lanes] = made[0]
            last_ref[s * rows : (s + 1) * rows, lanes] = made[cols - 1]


def make_inputs(arrived, take, reg):
    cols, rows, channels = reg.shape
    shapes = [(cols, 3 * rows, channels), (3 * rows, channels), (3 * rows, channels)]
    return pl.pallas_call(
        inputs_kernel,
        out_shape=[jax.ShapeDtypeStruct(s, jnp.bfloat16) for s in shapes],
        in_specs=[ON_CHIP] * 3,
        out_specs=[ON_CHIP] * 3,
        compiler_params=pltpu.CompilerParams(vmem_limit_bytes=5 * MIB),
        name="inputs",
    )(arrived, take, reg)


def row_shifts(x, rows):
    wide = x.astype(jnp.float32)
    total = x.shape[0]
    row = iota((total, 1), 0) % rows
    low = jnp.where(row > 0, pltpu.roll(wide, 1, 0), 0.0).astype(jnp.bfloat16)
    high = jnp.where(row < rows - 1, pltpu.roll(wide, total - 1, 0), 0.0).astype(jnp.bfloat16)
    return low, x, high


def inner_kernel(x_ref, outer_ref, conv_hbm_ref, sum_ref, held_ref, sem):
    copy = pltpu.make_async_copy(conv_hbm_ref.at[pl.ds(3, 3)], held_ref, sem)
    copy.start()
    cols, slab, channels = x_ref.shape
    cells = cols * slab
    shifts = row_shifts(x_ref[...].reshape(cells, channels), slab // 3)
    before = after = None
    for b, x in enumerate(shifts):
        one = dot(x[: cells - slab], outer_ref[b])
        two = dot(x[slab:], outer_ref[3 + b])
        before = one if before is None else before + one
        after = two if after is None else after + two
    copy.wait()
    middle = None
    for b, x in enumerate(shifts):
        one = dot(x, held_ref[b])
        middle = one if middle is None else middle + one
    sum_ref[:slab] = middle[:slab] + after[:slab]
    sum_ref[slab : cells - slab] = middle[slab : cells - slab] + before[: cells - 2 * slab] + after[slab:]
    sum_ref[cells - slab :] = middle[cells - slab :] + before[cells - 2 * slab :]


def convolve_inner(x, outer, conv_w):
    cols, slab, channels = x.shape
    return pl.pallas_call(
        inner_kernel,
        out_shape=jax.ShapeDtypeStruct((cols * slab, channels), jnp.float32),
        in_specs=[ON_CHIP] * 2 + [pl.BlockSpec(memory_space=pltpu.HBM)],
        out_specs=ON_CHIP,
        scratch_shapes=[
            pltpu.VMEM((3, channels, channels), jnp.bfloat16),
            pltpu.SemaphoreType.DMA(()),
        ],
        compiler_params=pltpu.CompilerParams(vmem_limit_bytes=16 * MIB),
        name="convolve_inner",
    )(x, outer, conv_w)


def finish_kernel(x_ref, before_ref, after_ref, outer_ref, sum_ref, out_ref):
    cols, slab, channels = x_ref.shape
    rows = slab // 3
    sides = []
    for side, ref in enumerate((before_ref, after_ref)):
        total = None
        for b, x in enumerate(row_shifts(ref[...], rows)):
            one = dot(x, outer_ref[3 * side + b])
            total = one if total is None else total + one
        sides.append(total)
    for col in range(cols):
        conv = sum_ref[col * slab : (col + 1) * slab]
        if col == 0:
            conv = conv + sides[0]
        if col == cols - 1:
            conv = conv + sides[1]
        result = x_ref[col].astype(jnp.float32) + conv / (1.0 + jnp.exp(-conv))
        result = result.astype(jnp.bfloat16)
        for s in range(3):
            out_ref[s, col] = result[s * rows : (s + 1) * rows]


def convolve_finish(x, before, after, outer, total):
    cols, slab, channels = x.shape
    shape = (3, cols, slab // 3, channels)
    return pl.pallas_call(
        finish_kernel,
        out_shape=jax.ShapeDtypeStruct(shape, jnp.bfloat16),
        in_specs=[ON_CHIP] * 5,
        out_specs=pl.BlockSpec(shape, lambda: (0, 0, 0, 0)),
        compiler_params=pltpu.CompilerParams(vmem_limit_bytes=8 * MIB),
        name="convolve_finish",
    )(x, before, after, outer, total)


def neighbours(last, first, axis):
    count = lax.axis_size(axis)
    up = [(i, i + 1) for i in range(count - 1)]
    down = [(j, i) for i, j in up]
    return lax.ppermute(last, axis, up), lax.ppermute(first, axis, down)


def per_device(
    global_state,
    band_codes,
    norm_gain,
    w_query,
    w_key,
    w_value,
    w_out,
    reg_state,
    src_band,
    src_tok,
    w_bound,
    conv_w,
):
    ranks = lax.axis_size("tp")
    bands = lax.axis_size(BANDS)
    tokens, features = global_state.shape
    half = tokens // 2
    gain = norm_gain
    cell_band = src_band.reshape(src_tok.shape)
    w_query, w_key, w_value = (in_hbm(w) for w in (w_query, w_key, w_value))

    up = [(i, (i + 1) % ranks) for i in range(ranks)]
    down = [(j, i) for i, j in up]
    before, after = neighbours(*make_edges(band_codes, in_hbm(global_state)), BANDS)
    w1, w3 = lax.ppermute(w_out, "tp", up), lax.ppermute(w_out, "tp", down)
    asked = ask(cell_band, src_tok, bands)

    q, k, v = project(band_codes, [in_hbm(global_state)], gain, [w_query, w_key, w_value], False)
    q, w1, w3 = lax.optimization_barrier((q, w1, w3))
    middle = w_out.shape[0] // 2
    top, low = lax.ppermute(w1[:middle], "tp", up), lax.ppermute(w3[middle:], "tp", down)
    q, before, after = lax.optimization_barrier((q, before, after))
    k_halo, v_halo = project(band_codes, [before, after], gain, [w_key, w_value], True)
    attended = attend(q, k, v, k_halo, v_halo, ranks, bands)
    attended, asked, top, low = lax.optimization_barrier((attended, asked, top, low))
    attended = [attended[0]] + [
        lax.ppermute(attended[d], "tp", [(i, (i + d) % ranks) for i in range(ranks)])
        for d in range(1, ranks)
    ]
    asked = lax.all_to_all(asked[:, None, :], ALONG, 0, 0, tiled=True)[:, 0, :]
    asked = lax.all_to_all(turn(asked)[:, None, :], ACROSS, 0, 0, tiled=True)[:, 0, :]
    global_out, send = combine(
        band_codes, attended, [w_out, w1, w3, top, low], global_state, w_bound, asked, bands
    )
    cell_band, send = lax.optimization_barrier((cell_band, send))
    conv_w = in_hbm(conv_w)
    take, outer = make_take(cell_band, bands, conv_w)
    arrived = lax.all_to_all(send, BANDS, 0, 0, tiled=True)
    inputs, first, last = make_inputs(arrived, take, reg_state)
    before, after = neighbours(last, first, CELLS)
    total = convolve_inner(inputs, outer, conv_w)
    return global_out, convolve_finish(inputs, before, after, outer, total)


def solution(mesh):
    parts = Mesh(
        mesh.devices.reshape(mesh.shape["sec"], 4, 4, 2, mesh.shape["tp"]), CELLS
    )
    placed = (
        P(BANDS, None),
        P(BANDS),
        P(),
        P(None, "tp"),
        P(None, "tp"),
        P(None, "tp"),
        P("tp", None),
        P(CELLS, None, None),
        P(CELLS, None, None),
        P(CELLS, None),
        P(),
        P(),
    )
    return jax.shard_map(
        per_device,
        mesh=parts,
        in_specs=placed,
        out_specs=(P(None, CELLS, None), P(None, CELLS, None, None)),
        check_vma=False,
    )
```

```python
import functools

import jax
import jax.numpy as jnp
from jax import lax
from jax.experimental import pallas as pl
from jax.experimental.pallas import tpu as pltpu
from jax.sharding import PartitionSpec as P

HD = 64
SIGNS = (0.0, 1.0, -1.0)
BANDS = ("sec", "tile")
CELLS = ("sec", "tile", "tp")
LOG2E = 1.4426950408889634
MIB = 1024 * 1024
ON_CHIP = pl.BlockSpec(memory_space=pltpu.VMEM)
SCALARS = pl.BlockSpec(memory_space=pltpu.SMEM)

mix_band = 73856093
mix_token = 19349663
mix_feature = 83492791
mix_again = 668265261


def iota(shape, dim):
    return lax.broadcasted_iota(jnp.int32, shape, dim)


def in_hbm(x):
    return pltpu.with_memory_space_constraint(x, pltpu.HBM)


def dot(a, b):
    return jnp.dot(a, b, preferred_element_type=jnp.float32)


def dot_t(a, b):
    return lax.dot_general(a, b, (((1,), (1,)), ((), ())), preferred_element_type=jnp.float32)


def wiggle(code, first_token, rows, features):
    by_row = code * mix_band + (first_token + iota((rows, 1), 0)) * mix_token
    mixed = by_row + iota((1, features), 1) * mix_feature
    mixed = lax.bitwise_xor(mixed, lax.shift_right_arithmetic(mixed, jnp.full_like(mixed, 15)))
    mixed = mixed * mix_again
    mixed = lax.bitwise_xor(mixed, lax.shift_right_arithmetic(mixed, jnp.full_like(mixed, 13)))
    level = lax.bitwise_and(mixed, 1023).astype(jnp.float32)
    return (level - 511.5) * (0.5 / 295.6)


def edges_kernel(code_ref, x_ref, *refs):
    *refs, sems = refs
    count = (len(refs) - 2) // 2
    weights, (last_ref, first_ref, *held) = refs[:count], refs[count:]
    half = x_ref.shape[0] // 2
    pairs = [
        (x_ref.at[pl.ds(half, half)], last_ref.at[pl.ds(0, half)]),
        (x_ref.at[pl.ds(0, half)], first_ref.at[pl.ds(0, half)]),
        *zip(weights, held),
    ]
    copies = [pltpu.make_async_copy(a, b, sems.at[i]) for i, (a, b) in enumerate(pairs)]
    for copy in copies:
        copy.start()
    code = jnp.full((16, x_ref.shape[1]), code_ref[0], jnp.int32)
    lane = iota(code.shape, 1)
    shift = jnp.where(lane == 0, 16, jnp.where(lane == 1, 8, 0))
    digit = lax.bitwise_and(lax.shift_right_arithmetic(code, shift), 255)
    digit = digit.astype(jnp.float32).astype(jnp.bfloat16)
    last_ref[half:] = digit
    first_ref[half:] = digit
    for copy in copies:
        copy.wait()


def make_edges(code, x, weights):
    tokens, features = x.shape
    shapes = [(tokens // 2 + 16, features)] * 2 + [w.shape for w in weights]
    return pl.pallas_call(
        edges_kernel,
        out_shape=[jax.ShapeDtypeStruct(s, jnp.bfloat16) for s in shapes],
        in_specs=[SCALARS] + [pl.BlockSpec(memory_space=pltpu.HBM)] * (1 + len(weights)),
        out_specs=[ON_CHIP] * len(shapes),
        scratch_shapes=[pltpu.SemaphoreType.DMA((2 + len(weights),))],
        compiler_params=pltpu.CompilerParams(vmem_limit_bytes=2 * MIB),
        name="edges",
    )(code, x, *weights)


def project_kernel(code_ref, *refs, halo):
    step = pl.program_id(0)
    both_ref, inv_ref = refs[-2:]
    if halo:
        before_ref, after_ref, gain_ref, *refs = refs[:-2]
        rows = before_ref.shape[0] - 16
        first = (1 - step) * rows
        digits = jnp.where(
            step == 0, before_ref[rows : rows + 16, 0:128], after_ref[rows : rows + 16, 0:128]
        ).astype(jnp.float32)[0:1]
        lane = iota((1, 128), 1)
        place = jnp.where(lane == 0, 65536.0, jnp.where(lane == 1, 256.0, 1.0))
        code = jnp.sum(jnp.where(lane < 3, digits * place, 0.0), -1, keepdims=True)
        code = code.astype(jnp.int32)
    else:
        x_ref, gain_ref, *refs = refs[:-2]
        rows = x_ref.shape[0]
        first = step * rows
        code = jnp.full((1, 1), code_ref[0], jnp.int32)
    weights, outs = refs[: len(refs) // 2], refs[len(refs) // 2 :]
    features = both_ref.shape[1]
    gain = gain_ref[...].astype(jnp.float32).reshape(1, features)
    chunk, block = 16, 128
    for at in range(0, rows, block):
        for r in range(at, at + block, chunk):
            if halo:
                x = jnp.where(step == 0, before_ref[r : r + chunk], after_ref[r : r + chunk])
            else:
                x = x_ref[r : r + chunk]
            x = x.astype(jnp.float32)
            p = wiggle(code, first + r, chunk, features)
            place = 2 * at + (r - at)
            both_ref[place : place + chunk] = (x * gain).astype(jnp.bfloat16)
            both_ref[place + block : place + block + chunk] = (p * gain).astype(jnp.bfloat16)
            for s, sign in enumerate(SIGNS):
                state = x if sign == 0.0 else (x + p if sign > 0 else x - p)
                mean = jnp.sum(state * state, -1, keepdims=True) * (1.0 / features)
                inv_ref[s, r : r + chunk] = lax.rsqrt(mean + 1e-06)
        here = slice(at, at + block)
        for index, (w_ref, out_ref) in enumerate(zip(weights, outs)):
            scale = HD**-0.5 * LOG2E if (index == 0 and not halo) else 1.0
            made = dot(both_ref[2 * at : 2 * at + 2 * block], w_ref[...])
            base, diff = made[:block], made[block:]
            for s, sign in enumerate(SIGNS):
                full = base if sign == 0.0 else (base + diff if sign > 0 else base - diff)
                out_ref[s, here] = (full * (inv_ref[s, here] * scale)).astype(jnp.bfloat16)


def project(code, arrays, gain, weights, halo):
    features = gain.shape[0]
    cols = weights[0].shape[1]
    if halo:
        tokens = 2 * (arrays[0].shape[0] - 16)
        specs = [ON_CHIP for a in arrays]
    else:
        tokens = arrays[0].shape[0]
        specs = [pl.BlockSpec((tokens // 2, features), lambda i: (i, 0))]
    rows = tokens // 2
    return pl.pallas_call(
        functools.partial(project_kernel, halo=halo),
        out_shape=[jax.ShapeDtypeStruct((3, tokens, cols), jnp.bfloat16) for _ in weights],
        grid=(2,),
        in_specs=[SCALARS]
        + specs
        + [pl.BlockSpec(gain.shape, lambda i: (0,))]
        + [ON_CHIP for w in weights],
        out_specs=[pl.BlockSpec((3, rows, cols), lambda i: (0, i, 0)) for _ in weights],
        scratch_shapes=[
            pltpu.VMEM((2 * rows, features), jnp.bfloat16),
            pltpu.VMEM((3, rows, 1), jnp.float32),
        ],
        compiler_params=pltpu.CompilerParams(vmem_limit_bytes=12 * MIB),
        name="project_halo" if halo else "project_own",
    )(code, *arrays, gain, *weights)


def attend_kernel(q_ref, k_ref, v_ref, k_halo_ref, v_halo_ref, *refs, bands):
    *out_refs, held_ref = refs
    tokens, cols = q_ref.shape[1:]
    half = tokens // 2
    band = lax.axis_index(BANDS)
    left = band > 0
    right = band < bands - 1
    head_of = iota((1, cols), 1) // HD
    k = k_ref[0]
    v = v_ref[0]
    row = iota((tokens, 1), 0)
    there = jnp.where(row < half, left.astype(jnp.int32), right.astype(jnp.int32)) > 0
    k_halo = jnp.where(there, k_halo_ref[0], k)
    v_halo = v_halo_ref[0]
    one = there.astype(jnp.bfloat16)
    v_halo = v_halo * one
    block = half
    for part in range(tokens // block):
        q = q_ref[0, part * block : (part + 1) * block, :]
        gathered = jnp.zeros((block, cols), jnp.float32)
        for head in range(cols // HD):
            mine = head_of == head
            q_head = jnp.where(mine, q, jnp.zeros_like(q))
            own = dot_t(q_head, k)
            far = dot_t(q_head, k_halo)
            top = jnp.maximum(
                jnp.max(own, -1, keepdims=True), jnp.max(far, -1, keepdims=True)
            )
            own = jnp.exp2(own - top).astype(jnp.bfloat16)
            far = jnp.exp2(far - top).astype(jnp.bfloat16)
            v_own = jnp.where(mine, v, jnp.ones_like(v))
            v_far = jnp.where(mine, v_halo, jnp.broadcast_to(one, v.shape))
            acc = dot(own, v_own) + dot(far, v_far)
            total = pltpu.roll(acc, cols // 2, 1)
            gathered = jnp.where(mine, acc / total, gathered)
        held_ref[part * block : (part + 1) * block] = gathered.astype(jnp.bfloat16)
    ranks = len(out_refs)
    quarter = tokens // ranks
    rank = lax.axis_index("tp")
    for distance, out_ref in enumerate(out_refs):
        first = pl.multiple_of(lax.rem(rank + distance, ranks) * quarter, quarter)
        out_ref[...] = held_ref[pl.ds(first, quarter), :]


def attend(q, k, v, k_halo, v_halo, ranks, bands):
    forwards, tokens, cols = q.shape
    spec = pl.BlockSpec((1, tokens, cols), lambda i: (i, 0, 0))
    quarter = tokens // ranks
    return pl.pallas_call(
        functools.partial(attend_kernel, bands=bands),
        out_shape=[jax.ShapeDtypeStruct((forwards * quarter, cols), jnp.bfloat16)] * ranks,
        grid=(forwards,),
        in_specs=[spec] * 5,
        out_specs=[pl.BlockSpec((quarter, cols), lambda i: (i, 0))] * ranks,
        scratch_shapes=[pltpu.VMEM((tokens, cols), jnp.bfloat16)],
        compiler_params=pltpu.CompilerParams(vmem_limit_bytes=14 * MIB),
        name="attend",
    )(q, k, v, k_halo, v_halo)


def cells_row(x):
    cols, rows = x.shape
    cells = cols * rows
    spread = (iota((rows, cells), 1) % rows == iota((rows, cells), 0)).astype(jnp.float32)
    wide = dot(x.astype(jnp.float32).astype(jnp.bfloat16), spread.astype(jnp.bfloat16))
    mine = iota((cols, cells), 1) // rows == iota((cols, cells), 0)
    return jnp.sum(jnp.where(mine, wide, 0.0), 0, keepdims=True)


def ask_kernel(band_ref, tok_ref, ask_ref):
    bands = ask_ref.shape[0]
    named = cells_row(band_ref[...])
    token = cells_row(tok_ref[...])
    cells = named.shape[1]
    match = (named.astype(jnp.int32) == iota((bands, cells), 0)).astype(jnp.float32)
    before = (iota((cells, cells), 0) < iota((cells, cells), 1)).astype(jnp.float32)
    slot = dot(match.astype(jnp.bfloat16), before.astype(jnp.bfloat16))
    lanes = iota((bands, cells), 1)
    asked = jnp.zeros((bands, cells), jnp.float32)
    for s in range(4):
        hit = jnp.where(slot == s, match, 0.0)
        token_s = jnp.sum(hit * (token + 1.0), -1, keepdims=True) - 1.0
        asked = jnp.where(lanes == s, token_s, asked)
    ask_ref[...] = asked[:, :4].astype(jnp.int32)


def ask(band, tok, bands):
    return pl.pallas_call(
        ask_kernel,
        out_shape=jax.ShapeDtypeStruct((bands, 4), jnp.int32),
        in_specs=[ON_CHIP] * 2,
        out_specs=ON_CHIP,
        compiler_params=pltpu.CompilerParams(vmem_limit_bytes=4 * MIB),
        name="ask",
    )(band, tok)


def fetch_kernel(conv_hbm_ref, outer_ref, sems):
    copies = [
        pltpu.make_async_copy(
            conv_hbm_ref.at[pl.ds(6 * i, 3)], outer_ref.at[pl.ds(3 * i, 3)], sems.at[i]
        )
        for i in range(2)
    ]
    for copy in copies:
        copy.start()
    for copy in copies:
        copy.wait()


def fetch_outer(conv_w):
    return pl.pallas_call(
        fetch_kernel,
        out_shape=jax.ShapeDtypeStruct((6, *conv_w.shape[1:]), conv_w.dtype),
        in_specs=[pl.BlockSpec(memory_space=pltpu.HBM)],
        out_specs=ON_CHIP,
        scratch_shapes=[pltpu.SemaphoreType.DMA((2,))],
        compiler_params=pltpu.CompilerParams(vmem_limit_bytes=2 * MIB),
        name="fetch",
    )(conv_w)


def pick_rows(asked, rows, cells):
    bands = asked.shape[0]
    spread = (iota((rows, bands), 0) // 16 == iota((rows, bands), 1)).astype(jnp.float32)
    per_row = dot(spread.astype(jnp.bfloat16), asked.astype(jnp.float32).astype(jnp.bfloat16))
    r = iota((rows, 1), 0)
    mine = iota((rows, 4), 1) == (r // 4) % 4
    token_r = jnp.sum(jnp.where(mine, per_row, 0.0), -1, keepdims=True).astype(jnp.int32)
    target = jnp.where(token_r >= 0, (r % 4) * cells + token_r, -1)
    return (iota((rows, 4 * cells), 1) == target).astype(jnp.float32).astype(jnp.bfloat16)


def combine_kernel(code_ref, att0_ref, att1_ref, att2_ref, att3_ref, w0_ref, w1_ref, w3_ref, top_ref, low_ref, x_ref, w_bound_ref, asked_ref, out_ref, send_ref):
    cols = att0_ref.shape[1]
    features = x_ref.shape[1]
    quarter = out_ref.shape[1]
    rank = lax.axis_index("tp")
    x = x_ref[pl.ds(pl.multiple_of(rank * quarter, quarter), quarter), :].astype(jnp.float32)
    code = jnp.full((1, 1), code_ref[0], jnp.int32)
    p = wiggle(code, rank * quarter, quarter, features)
    pick = pick_rows(asked_ref[...], send_ref.shape[0] * 16, quarter)
    total = dot(att0_ref[...], w0_ref[...]) + dot(att1_ref[...], w1_ref[...])
    total = total + dot(att3_ref[...], w3_ref[...])
    total = total + dot(att2_ref[:, : cols // 2], top_ref[...])
    total = total + dot(att2_ref[:, cols // 2 :], low_ref[...])
    made = []
    for s, sign in enumerate(SIGNS):
        part = x if sign == 0.0 else (x + p if sign > 0 else x - p)
        part = (part + total[s * quarter : (s + 1) * quarter]).astype(jnp.bfloat16)
        out_ref[s] = part
        made.append(part)
    forced = dot(jnp.concatenate(made, 0), w_bound_ref[...]).astype(jnp.bfloat16)
    rows = [forced[s * quarter : (s + 1) * quarter] for s in range(3)]
    parts = forced.shape[1] // 128
    table = jnp.concatenate(
        [
            jnp.concatenate([f[:, c * 128 : (c + 1) * 128] for f in rows], 1)
            for c in range(parts)
        ],
        0,
    )
    picked = dot(pick, table).astype(jnp.bfloat16)
    send_ref[...] = picked.reshape(send_ref.shape)


def combine(code, att, w_outs, x, w_bound, asked):
    shapes = [(3, att[0].shape[0] // 3, x.shape[1]), (asked.shape[0], 16, 384)]
    operands = [*att, *w_outs, x, w_bound, asked]
    whole = lambda: (0, 0, 0)
    return pl.pallas_call(
        combine_kernel,
        out_shape=[jax.ShapeDtypeStruct(s, jnp.bfloat16) for s in shapes],
        in_specs=[SCALARS] + [ON_CHIP] * len(operands),
        out_specs=[pl.BlockSpec(s, whole) for s in shapes],
        compiler_params=pltpu.CompilerParams(vmem_limit_bytes=16 * MIB),
        name="combine",
    )(code, *operands)


def inputs_kernel(arrived_ref, band_ref, reg_ref, out_ref, first_ref, last_ref):
    cols, rows, channels = reg_ref.shape
    cells = cols * rows
    slots = arrived_ref.shape[0] * arrived_ref.shape[1]
    table = arrived_ref[...].reshape(slots, 384)
    band_row = cells_row(band_ref[...])
    r, c = iota((cells, cells), 0), iota((cells, cells), 1)
    band_col = jnp.sum(jnp.where(r == c, band_row, 0.0), -1, keepdims=True)
    earlier = (band_col == band_row) & (c < r)
    slot = jnp.sum(jnp.where(earlier, 1.0, 0.0), -1, keepdims=True)
    target = (band_col * 16.0 + slot * 4.0).astype(jnp.int32)
    lane = iota((cells, slots), 1) - target
    for part in range(channels // 128):
        take = jnp.where(lane == part, 1.0, 0.0).astype(jnp.bfloat16)
        taken = dot(take, table)
        lanes = slice(part * 128, (part + 1) * 128)
        reg = reg_ref[:, :, lanes].astype(jnp.float32)
        for s in range(3):
            forced = taken[:, s * 128 : (s + 1) * 128]
            made = (reg + forced.reshape(cols, rows, 128)).astype(jnp.bfloat16)
            out_ref[:, s * rows : (s + 1) * rows, lanes] = made
            first_ref[s * rows : (s + 1) * rows, lanes] = made[0]
            last_ref[s * rows : (s + 1) * rows, lanes] = made[cols - 1]


def make_inputs(arrived, band, reg):
    cols, rows, channels = reg.shape
    shapes = [(cols, 3 * rows, channels), (3 * rows, channels), (3 * rows, channels)]
    return pl.pallas_call(
        inputs_kernel,
        out_shape=[jax.ShapeDtypeStruct(s, jnp.bfloat16) for s in shapes],
        in_specs=[ON_CHIP] * 3,
        out_specs=[ON_CHIP] * 3,
        compiler_params=pltpu.CompilerParams(vmem_limit_bytes=6 * MIB),
        name="inputs",
    )(arrived, band, reg)


def row_shifts(x, rows):
    wide = x.astype(jnp.float32)
    total = x.shape[0]
    row = iota((total, 1), 0) % rows
    low = jnp.where(row > 0, pltpu.roll(wide, 1, 0), 0.0).astype(jnp.bfloat16)
    high = jnp.where(row < rows - 1, pltpu.roll(wide, total - 1, 0), 0.0).astype(jnp.bfloat16)
    return low, x, high


def inner_kernel(x_ref, outer_ref, conv_hbm_ref, sum_ref, held_ref, sem):
    copy = pltpu.make_async_copy(conv_hbm_ref.at[pl.ds(3, 3)], held_ref, sem)
    copy.start()
    cols, slab, channels = x_ref.shape
    cells = cols * slab
    shifts = row_shifts(x_ref[...].reshape(cells, channels), slab // 3)
    before = after = None
    for b, x in enumerate(shifts):
        one = dot(x[: cells - slab], outer_ref[b])
        two = dot(x[slab:], outer_ref[3 + b])
        before = one if before is None else before + one
        after = two if after is None else after + two
    copy.wait()
    middle = None
    for b, x in enumerate(shifts):
        one = dot(x, held_ref[b])
        middle = one if middle is None else middle + one
    sum_ref[:slab] = middle[:slab] + after[:slab]
    sum_ref[slab : cells - slab] = middle[slab : cells - slab] + before[: cells - 2 * slab] + after[slab:]
    sum_ref[cells - slab :] = middle[cells - slab :] + before[cells - 2 * slab :]


def convolve_inner(x, outer, conv_w):
    cols, slab, channels = x.shape
    return pl.pallas_call(
        inner_kernel,
        out_shape=jax.ShapeDtypeStruct((cols * slab, channels), jnp.float32),
        in_specs=[ON_CHIP] * 2 + [pl.BlockSpec(memory_space=pltpu.HBM)],
        out_specs=ON_CHIP,
        scratch_shapes=[
            pltpu.VMEM((3, channels, channels), jnp.bfloat16),
            pltpu.SemaphoreType.DMA(()),
        ],
        compiler_params=pltpu.CompilerParams(vmem_limit_bytes=16 * MIB),
        name="convolve_inner",
    )(x, outer, conv_w)


def finish_kernel(x_ref, before_ref, after_ref, outer_ref, sum_ref, out_ref):
    cols, slab, channels = x_ref.shape
    rows = slab // 3
    sides = []
    for side, ref in enumerate((before_ref, after_ref)):
        total = None
        for b, x in enumerate(row_shifts(ref[...], rows)):
            one = dot(x, outer_ref[3 * side + b])
            total = one if total is None else total + one
        sides.append(total)
    for col in range(cols):
        conv = sum_ref[col * slab : (col + 1) * slab]
        if col == 0:
            conv = conv + sides[0]
        if col == cols - 1:
            conv = conv + sides[1]
        result = x_ref[col].astype(jnp.float32) + conv / (1.0 + jnp.exp(-conv))
        result = result.astype(jnp.bfloat16)
        for s in range(3):
            out_ref[s, col] = result[s * rows : (s + 1) * rows]


def convolve_finish(x, before, after, outer, total):
    cols, slab, channels = x.shape
    shape = (3, cols, slab // 3, channels)
    return pl.pallas_call(
        finish_kernel,
        out_shape=jax.ShapeDtypeStruct(shape, jnp.bfloat16),
        in_specs=[ON_CHIP] * 5,
        out_specs=pl.BlockSpec(shape, lambda: (0, 0, 0, 0)),
        compiler_params=pltpu.CompilerParams(vmem_limit_bytes=8 * MIB),
        name="convolve_finish",
    )(x, before, after, outer, total)


def neighbours(last, first, axis):
    count = lax.axis_size(axis)
    up = [(i, i + 1) for i in range(count - 1)]
    down = [(j, i) for i, j in up]
    return lax.ppermute(last, axis, up), lax.ppermute(first, axis, down)


def per_device(
    global_state,
    band_codes,
    norm_gain,
    w_query,
    w_key,
    w_value,
    w_out,
    reg_state,
    src_band,
    src_tok,
    w_bound,
    conv_w,
):
    ranks = lax.axis_size("tp")
    bands = lax.axis_size(BANDS)
    tokens, features = global_state.shape
    half = tokens // 2
    gain = norm_gain
    cell_band = src_band.reshape(src_tok.shape)

    up = [(i, (i + 1) % ranks) for i in range(ranks)]
    down = [(j, i) for i, j in up]
    last, first, *weights = make_edges(
        band_codes, in_hbm(global_state), [in_hbm(w) for w in (w_query, w_key, w_value)]
    )
    before, after = neighbours(last, first, BANDS)
    q, k, v = project(band_codes, [in_hbm(global_state)], gain, weights, False)
    q, w_out = lax.optimization_barrier((q, w_out))
    w1, w3 = lax.ppermute(w_out, "tp", up), lax.ppermute(w_out, "tp", down)
    asked = ask(cell_band, src_tok, bands)
    q, before, after = lax.optimization_barrier((q, before, after))
    k_halo, v_halo = project(band_codes, [before, after], gain, weights[1:], True)
    k_halo, w1, w3 = lax.optimization_barrier((k_halo, w1, w3))
    middle = w_out.shape[0] // 2
    top, low = lax.ppermute(w1[:middle], "tp", up), lax.ppermute(w3[middle:], "tp", down)
    attended = attend(q, k, v, k_halo, v_halo, ranks, bands)
    attended, asked, top, low = lax.optimization_barrier((attended, asked, top, low))
    attended = [attended[0]] + [
        lax.ppermute(attended[d], "tp", [(i, (i + d) % ranks) for i in range(ranks)])
        for d in range(1, ranks)
    ]
    asked = lax.all_to_all(asked[:, None, :], BANDS, 0, 0, tiled=True)[:, 0, :]
    global_out, send = combine(
        band_codes, attended, [w_out, w1, w3, top, low], global_state, w_bound, asked
    )
    conv_w, send = lax.optimization_barrier((conv_w, send))
    conv_w = in_hbm(conv_w)
    outer = fetch_outer(conv_w)
    arrived = lax.all_to_all(send, BANDS, 0, 0, tiled=True)
    outer, arrived = lax.optimization_barrier((outer, arrived))
    inputs, first, last = make_inputs(arrived, cell_band, reg_state)
    before, after = neighbours(last, first, CELLS)
    total = convolve_inner(inputs, outer, conv_w)
    return global_out, convolve_finish(inputs, before, after, outer, total)


def solution(mesh):
    placed = (
        P(("sec", "tile"), None),
        P(("sec", "tile")),
        P(),
        P(None, "tp"),
        P(None, "tp"),
        P(None, "tp"),
        P("tp", None),
        P(("sec", "tile", "tp"), None, None),
        P(("sec", "tile", "tp"), None, None),
        P(("sec", "tile", "tp"), None),
        P(),
        P(),
    )
    return jax.shard_map(
        per_device,
        mesh=mesh,
        in_specs=placed,
        out_specs=(
            P(None, ("sec", "tile", "tp"), None),
            P(None, ("sec", "tile", "tp"), None, None),
        ),
        check_vma=False,
    )
```

```python
import functools

import jax
import jax.numpy as jnp
from jax import lax
from jax.experimental import pallas as pl
from jax.experimental.pallas import tpu as pltpu
from jax.sharding import PartitionSpec as P

HD = 64
SIGNS = (0.0, 1.0, -1.0)
BANDS = ("sec", "tile")
CELLS = ("sec", "tile", "tp")
LOG2E = 1.4426950408889634
MIB = 1024 * 1024
ON_CHIP = pl.BlockSpec(memory_space=pltpu.VMEM)
SCALARS = pl.BlockSpec(memory_space=pltpu.SMEM)

mix_band = 73856093
mix_token = 19349663
mix_feature = 83492791
mix_again = 668265261


def iota(shape, dim):
    return lax.broadcasted_iota(jnp.int32, shape, dim)


def in_hbm(x):
    return pltpu.with_memory_space_constraint(x, pltpu.HBM)


def dot(a, b):
    return jnp.dot(a, b, preferred_element_type=jnp.float32)


def dot_t(a, b):
    return lax.dot_general(a, b, (((1,), (1,)), ((), ())), preferred_element_type=jnp.float32)


def wiggle(code, first_token, rows, features):
    by_row = code * mix_band + (first_token + iota((rows, 1), 0)) * mix_token
    mixed = by_row + iota((1, features), 1) * mix_feature
    mixed = lax.bitwise_xor(mixed, lax.shift_right_arithmetic(mixed, jnp.full_like(mixed, 15)))
    mixed = mixed * mix_again
    mixed = lax.bitwise_xor(mixed, lax.shift_right_arithmetic(mixed, jnp.full_like(mixed, 13)))
    level = lax.bitwise_and(mixed, 1023).astype(jnp.float32)
    return (level - 511.5) * (0.5 / 295.6)


def edges_kernel(code_ref, x_ref, *refs):
    *refs, sems = refs
    count = (len(refs) - 2) // 2
    weights, (last_ref, first_ref, *held) = refs[:count], refs[count:]
    half = x_ref.shape[0] // 2
    pairs = [
        (x_ref.at[pl.ds(half, half)], last_ref.at[pl.ds(0, half)]),
        (x_ref.at[pl.ds(0, half)], first_ref.at[pl.ds(0, half)]),
        *zip(weights, held),
    ]
    copies = [pltpu.make_async_copy(a, b, sems.at[i]) for i, (a, b) in enumerate(pairs)]
    for copy in copies:
        copy.start()
    code = jnp.full((16, x_ref.shape[1]), code_ref[0], jnp.int32)
    lane = iota(code.shape, 1)
    shift = jnp.where(lane == 0, 16, jnp.where(lane == 1, 8, 0))
    digit = lax.bitwise_and(lax.shift_right_arithmetic(code, shift), 255)
    digit = digit.astype(jnp.float32).astype(jnp.bfloat16)
    last_ref[half:] = digit
    first_ref[half:] = digit
    for copy in copies:
        copy.wait()


def make_edges(code, x, weights):
    tokens, features = x.shape
    shapes = [(tokens // 2 + 16, features)] * 2 + [w.shape for w in weights]
    return pl.pallas_call(
        edges_kernel,
        out_shape=[jax.ShapeDtypeStruct(s, jnp.bfloat16) for s in shapes],
        in_specs=[SCALARS] + [pl.BlockSpec(memory_space=pltpu.HBM)] * (1 + len(weights)),
        out_specs=[ON_CHIP] * len(shapes),
        scratch_shapes=[pltpu.SemaphoreType.DMA((2 + len(weights),))],
        compiler_params=pltpu.CompilerParams(vmem_limit_bytes=2 * MIB),
        name="edges",
    )(code, x, *weights)


def project_kernel(code_ref, *refs, halo):
    step = pl.program_id(0)
    both_ref, inv_ref = refs[-2:]
    if halo:
        before_ref, after_ref, gain_ref, *refs = refs[:-2]
        rows = before_ref.shape[0] - 16
        first = (1 - step) * rows
        digits = jnp.where(
            step == 0, before_ref[rows : rows + 16, 0:128], after_ref[rows : rows + 16, 0:128]
        ).astype(jnp.float32)[0:1]
        lane = iota((1, 128), 1)
        place = jnp.where(lane == 0, 65536.0, jnp.where(lane == 1, 256.0, 1.0))
        code = jnp.sum(jnp.where(lane < 3, digits * place, 0.0), -1, keepdims=True)
        code = code.astype(jnp.int32)
    else:
        x_ref, gain_ref, *refs = refs[:-2]
        rows = x_ref.shape[0]
        first = step * rows
        code = jnp.full((1, 1), code_ref[0], jnp.int32)
    weights, outs = refs[: len(refs) // 2], refs[len(refs) // 2 :]
    features = both_ref.shape[1]
    gain = gain_ref[...].astype(jnp.float32).reshape(1, features)
    chunk, block = 16, 128
    for at in range(0, rows, block):
        for r in range(at, at + block, chunk):
            if halo:
                x = jnp.where(step == 0, before_ref[r : r + chunk], after_ref[r : r + chunk])
            else:
                x = x_ref[r : r + chunk]
            x = x.astype(jnp.float32)
            p = wiggle(code, first + r, chunk, features)
            place = 2 * at + (r - at)
            both_ref[place : place + chunk] = (x * gain).astype(jnp.bfloat16)
            both_ref[place + block : place + block + chunk] = (p * gain).astype(jnp.bfloat16)
            for s, sign in enumerate(SIGNS):
                state = x if sign == 0.0 else (x + p if sign > 0 else x - p)
                mean = jnp.sum(state * state, -1, keepdims=True) * (1.0 / features)
                inv_ref[s, r : r + chunk] = lax.rsqrt(mean + 1e-06)
        here = slice(at, at + block)
        for index, (w_ref, out_ref) in enumerate(zip(weights, outs)):
            scale = HD**-0.5 * LOG2E if (index == 0 and not halo) else 1.0
            made = dot(both_ref[2 * at : 2 * at + 2 * block], w_ref[...])
            base, diff = made[:block], made[block:]
            for s, sign in enumerate(SIGNS):
                full = base if sign == 0.0 else (base + diff if sign > 0 else base - diff)
                out_ref[s, here] = (full * (inv_ref[s, here] * scale)).astype(jnp.bfloat16)


def project(code, arrays, gain, weights, halo):
    features = gain.shape[0]
    cols = weights[0].shape[1]
    if halo:
        tokens = 2 * (arrays[0].shape[0] - 16)
        specs = [ON_CHIP for a in arrays]
    else:
        tokens = arrays[0].shape[0]
        specs = [pl.BlockSpec((tokens // 2, features), lambda i: (i, 0))]
    rows = tokens // 2
    return pl.pallas_call(
        functools.partial(project_kernel, halo=halo),
        out_shape=[jax.ShapeDtypeStruct((3, tokens, cols), jnp.bfloat16) for _ in weights],
        grid=(2,),
        in_specs=[SCALARS]
        + specs
        + [pl.BlockSpec(gain.shape, lambda i: (0,))]
        + [ON_CHIP for w in weights],
        out_specs=[pl.BlockSpec((3, rows, cols), lambda i: (0, i, 0)) for _ in weights],
        scratch_shapes=[
            pltpu.VMEM((2 * rows, features), jnp.bfloat16),
            pltpu.VMEM((3, rows, 1), jnp.float32),
        ],
        compiler_params=pltpu.CompilerParams(vmem_limit_bytes=12 * MIB),
        name="project_halo" if halo else "project_own",
    )(code, *arrays, gain, *weights)


def attend_kernel(q_ref, k_ref, v_ref, k_halo_ref, v_halo_ref, *refs, bands):
    *out_refs, held_ref = refs
    tokens, cols = q_ref.shape[1:]
    half = tokens // 2
    band = lax.axis_index(BANDS)
    left = band > 0
    right = band < bands - 1
    head_of = iota((1, cols), 1) // HD
    k = k_ref[0]
    v = v_ref[0]
    row = iota((tokens, 1), 0)
    there = jnp.where(row < half, left.astype(jnp.int32), right.astype(jnp.int32)) > 0
    k_halo = jnp.where(there, k_halo_ref[0], k)
    v_halo = v_halo_ref[0]
    one = there.astype(jnp.bfloat16)
    v_halo = v_halo * one
    block = half
    for part in range(tokens // block):
        q = q_ref[0, part * block : (part + 1) * block, :]
        gathered = jnp.zeros((block, cols), jnp.float32)
        for head in range(cols // HD):
            mine = head_of == head
            q_head = jnp.where(mine, q, jnp.zeros_like(q))
            own = dot_t(q_head, k)
            far = dot_t(q_head, k_halo)
            top = jnp.maximum(
                jnp.max(own, -1, keepdims=True), jnp.max(far, -1, keepdims=True)
            )
            own = jnp.exp2(own - top).astype(jnp.bfloat16)
            far = jnp.exp2(far - top).astype(jnp.bfloat16)
            v_own = jnp.where(mine, v, jnp.ones_like(v))
            v_far = jnp.where(mine, v_halo, jnp.broadcast_to(one, v.shape))
            acc = dot(own, v_own) + dot(far, v_far)
            total = pltpu.roll(acc, cols // 2, 1)
            gathered = jnp.where(mine, acc / total, gathered)
        held_ref[part * block : (part + 1) * block] = gathered.astype(jnp.bfloat16)
    ranks = len(out_refs)
    quarter = tokens // ranks
    rank = lax.axis_index("tp")
    for distance, out_ref in enumerate(out_refs):
        first = pl.multiple_of(lax.rem(rank + distance, ranks) * quarter, quarter)
        out_ref[...] = held_ref[pl.ds(first, quarter), :]


def attend(q, k, v, k_halo, v_halo, ranks, bands):
    forwards, tokens, cols = q.shape
    spec = pl.BlockSpec((1, tokens, cols), lambda i: (i, 0, 0))
    quarter = tokens // ranks
    return pl.pallas_call(
        functools.partial(attend_kernel, bands=bands),
        out_shape=[jax.ShapeDtypeStruct((forwards * quarter, cols), jnp.bfloat16)] * ranks,
        grid=(forwards,),
        in_specs=[spec] * 5,
        out_specs=[pl.BlockSpec((quarter, cols), lambda i: (i, 0))] * ranks,
        scratch_shapes=[pltpu.VMEM((tokens, cols), jnp.bfloat16)],
        compiler_params=pltpu.CompilerParams(vmem_limit_bytes=14 * MIB),
        name="attend",
    )(q, k, v, k_halo, v_halo)


def cells_row(x):
    cols, rows = x.shape
    cells = cols * rows
    spread = (iota((rows, cells), 1) % rows == iota((rows, cells), 0)).astype(jnp.float32)
    wide = dot(x.astype(jnp.float32).astype(jnp.bfloat16), spread.astype(jnp.bfloat16))
    mine = iota((cols, cells), 1) // rows == iota((cols, cells), 0)
    return jnp.sum(jnp.where(mine, wide, 0.0), 0, keepdims=True)


def ask_kernel(band_ref, tok_ref, ask_ref):
    bands = ask_ref.shape[0]
    named = cells_row(band_ref[...])
    token = cells_row(tok_ref[...])
    cells = named.shape[1]
    match = (named.astype(jnp.int32) == iota((bands, cells), 0)).astype(jnp.float32)
    before = (iota((cells, cells), 0) < iota((cells, cells), 1)).astype(jnp.float32)
    slot = dot(match.astype(jnp.bfloat16), before.astype(jnp.bfloat16))
    lanes = iota((bands, cells), 1)
    asked = jnp.zeros((bands, cells), jnp.float32)
    for s in range(4):
        hit = jnp.where(slot == s, match, 0.0)
        token_s = jnp.sum(hit * (token + 1.0), -1, keepdims=True) - 1.0
        asked = jnp.where(lanes == s, token_s, asked)
    ask_ref[...] = asked[:, :4].astype(jnp.int32)


def ask(band, tok, bands):
    return pl.pallas_call(
        ask_kernel,
        out_shape=jax.ShapeDtypeStruct((bands, 4), jnp.int32),
        in_specs=[ON_CHIP] * 2,
        out_specs=ON_CHIP,
        compiler_params=pltpu.CompilerParams(vmem_limit_bytes=4 * MIB),
        name="ask",
    )(band, tok)


def fetch_kernel(conv_hbm_ref, outer_ref, sems):
    copies = [
        pltpu.make_async_copy(
            conv_hbm_ref.at[pl.ds(6 * i, 3)], outer_ref.at[pl.ds(3 * i, 3)], sems.at[i]
        )
        for i in range(2)
    ]
    for copy in copies:
        copy.start()
    for copy in copies:
        copy.wait()


def fetch_outer(conv_w):
    return pl.pallas_call(
        fetch_kernel,
        out_shape=jax.ShapeDtypeStruct((6, *conv_w.shape[1:]), conv_w.dtype),
        in_specs=[pl.BlockSpec(memory_space=pltpu.HBM)],
        out_specs=ON_CHIP,
        scratch_shapes=[pltpu.SemaphoreType.DMA((2,))],
        compiler_params=pltpu.CompilerParams(vmem_limit_bytes=2 * MIB),
        name="fetch",
    )(conv_w)


def pick_rows(asked, rows, cells):
    bands = asked.shape[0]
    spread = (iota((rows, bands), 0) // 16 == iota((rows, bands), 1)).astype(jnp.float32)
    per_row = dot(spread.astype(jnp.bfloat16), asked.astype(jnp.float32).astype(jnp.bfloat16))
    r = iota((rows, 1), 0)
    mine = iota((rows, 4), 1) == (r // 4) % 4
    token_r = jnp.sum(jnp.where(mine, per_row, 0.0), -1, keepdims=True).astype(jnp.int32)
    target = jnp.where(token_r >= 0, (r % 4) * cells + token_r, -1)
    return (iota((rows, 4 * cells), 1) == target).astype(jnp.float32).astype(jnp.bfloat16)


def combine_kernel(code_ref, att0_ref, att1_ref, att2_ref, att3_ref, w0_ref, w1_ref, w3_ref, top_ref, low_ref, x_ref, w_bound_ref, out_ref, table_ref, own_ref, sem):
    cols = att0_ref.shape[1]
    features = x_ref.shape[1]
    quarter = out_ref.shape[1]
    rank = lax.axis_index("tp")
    rows = pl.ds(pl.multiple_of(rank * quarter, quarter), quarter)
    copy = pltpu.make_async_copy(x_ref.at[rows], own_ref, sem)
    copy.start()
    code = jnp.full((1, 1), code_ref[0], jnp.int32)
    p = wiggle(code, rank * quarter, quarter, features)
    total = dot(att0_ref[...], w0_ref[...]) + dot(att1_ref[...], w1_ref[...])
    total = total + dot(att3_ref[...], w3_ref[...])
    total = total + dot(att2_ref[:, : cols // 2], top_ref[...])
    total = total + dot(att2_ref[:, cols // 2 :], low_ref[...])
    copy.wait()
    x = own_ref[...].astype(jnp.float32)
    made = []
    for s, sign in enumerate(SIGNS):
        part = x if sign == 0.0 else (x + p if sign > 0 else x - p)
        part = (part + total[s * quarter : (s + 1) * quarter]).astype(jnp.bfloat16)
        out_ref[s] = part
        made.append(part)
    forced = dot(jnp.concatenate(made, 0), w_bound_ref[...]).astype(jnp.bfloat16)
    for part in range(forced.shape[1] // 128):
        for s in range(3):
            table_ref[part * quarter : (part + 1) * quarter, s * 128 : (s + 1) * 128] = forced[
                s * quarter : (s + 1) * quarter, part * 128 : (part + 1) * 128
            ]


def combine(code, att, w_outs, x, w_bound):
    quarter = att[0].shape[0] // 3
    shape = (3, quarter, x.shape[1])
    table = (quarter * w_bound.shape[1] // 128, 384)
    operands = [*att, *(in_hbm(a) for a in (*w_outs, x, w_bound))]
    specs = [pl.BlockSpec(a.shape, lambda: (0, 0)) for a in operands]
    specs[-2] = pl.BlockSpec(memory_space=pltpu.HBM)
    return pl.pallas_call(
        combine_kernel,
        out_shape=[jax.ShapeDtypeStruct(s, jnp.bfloat16) for s in (shape, table)],
        in_specs=[SCALARS] + specs,
        out_specs=[pl.BlockSpec(shape, lambda: (0, 0, 0)), ON_CHIP],
        scratch_shapes=[
            pltpu.VMEM((quarter, x.shape[1]), jnp.bfloat16),
            pltpu.SemaphoreType.DMA(()),
        ],
        compiler_params=pltpu.CompilerParams(vmem_limit_bytes=16 * MIB),
        name="combine",
    )(code, *operands)


def serve_kernel(asked_ref, table_ref, send_ref):
    pick = pick_rows(asked_ref[...], send_ref.shape[0] * 16, table_ref.shape[0] // 4)
    send_ref[...] = dot(pick, table_ref[...]).astype(jnp.bfloat16).reshape(send_ref.shape)


def serve(asked, table):
    shape = (asked.shape[0], 16, table.shape[1])
    return pl.pallas_call(
        serve_kernel,
        out_shape=jax.ShapeDtypeStruct(shape, jnp.bfloat16),
        in_specs=[ON_CHIP] * 2,
        out_specs=pl.BlockSpec(shape, lambda: (0, 0, 0)),
        compiler_params=pltpu.CompilerParams(vmem_limit_bytes=8 * MIB),
        name="serve",
    )(asked, table)


def inputs_kernel(arrived_ref, band_ref, reg_ref, out_ref, first_ref, last_ref):
    cols, rows, channels = reg_ref.shape
    cells = cols * rows
    slots = arrived_ref.shape[0] * arrived_ref.shape[1]
    table = arrived_ref[...].reshape(slots, 384)
    band_row = cells_row(band_ref[...])
    r, c = iota((cells, cells), 0), iota((cells, cells), 1)
    band_col = jnp.sum(jnp.where(r == c, band_row, 0.0), -1, keepdims=True)
    earlier = (band_col == band_row) & (c < r)
    slot = jnp.sum(jnp.where(earlier, 1.0, 0.0), -1, keepdims=True)
    target = (band_col * 16.0 + slot * 4.0).astype(jnp.int32)
    lane = iota((cells, slots), 1) - target
    for part in range(channels // 128):
        take = jnp.where(lane == part, 1.0, 0.0).astype(jnp.bfloat16)
        taken = dot(take, table)
        lanes = slice(part * 128, (part + 1) * 128)
        reg = reg_ref[:, :, lanes].astype(jnp.float32)
        for s in range(3):
            forced = taken[:, s * 128 : (s + 1) * 128]
            made = (reg + forced.reshape(cols, rows, 128)).astype(jnp.bfloat16)
            out_ref[:, s * rows : (s + 1) * rows, lanes] = made
            first_ref[s * rows : (s + 1) * rows, lanes] = made[0]
            last_ref[s * rows : (s + 1) * rows, lanes] = made[cols - 1]


def make_inputs(arrived, band, reg):
    cols, rows, channels = reg.shape
    shapes = [(cols, 3 * rows, channels), (3 * rows, channels), (3 * rows, channels)]
    return pl.pallas_call(
        inputs_kernel,
        out_shape=[jax.ShapeDtypeStruct(s, jnp.bfloat16) for s in shapes],
        in_specs=[ON_CHIP] * 3,
        out_specs=[ON_CHIP] * 3,
        compiler_params=pltpu.CompilerParams(vmem_limit_bytes=6 * MIB),
        name="inputs",
    )(arrived, band, reg)


def row_shifts(x, rows):
    wide = x.astype(jnp.float32)
    total = x.shape[0]
    row = iota((total, 1), 0) % rows
    low = jnp.where(row > 0, pltpu.roll(wide, 1, 0), 0.0).astype(jnp.bfloat16)
    high = jnp.where(row < rows - 1, pltpu.roll(wide, total - 1, 0), 0.0).astype(jnp.bfloat16)
    return low, x, high


def inner_kernel(x_ref, outer_ref, conv_hbm_ref, sum_ref, held_ref, sem):
    copy = pltpu.make_async_copy(conv_hbm_ref.at[pl.ds(3, 3)], held_ref, sem)
    copy.start()
    cols, slab, channels = x_ref.shape
    cells = cols * slab
    shifts = row_shifts(x_ref[...].reshape(cells, channels), slab // 3)
    before = after = None
    for b, x in enumerate(shifts):
        one = dot(x[: cells - slab], outer_ref[b])
        two = dot(x[slab:], outer_ref[3 + b])
        before = one if before is None else before + one
        after = two if after is None else after + two
    copy.wait()
    middle = None
    for b, x in enumerate(shifts):
        one = dot(x, held_ref[b])
        middle = one if middle is None else middle + one
    sum_ref[:slab] = middle[:slab] + after[:slab]
    sum_ref[slab : cells - slab] = middle[slab : cells - slab] + before[: cells - 2 * slab] + after[slab:]
    sum_ref[cells - slab :] = middle[cells - slab :] + before[cells - 2 * slab :]


def convolve_inner(x, outer, conv_w):
    cols, slab, channels = x.shape
    return pl.pallas_call(
        inner_kernel,
        out_shape=jax.ShapeDtypeStruct((cols * slab, channels), jnp.float32),
        in_specs=[ON_CHIP] * 2 + [pl.BlockSpec(memory_space=pltpu.HBM)],
        out_specs=ON_CHIP,
        scratch_shapes=[
            pltpu.VMEM((3, channels, channels), jnp.bfloat16),
            pltpu.SemaphoreType.DMA(()),
        ],
        compiler_params=pltpu.CompilerParams(vmem_limit_bytes=16 * MIB),
        name="convolve_inner",
    )(x, outer, conv_w)


def finish_kernel(x_ref, before_ref, after_ref, outer_ref, sum_ref, out_ref):
    cols, slab, channels = x_ref.shape
    rows = slab // 3
    sides = []
    for side, ref in enumerate((before_ref, after_ref)):
        total = None
        for b, x in enumerate(row_shifts(ref[...], rows)):
            one = dot(x, outer_ref[3 * side + b])
            total = one if total is None else total + one
        sides.append(total)
    for col in range(cols):
        conv = sum_ref[col * slab : (col + 1) * slab]
        if col == 0:
            conv = conv + sides[0]
        if col == cols - 1:
            conv = conv + sides[1]
        result = x_ref[col].astype(jnp.float32) + conv / (1.0 + jnp.exp(-conv))
        result = result.astype(jnp.bfloat16)
        for s in range(3):
            out_ref[s, col] = result[s * rows : (s + 1) * rows]


def convolve_finish(x, before, after, outer, total):
    cols, slab, channels = x.shape
    shape = (3, cols, slab // 3, channels)
    return pl.pallas_call(
        finish_kernel,
        out_shape=jax.ShapeDtypeStruct(shape, jnp.bfloat16),
        in_specs=[ON_CHIP] * 5,
        out_specs=pl.BlockSpec(shape, lambda: (0, 0, 0, 0)),
        compiler_params=pltpu.CompilerParams(vmem_limit_bytes=8 * MIB),
        name="convolve_finish",
    )(x, before, after, outer, total)


def neighbours(last, first, axis):
    count = lax.axis_size(axis)
    up = [(i, i + 1) for i in range(count - 1)]
    down = [(j, i) for i, j in up]
    return lax.ppermute(last, axis, up), lax.ppermute(first, axis, down)


def per_device(
    global_state,
    band_codes,
    norm_gain,
    w_query,
    w_key,
    w_value,
    w_out,
    reg_state,
    src_band,
    src_tok,
    w_bound,
    conv_w,
):
    ranks = lax.axis_size("tp")
    bands = lax.axis_size(BANDS)
    tokens, features = global_state.shape
    half = tokens // 2
    gain = in_hbm(norm_gain)
    cell_band = src_band.reshape(src_tok.shape)

    up = [(i, (i + 1) % ranks) for i in range(ranks)]
    down = [(j, i) for i, j in up]
    last, first, *weights = make_edges(
        band_codes, in_hbm(global_state), [in_hbm(w) for w in (w_query, w_key, w_value)]
    )
    before, after = neighbours(last, first, BANDS)
    w1, w3 = lax.ppermute(w_out, "tp", up), lax.ppermute(w_out, "tp", down)
    q, k, v = project(band_codes, [in_hbm(global_state)], gain, weights, False)
    asked = ask(cell_band, src_tok, bands)
    q, w1, w3 = lax.optimization_barrier((q, w1, w3))
    middle = w_out.shape[0] // 2
    top, low = lax.ppermute(w1[:middle], "tp", up), lax.ppermute(w3[middle:], "tp", down)
    q, before, after = lax.optimization_barrier((q, before, after))
    k_halo, v_halo = project(band_codes, [before, after], gain, weights[1:], True)
    attended = attend(q, k, v, k_halo, v_halo, ranks, bands)
    attended, asked, top, low = lax.optimization_barrier((attended, asked, top, low))
    attended = [attended[0]] + [
        lax.ppermute(attended[d], "tp", [(i, (i + d) % ranks) for i in range(ranks)])
        for d in range(1, ranks)
    ]
    asked = lax.all_to_all(asked[:, None, :], BANDS, 0, 0, tiled=True)[:, 0, :]
    global_out, table = combine(band_codes, attended, [w_out, w1, w3, top, low], global_state, w_bound)
    send = serve(asked, table)
    conv_w, send = lax.optimization_barrier((conv_w, send))
    conv_w = in_hbm(conv_w)
    outer = fetch_outer(conv_w)
    arrived = lax.all_to_all(send, BANDS, 0, 0, tiled=True)
    outer, arrived = lax.optimization_barrier((outer, arrived))
    inputs, first, last = make_inputs(arrived, cell_band, reg_state)
    before, after = neighbours(last, first, CELLS)
    total = convolve_inner(inputs, outer, conv_w)
    return global_out, convolve_finish(inputs, before, after, outer, total)


def solution(mesh):
    placed = (
        P(("sec", "tile"), None),
        P(("sec", "tile")),
        P(),
        P(None, "tp"),
        P(None, "tp"),
        P(None, "tp"),
        P("tp", None),
        P(("sec", "tile", "tp"), None, None),
        P(("sec", "tile", "tp"), None, None),
        P(("sec", "tile", "tp"), None),
        P(),
        P(),
    )
    return jax.shard_map(
        per_device,
        mesh=mesh,
        in_specs=placed,
        out_specs=(
            P(None, ("sec", "tile", "tp"), None),
            P(None, ("sec", "tile", "tp"), None, None),
        ),
        check_vma=False,
    )
```

```python
import functools

import jax
import jax.numpy as jnp
from jax import lax
from jax.experimental import pallas as pl
from jax.experimental.pallas import tpu as pltpu
from jax.sharding import PartitionSpec as P

HD = 64
SIGNS = (0.0, 1.0, -1.0)
BANDS = ("sec", "tile")
CELLS = ("sec", "tile", "tp")
LOG2E = 1.4426950408889634
MIB = 1024 * 1024
ON_CHIP = pl.BlockSpec(memory_space=pltpu.VMEM)
SCALARS = pl.BlockSpec(memory_space=pltpu.SMEM)

mix_band = 73856093
mix_token = 19349663
mix_feature = 83492791
mix_again = 668265261


def iota(shape, dim):
    return lax.broadcasted_iota(jnp.int32, shape, dim)


def in_hbm(x):
    return pltpu.with_memory_space_constraint(x, pltpu.HBM)


def dot(a, b):
    return jnp.dot(a, b, preferred_element_type=jnp.float32)


def dot_t(a, b):
    return lax.dot_general(a, b, (((1,), (1,)), ((), ())), preferred_element_type=jnp.float32)


def wiggle(code, first_token, rows, features):
    by_row = code * mix_band + (first_token + iota((rows, 1), 0)) * mix_token
    mixed = by_row + iota((1, features), 1) * mix_feature
    mixed = lax.bitwise_xor(mixed, lax.shift_right_arithmetic(mixed, jnp.full_like(mixed, 15)))
    mixed = mixed * mix_again
    mixed = lax.bitwise_xor(mixed, lax.shift_right_arithmetic(mixed, jnp.full_like(mixed, 13)))
    level = lax.bitwise_and(mixed, 1023).astype(jnp.float32)
    return (level - 511.5) * (0.5 / 295.6)


def edges_kernel(code_ref, x_ref, *refs):
    *refs, sems = refs
    count = (len(refs) - 2) // 2
    weights, (last_ref, first_ref, *held) = refs[:count], refs[count:]
    half = x_ref.shape[0] // 2
    pairs = [
        (x_ref.at[pl.ds(half, half)], last_ref.at[pl.ds(0, half)]),
        (x_ref.at[pl.ds(0, half)], first_ref.at[pl.ds(0, half)]),
        *zip(weights, held),
    ]
    copies = [pltpu.make_async_copy(a, b, sems.at[i]) for i, (a, b) in enumerate(pairs)]
    for copy in copies:
        copy.start()
    code = jnp.full((16, x_ref.shape[1]), code_ref[0], jnp.int32)
    lane = iota(code.shape, 1)
    shift = jnp.where(lane == 0, 16, jnp.where(lane == 1, 8, 0))
    digit = lax.bitwise_and(lax.shift_right_arithmetic(code, shift), 255)
    digit = digit.astype(jnp.float32).astype(jnp.bfloat16)
    last_ref[half:] = digit
    first_ref[half:] = digit
    for copy in copies:
        copy.wait()


def make_edges(code, x, weights):
    tokens, features = x.shape
    shapes = [(tokens // 2 + 16, features)] * 2 + [w.shape for w in weights]
    return pl.pallas_call(
        edges_kernel,
        out_shape=[jax.ShapeDtypeStruct(s, jnp.bfloat16) for s in shapes],
        in_specs=[SCALARS] + [pl.BlockSpec(memory_space=pltpu.HBM)] * (1 + len(weights)),
        out_specs=[ON_CHIP] * len(shapes),
        scratch_shapes=[pltpu.SemaphoreType.DMA((2 + len(weights),))],
        compiler_params=pltpu.CompilerParams(vmem_limit_bytes=2 * MIB),
        name="edges",
    )(code, x, *weights)


def project_kernel(code_ref, early_ref, late_ref, gain_ref, *refs, halo):
    *refs, both_ref, inv_ref = refs
    step = pl.program_id(0)
    rows = early_ref.shape[0] - 16
    if halo:
        first = (1 - step) * rows
        digits = jnp.where(
            step == 0, early_ref[rows : rows + 16, 0:128], late_ref[rows : rows + 16, 0:128]
        ).astype(jnp.float32)[0:1]
        lane = iota((1, 128), 1)
        place = jnp.where(lane == 0, 65536.0, jnp.where(lane == 1, 256.0, 1.0))
        code = jnp.sum(jnp.where(lane < 3, digits * place, 0.0), -1, keepdims=True)
        code = code.astype(jnp.int32)
    else:
        first = step * rows
        code = jnp.full((1, 1), code_ref[0], jnp.int32)
    weights, outs = refs[: len(refs) // 2], refs[len(refs) // 2 :]
    features = both_ref.shape[1]
    gain = gain_ref[...].astype(jnp.float32).reshape(1, features)
    chunk, block = 16, 128
    for at in range(0, rows, block):
        for r in range(at, at + block, chunk):
            x = jnp.where(step == 0, early_ref[r : r + chunk], late_ref[r : r + chunk])
            x = x.astype(jnp.float32)
            p = wiggle(code, first + r, chunk, features)
            place = 2 * at + (r - at)
            both_ref[place : place + chunk] = (x * gain).astype(jnp.bfloat16)
            both_ref[place + block : place + block + chunk] = (p * gain).astype(jnp.bfloat16)
            for s, sign in enumerate(SIGNS):
                state = x if sign == 0.0 else (x + p if sign > 0 else x - p)
                mean = jnp.sum(state * state, -1, keepdims=True) * (1.0 / features)
                inv_ref[s, r : r + chunk] = lax.rsqrt(mean + 1e-06)
        here = slice(at, at + block)
        for index, (w_ref, out_ref) in enumerate(zip(weights, outs)):
            scale = HD**-0.5 * LOG2E if (index == 0 and not halo) else 1.0
            made = dot(both_ref[2 * at : 2 * at + 2 * block], w_ref[...])
            base, diff = made[:block], made[block:]
            for s, sign in enumerate(SIGNS):
                full = base if sign == 0.0 else (base + diff if sign > 0 else base - diff)
                out_ref[s, here] = (full * (inv_ref[s, here] * scale)).astype(jnp.bfloat16)


def project(code, arrays, gain, weights, halo):
    features = gain.shape[0]
    cols = weights[0].shape[1]
    tokens = 2 * (arrays[0].shape[0] - 16)
    specs = [ON_CHIP for a in arrays]
    rows = tokens // 2
    return pl.pallas_call(
        functools.partial(project_kernel, halo=halo),
        out_shape=[jax.ShapeDtypeStruct((3, tokens, cols), jnp.bfloat16) for _ in weights],
        grid=(2,),
        in_specs=[SCALARS]
        + specs
        + [pl.BlockSpec(gain.shape, lambda i: (0,))]
        + [ON_CHIP for w in weights],
        out_specs=[pl.BlockSpec((3, rows, cols), lambda i: (0, i, 0)) for _ in weights],
        scratch_shapes=[
            pltpu.VMEM((2 * rows, features), jnp.bfloat16),
            pltpu.VMEM((3, rows, 1), jnp.float32),
        ],
        compiler_params=pltpu.CompilerParams(vmem_limit_bytes=12 * MIB),
        name="project_halo" if halo else "project_own",
    )(code, *arrays, gain, *weights)


def attend_kernel(q_ref, k_ref, v_ref, k_halo_ref, v_halo_ref, *refs, bands):
    *out_refs, held_ref = refs
    tokens, cols = q_ref.shape[1:]
    half = tokens // 2
    band = lax.axis_index(BANDS)
    left = band > 0
    right = band < bands - 1
    head_of = iota((1, cols), 1) // HD
    k = k_ref[0]
    v = v_ref[0]
    row = iota((tokens, 1), 0)
    there = jnp.where(row < half, left.astype(jnp.int32), right.astype(jnp.int32)) > 0
    k_halo = jnp.where(there, k_halo_ref[0], k)
    v_halo = v_halo_ref[0]
    one = there.astype(jnp.bfloat16)
    v_halo = v_halo * one
    block = half
    for part in range(tokens // block):
        q = q_ref[0, part * block : (part + 1) * block, :]
        gathered = jnp.zeros((block, cols), jnp.float32)
        for head in range(cols // HD):
            mine = head_of == head
            q_head = jnp.where(mine, q, jnp.zeros_like(q))
            own = dot_t(q_head, k)
            far = dot_t(q_head, k_halo)
            top = jnp.maximum(
                jnp.max(own, -1, keepdims=True), jnp.max(far, -1, keepdims=True)
            )
            own = jnp.exp2(own - top).astype(jnp.bfloat16)
            far = jnp.exp2(far - top).astype(jnp.bfloat16)
            v_own = jnp.where(mine, v, jnp.ones_like(v))
            v_far = jnp.where(mine, v_halo, jnp.broadcast_to(one, v.shape))
            acc = dot(own, v_own) + dot(far, v_far)
            total = pltpu.roll(acc, cols // 2, 1)
            gathered = jnp.where(mine, acc / total, gathered)
        held_ref[part * block : (part + 1) * block] = gathered.astype(jnp.bfloat16)
    ranks = len(out_refs)
    quarter = tokens // ranks
    rank = lax.axis_index("tp")
    for distance, out_ref in enumerate(out_refs):
        first = pl.multiple_of(lax.rem(rank + distance, ranks) * quarter, quarter)
        out_ref[...] = held_ref[pl.ds(first, quarter), :]


def attend(q, k, v, k_halo, v_halo, ranks, bands):
    forwards, tokens, cols = q.shape
    spec = pl.BlockSpec((1, tokens, cols), lambda i: (i, 0, 0))
    quarter = tokens // ranks
    return pl.pallas_call(
        functools.partial(attend_kernel, bands=bands),
        out_shape=[jax.ShapeDtypeStruct((forwards * quarter, cols), jnp.bfloat16)] * ranks,
        grid=(forwards,),
        in_specs=[spec] * 5,
        out_specs=[pl.BlockSpec((quarter, cols), lambda i: (i, 0))] * ranks,
        scratch_shapes=[pltpu.VMEM((tokens, cols), jnp.bfloat16)],
        compiler_params=pltpu.CompilerParams(vmem_limit_bytes=14 * MIB),
        name="attend",
    )(q, k, v, k_halo, v_halo)


def cells_row(x):
    cols, rows = x.shape
    cells = cols * rows
    spread = (iota((rows, cells), 1) % rows == iota((rows, cells), 0)).astype(jnp.float32)
    wide = dot(x.astype(jnp.float32).astype(jnp.bfloat16), spread.astype(jnp.bfloat16))
    mine = iota((cols, cells), 1) // rows == iota((cols, cells), 0)
    return jnp.sum(jnp.where(mine, wide, 0.0), 0, keepdims=True)


def ask_kernel(band_ref, tok_ref, ask_ref):
    bands = ask_ref.shape[0]
    named = cells_row(band_ref[...])
    token = cells_row(tok_ref[...])
    cells = named.shape[1]
    match = (named.astype(jnp.int32) == iota((bands, cells), 0)).astype(jnp.float32)
    before = (iota((cells, cells), 0) < iota((cells, cells), 1)).astype(jnp.float32)
    slot = dot(match.astype(jnp.bfloat16), before.astype(jnp.bfloat16))
    lanes = iota((bands, cells), 1)
    asked = jnp.zeros((bands, cells), jnp.float32)
    for s in range(4):
        hit = jnp.where(slot == s, match, 0.0)
        token_s = jnp.sum(hit * (token + 1.0), -1, keepdims=True) - 1.0
        asked = jnp.where(lanes == s, token_s, asked)
    ask_ref[...] = asked[:, :4].astype(jnp.int32)


def ask(band, tok, bands):
    return pl.pallas_call(
        ask_kernel,
        out_shape=jax.ShapeDtypeStruct((bands, 4), jnp.int32),
        in_specs=[ON_CHIP] * 2,
        out_specs=ON_CHIP,
        compiler_params=pltpu.CompilerParams(vmem_limit_bytes=4 * MIB),
        name="ask",
    )(band, tok)


def fetch_kernel(conv_hbm_ref, taps_ref, sem):
    copy = pltpu.make_async_copy(conv_hbm_ref.at[pl.ds(0, 3)], taps_ref, sem)
    copy.start()
    copy.wait()


def fetch_taps(conv_w):
    return pl.pallas_call(
        fetch_kernel,
        out_shape=jax.ShapeDtypeStruct((3, *conv_w.shape[1:]), conv_w.dtype),
        in_specs=[pl.BlockSpec(memory_space=pltpu.HBM)],
        out_specs=ON_CHIP,
        scratch_shapes=[pltpu.SemaphoreType.DMA(())],
        compiler_params=pltpu.CompilerParams(vmem_limit_bytes=2 * MIB),
        name="fetch",
    )(conv_w)


def pick_rows(asked, rows, cells):
    bands = asked.shape[0]
    spread = (iota((rows, bands), 0) // 16 == iota((rows, bands), 1)).astype(jnp.float32)
    per_row = dot(spread.astype(jnp.bfloat16), asked.astype(jnp.float32).astype(jnp.bfloat16))
    r = iota((rows, 1), 0)
    mine = iota((rows, 4), 1) == (r // 4) % 4
    token_r = jnp.sum(jnp.where(mine, per_row, 0.0), -1, keepdims=True).astype(jnp.int32)
    target = jnp.where(token_r >= 0, (r % 4) * cells + token_r, -1)
    return (iota((rows, 4 * cells), 1) == target).astype(jnp.float32).astype(jnp.bfloat16)


def combine_kernel(code_ref, att0_ref, att1_ref, att2_ref, att3_ref, w0_ref, w1_ref, w3_ref, top_ref, low_ref, x_ref, w_bound_ref, out_ref, table_ref, own_ref, held_ref, bound_ref, sems):
    cols = att0_ref.shape[1]
    half = cols // 2
    features = x_ref.shape[1]
    quarter = out_ref.shape[1]
    rank = lax.axis_index("tp")
    rows = pl.ds(pl.multiple_of(rank * quarter, quarter), quarter)
    pairs = [
        (w0_ref, held_ref.at[pl.ds(0, cols)]),
        (w1_ref, held_ref.at[pl.ds(cols, cols)]),
        (w3_ref, held_ref.at[pl.ds(2 * cols, cols)]),
        (top_ref, held_ref.at[pl.ds(3 * cols, half)]),
        (low_ref, held_ref.at[pl.ds(3 * cols + half, half)]),
        (x_ref.at[rows], own_ref),
        (w_bound_ref, bound_ref),
    ]
    copies = [pltpu.make_async_copy(a, b, sems.at[i]) for i, (a, b) in enumerate(pairs)]
    for copy in copies:
        copy.start()
    code = jnp.full((1, 1), code_ref[0], jnp.int32)
    p = wiggle(code, rank * quarter, quarter, features)
    copies[0].wait()
    total = dot(att0_ref[...], held_ref[:cols])
    copies[1].wait()
    total = total + dot(att1_ref[...], held_ref[cols : 2 * cols])
    copies[2].wait()
    total = total + dot(att3_ref[...], held_ref[2 * cols : 3 * cols])
    copies[3].wait()
    copies[4].wait()
    total = total + dot(att2_ref[...], held_ref[3 * cols :])
    copies[5].wait()
    x = own_ref[...].astype(jnp.float32)
    made = []
    for s, sign in enumerate(SIGNS):
        part = x if sign == 0.0 else (x + p if sign > 0 else x - p)
        part = (part + total[s * quarter : (s + 1) * quarter]).astype(jnp.bfloat16)
        out_ref[s] = part
        made.append(part)
    copies[6].wait()
    forced = dot(jnp.concatenate(made, 0), bound_ref[...]).astype(jnp.bfloat16)
    for part in range(forced.shape[1] // 128):
        for s in range(3):
            table_ref[part * quarter : (part + 1) * quarter, s * 128 : (s + 1) * 128] = forced[
                s * quarter : (s + 1) * quarter, part * 128 : (part + 1) * 128
            ]


def combine(code, att, w_outs, x, w_bound):
    quarter = att[0].shape[0] // 3
    shape = (3, quarter, x.shape[1])
    table = (quarter * w_bound.shape[1] // 128, 384)
    far = [in_hbm(a) for a in (*w_outs, x, w_bound)]
    return pl.pallas_call(
        combine_kernel,
        out_shape=[jax.ShapeDtypeStruct(s, jnp.bfloat16) for s in (shape, table)],
        in_specs=[SCALARS]
        + [pl.BlockSpec(a.shape, lambda: (0, 0)) for a in att]
        + [pl.BlockSpec(memory_space=pltpu.HBM)] * len(far),
        out_specs=[pl.BlockSpec(shape, lambda: (0, 0, 0)), ON_CHIP],
        scratch_shapes=[
            pltpu.VMEM((quarter, x.shape[1]), jnp.bfloat16),
            pltpu.VMEM((len(att) * att[0].shape[1], x.shape[1]), jnp.bfloat16),
            pltpu.VMEM(w_bound.shape, jnp.bfloat16),
            pltpu.SemaphoreType.DMA((len(far),)),
        ],
        compiler_params=pltpu.CompilerParams(vmem_limit_bytes=16 * MIB),
        name="combine",
    )(code, *att, *far)


def serve_kernel(asked_ref, table_ref, send_ref):
    pick = pick_rows(asked_ref[...], send_ref.shape[0] * 16, table_ref.shape[0] // 4)
    send_ref[...] = dot(pick, table_ref[...]).astype(jnp.bfloat16).reshape(send_ref.shape)


def serve(asked, table):
    shape = (asked.shape[0], 16, table.shape[1])
    return pl.pallas_call(
        serve_kernel,
        out_shape=jax.ShapeDtypeStruct(shape, jnp.bfloat16),
        in_specs=[ON_CHIP] * 2,
        out_specs=pl.BlockSpec(shape, lambda: (0, 0, 0)),
        compiler_params=pltpu.CompilerParams(vmem_limit_bytes=8 * MIB),
        name="serve",
    )(asked, table)


def inputs_kernel(arrived_ref, band_ref, reg_ref, out_ref, first_ref, last_ref):
    cols, rows, channels = reg_ref.shape
    cells = cols * rows
    slots = arrived_ref.shape[0] * arrived_ref.shape[1]
    table = arrived_ref[...].reshape(slots, 384)
    band_row = cells_row(band_ref[...])
    r, c = iota((cells, cells), 0), iota((cells, cells), 1)
    band_col = jnp.sum(jnp.where(r == c, band_row, 0.0), -1, keepdims=True)
    earlier = (band_col == band_row) & (c < r)
    slot = jnp.sum(jnp.where(earlier, 1.0, 0.0), -1, keepdims=True)
    target = (band_col * 16.0 + slot * 4.0).astype(jnp.int32)
    lane = iota((cells, slots), 1) - target
    for part in range(channels // 128):
        take = jnp.where(lane == part, 1.0, 0.0).astype(jnp.bfloat16)
        taken = dot(take, table)
        lanes = slice(part * 128, (part + 1) * 128)
        reg = reg_ref[:, :, lanes].astype(jnp.float32)
        for s in range(3):
            forced = taken[:, s * 128 : (s + 1) * 128]
            made = (reg + forced.reshape(cols, rows, 128)).astype(jnp.bfloat16)
            out_ref[:, s * rows : (s + 1) * rows, lanes] = made
            first_ref[s * rows : (s + 1) * rows, lanes] = made[0]
            last_ref[s * rows : (s + 1) * rows, lanes] = made[cols - 1]


def make_inputs(arrived, band, reg):
    cols, rows, channels = reg.shape
    shapes = [(cols, 3 * rows, channels), (3 * rows, channels), (3 * rows, channels)]
    return pl.pallas_call(
        inputs_kernel,
        out_shape=[jax.ShapeDtypeStruct(s, jnp.bfloat16) for s in shapes],
        in_specs=[ON_CHIP] * 3,
        out_specs=[ON_CHIP] * 3,
        compiler_params=pltpu.CompilerParams(vmem_limit_bytes=6 * MIB),
        name="inputs",
    )(arrived, band, reg)


def row_shifts(x, rows):
    wide = x.astype(jnp.float32)
    total = x.shape[0]
    row = iota((total, 1), 0) % rows
    low = jnp.where(row > 0, pltpu.roll(wide, 1, 0), 0.0).astype(jnp.bfloat16)
    high = jnp.where(row < rows - 1, pltpu.roll(wide, total - 1, 0), 0.0).astype(jnp.bfloat16)
    return low, x, high


def inner_kernel(x_ref, before_ref, conv_hbm_ref, sum_ref, after_ref, held_ref, sems):
    copies = [
        pltpu.make_async_copy(conv_hbm_ref.at[pl.ds(3, 3)], held_ref, sems.at[0]),
        pltpu.make_async_copy(conv_hbm_ref.at[pl.ds(6, 3)], after_ref, sems.at[1]),
    ]
    for copy in copies:
        copy.start()
    cols, slab, channels = x_ref.shape
    cells = cols * slab
    shifts = row_shifts(x_ref[...].reshape(cells, channels), slab // 3)

    def product(first, last, w_ref):
        total = None
        for b, x in enumerate(shifts):
            one = dot(x[first:last], w_ref[b])
            total = one if total is None else total + one
        return total

    before = product(0, cells - slab, before_ref)
    copies[0].wait()
    middle = product(0, cells, held_ref)
    copies[1].wait()
    after = product(slab, cells, after_ref)
    sum_ref[:slab] = middle[:slab] + after[:slab]
    sum_ref[slab : cells - slab] = middle[slab : cells - slab] + before[: cells - 2 * slab] + after[slab:]
    sum_ref[cells - slab :] = middle[cells - slab :] + before[cells - 2 * slab :]


def convolve_inner(x, taps, conv_w):
    cols, slab, channels = x.shape
    return pl.pallas_call(
        inner_kernel,
        out_shape=[
            jax.ShapeDtypeStruct((cols * slab, channels), jnp.float32),
            jax.ShapeDtypeStruct(taps.shape, taps.dtype),
        ],
        in_specs=[ON_CHIP] * 2 + [pl.BlockSpec(memory_space=pltpu.HBM)],
        out_specs=[ON_CHIP] * 2,
        scratch_shapes=[
            pltpu.VMEM((3, channels, channels), jnp.bfloat16),
            pltpu.SemaphoreType.DMA((2,)),
        ],
        compiler_params=pltpu.CompilerParams(vmem_limit_bytes=16 * MIB),
        name="convolve_inner",
    )(x, taps, conv_w)


def finish_kernel(x_ref, before_ref, after_ref, w_before_ref, w_after_ref, sum_ref, out_ref):
    cols, slab, channels = x_ref.shape
    rows = slab // 3
    sides = []
    for ref, w_ref in ((before_ref, w_before_ref), (after_ref, w_after_ref)):
        total = None
        for b, x in enumerate(row_shifts(ref[...], rows)):
            one = dot(x, w_ref[b])
            total = one if total is None else total + one
        sides.append(total)
    for col in range(cols):
        conv = sum_ref[col * slab : (col + 1) * slab]
        if col == 0:
            conv = conv + sides[0]
        if col == cols - 1:
            conv = conv + sides[1]
        result = x_ref[col].astype(jnp.float32) + conv / (1.0 + jnp.exp(-conv))
        result = result.astype(jnp.bfloat16)
        for s in range(3):
            out_ref[s, col] = result[s * rows : (s + 1) * rows]


def convolve_finish(x, before, after, w_before, w_after, total):
    cols, slab, channels = x.shape
    shape = (3, cols, slab // 3, channels)
    return pl.pallas_call(
        finish_kernel,
        out_shape=jax.ShapeDtypeStruct(shape, jnp.bfloat16),
        in_specs=[ON_CHIP] * 6,
        out_specs=pl.BlockSpec(shape, lambda: (0, 0, 0, 0)),
        compiler_params=pltpu.CompilerParams(vmem_limit_bytes=8 * MIB),
        name="convolve_finish",
    )(x, before, after, w_before, w_after, total)


def neighbours(last, first, axis):
    count = lax.axis_size(axis)
    up = [(i, i + 1) for i in range(count - 1)]
    down = [(j, i) for i, j in up]
    return lax.ppermute(last, axis, up), lax.ppermute(first, axis, down)


def per_device(
    global_state,
    band_codes,
    norm_gain,
    w_query,
    w_key,
    w_value,
    w_out,
    reg_state,
    src_band,
    src_tok,
    w_bound,
    conv_w,
):
    ranks = lax.axis_size("tp")
    bands = lax.axis_size(BANDS)
    tokens, features = global_state.shape
    half = tokens // 2
    gain = in_hbm(norm_gain)
    cell_band = src_band.reshape(src_tok.shape)

    up = [(i, (i + 1) % ranks) for i in range(ranks)]
    down = [(j, i) for i, j in up]
    last, first, *weights = make_edges(
        band_codes, in_hbm(global_state), [in_hbm(w) for w in (w_query, w_key, w_value)]
    )
    before, after = neighbours(last, first, BANDS)
    w1, w3 = lax.ppermute(w_out, "tp", up), lax.ppermute(w_out, "tp", down)
    q, k, v = project(band_codes, [first, last], gain, weights, False)
    asked = ask(cell_band, src_tok, bands)
    q, w1, w3 = lax.optimization_barrier((q, w1, w3))
    middle = w_out.shape[0] // 2
    top, low = lax.ppermute(w1[:middle], "tp", up), lax.ppermute(w3[middle:], "tp", down)
    q, before, after = lax.optimization_barrier((q, before, after))
    k_halo, v_halo = project(band_codes, [before, after], gain, weights[1:], True)
    attended = attend(q, k, v, k_halo, v_halo, ranks, bands)
    attended, asked, top, low = lax.optimization_barrier((attended, asked, top, low))
    attended = [attended[0]] + [
        lax.ppermute(attended[d], "tp", [(i, (i + d) % ranks) for i in range(ranks)])
        for d in range(1, ranks)
    ]
    asked = lax.all_to_all(asked[:, None, :], BANDS, 0, 0, tiled=True)[:, 0, :]
    global_out, table = combine(band_codes, attended, [w_out, w1, w3, top, low], global_state, w_bound)
    send = serve(asked, table)
    conv_w, send = lax.optimization_barrier((conv_w, send))
    conv_w = in_hbm(conv_w)
    taps = fetch_taps(conv_w)
    arrived = lax.all_to_all(send, BANDS, 0, 0, tiled=True)
    taps, arrived = lax.optimization_barrier((taps, arrived))
    inputs, first, last = make_inputs(arrived, cell_band, reg_state)
    before, after = neighbours(last, first, CELLS)
    total, late = convolve_inner(inputs, taps, conv_w)
    return global_out, convolve_finish(inputs, before, after, taps, late, total)


def solution(mesh):
    placed = (
        P(("sec", "tile"), None),
        P(("sec", "tile")),
        P(),
        P(None, "tp"),
        P(None, "tp"),
        P(None, "tp"),
        P("tp", None),
        P(("sec", "tile", "tp"), None, None),
        P(("sec", "tile", "tp"), None, None),
        P(("sec", "tile", "tp"), None),
        P(),
        P(),
    )
    return jax.shard_map(
        per_device,
        mesh=mesh,
        in_specs=placed,
        out_specs=(
            P(None, ("sec", "tile", "tp"), None),
            P(None, ("sec", "tile", "tp"), None, None),
        ),
        check_vma=False,
    )
```

```python
import functools

import jax
import jax.numpy as jnp
from jax import lax
from jax.experimental import pallas as pl
from jax.experimental.pallas import tpu as pltpu
from jax.sharding import PartitionSpec as P

HD = 64
SIGNS = (0.0, 1.0, -1.0)
BANDS = ("sec", "tile")
CELLS = ("sec", "tile", "tp")
LOG2E = 1.4426950408889634
MIB = 1024 * 1024
ON_CHIP = pl.BlockSpec(memory_space=pltpu.VMEM)
SCALARS = pl.BlockSpec(memory_space=pltpu.SMEM)

mix_band = 73856093
mix_token = 19349663
mix_feature = 83492791
mix_again = 668265261


def iota(shape, dim):
    return lax.broadcasted_iota(jnp.int32, shape, dim)


def in_hbm(x):
    return pltpu.with_memory_space_constraint(x, pltpu.HBM)


def dot(a, b):
    return jnp.dot(a, b, preferred_element_type=jnp.float32)


def dot_t(a, b):
    return lax.dot_general(a, b, (((1,), (1,)), ((), ())), preferred_element_type=jnp.float32)


def wiggle(code, first_token, rows, features):
    by_row = code * mix_band + (first_token + iota((rows, 1), 0)) * mix_token
    mixed = by_row + iota((1, features), 1) * mix_feature
    mixed = lax.bitwise_xor(mixed, lax.shift_right_arithmetic(mixed, jnp.full_like(mixed, 15)))
    mixed = mixed * mix_again
    mixed = lax.bitwise_xor(mixed, lax.shift_right_arithmetic(mixed, jnp.full_like(mixed, 13)))
    level = lax.bitwise_and(mixed, 1023).astype(jnp.float32)
    return (level - 511.5) * (0.5 / 295.6)


def edges_kernel(code_ref, x_ref, *refs):
    *refs, sems = refs
    count = (len(refs) - 2) // 2
    weights, (last_ref, first_ref, *held) = refs[:count], refs[count:]
    half = x_ref.shape[0] // 2
    pairs = [
        (x_ref.at[pl.ds(half, half)], last_ref.at[pl.ds(0, half)]),
        (x_ref.at[pl.ds(0, half)], first_ref.at[pl.ds(0, half)]),
        *zip(weights, held),
    ]
    copies = [pltpu.make_async_copy(a, b, sems.at[i]) for i, (a, b) in enumerate(pairs)]
    for copy in copies:
        copy.start()
    code = jnp.full((16, x_ref.shape[1]), code_ref[0], jnp.int32)
    lane = iota(code.shape, 1)
    shift = jnp.where(lane == 0, 16, jnp.where(lane == 1, 8, 0))
    digit = lax.bitwise_and(lax.shift_right_arithmetic(code, shift), 255)
    digit = digit.astype(jnp.float32).astype(jnp.bfloat16)
    last_ref[half:] = digit
    first_ref[half:] = digit
    for copy in copies:
        copy.wait()


def make_edges(code, x, weights):
    tokens, features = x.shape
    shapes = [(tokens // 2 + 16, features)] * 2 + [w.shape for w in weights]
    return pl.pallas_call(
        edges_kernel,
        out_shape=[jax.ShapeDtypeStruct(s, jnp.bfloat16) for s in shapes],
        in_specs=[SCALARS] + [pl.BlockSpec(memory_space=pltpu.HBM)] * (1 + len(weights)),
        out_specs=[ON_CHIP] * len(shapes),
        scratch_shapes=[pltpu.SemaphoreType.DMA((2 + len(weights),))],
        compiler_params=pltpu.CompilerParams(vmem_limit_bytes=2 * MIB),
        name="edges",
    )(code, x, *weights)


def project_kernel(code_ref, early_ref, late_ref, gain_ref, *refs, halo):
    *refs, both_ref, inv_ref = refs
    step = pl.program_id(0)
    rows = early_ref.shape[0] - 16
    if halo:
        first = (1 - step) * rows
        digits = jnp.where(
            step == 0, early_ref[rows : rows + 16, 0:128], late_ref[rows : rows + 16, 0:128]
        ).astype(jnp.float32)[0:1]
        lane = iota((1, 128), 1)
        place = jnp.where(lane == 0, 65536.0, jnp.where(lane == 1, 256.0, 1.0))
        code = jnp.sum(jnp.where(lane < 3, digits * place, 0.0), -1, keepdims=True)
        code = code.astype(jnp.int32)
    else:
        first = step * rows
        code = jnp.full((1, 1), code_ref[0], jnp.int32)
    weights, outs = refs[: len(refs) // 2], refs[len(refs) // 2 :]
    features = both_ref.shape[1]
    gain = gain_ref[...].astype(jnp.float32).reshape(1, features)
    chunk, block = 16, 128
    for at in range(0, rows, block):
        for r in range(at, at + block, chunk):
            x = jnp.where(step == 0, early_ref[r : r + chunk], late_ref[r : r + chunk])
            x = x.astype(jnp.float32)
            p = wiggle(code, first + r, chunk, features)
            place = 2 * at + (r - at)
            both_ref[place : place + chunk] = (x * gain).astype(jnp.bfloat16)
            both_ref[place + block : place + block + chunk] = (p * gain).astype(jnp.bfloat16)
            for s, sign in enumerate(SIGNS):
                state = x if sign == 0.0 else (x + p if sign > 0 else x - p)
                mean = jnp.sum(state * state, -1, keepdims=True) * (1.0 / features)
                inv_ref[s, r : r + chunk] = lax.rsqrt(mean + 1e-06)
        here = slice(at, at + block)
        for index, (w_ref, out_ref) in enumerate(zip(weights, outs)):
            scale = HD**-0.5 * LOG2E if (index == 0 and not halo) else 1.0
            made = dot(both_ref[2 * at : 2 * at + 2 * block], w_ref[...])
            base, diff = made[:block], made[block:]
            for s, sign in enumerate(SIGNS):
                full = base if sign == 0.0 else (base + diff if sign > 0 else base - diff)
                out_ref[s, here] = (full * (inv_ref[s, here] * scale)).astype(jnp.bfloat16)


def project(code, arrays, gain, weights, halo):
    features = gain.shape[0]
    cols = weights[0].shape[1]
    tokens = 2 * (arrays[0].shape[0] - 16)
    specs = [ON_CHIP for a in arrays]
    rows = tokens // 2
    return pl.pallas_call(
        functools.partial(project_kernel, halo=halo),
        out_shape=[jax.ShapeDtypeStruct((3, tokens, cols), jnp.bfloat16) for _ in weights],
        grid=(2,),
        in_specs=[SCALARS]
        + specs
        + [pl.BlockSpec(gain.shape, lambda i: (0,))]
        + [ON_CHIP for w in weights],
        out_specs=[pl.BlockSpec((3, rows, cols), lambda i: (0, i, 0)) for _ in weights],
        scratch_shapes=[
            pltpu.VMEM((2 * rows, features), jnp.bfloat16),
            pltpu.VMEM((3, rows, 1), jnp.float32),
        ],
        compiler_params=pltpu.CompilerParams(vmem_limit_bytes=12 * MIB),
        name="project_halo" if halo else "project_own",
    )(code, *arrays, gain, *weights)


def attend_kernel(q_ref, k_ref, v_ref, k_halo_ref, v_halo_ref, *refs, bands):
    *out_refs, held_ref = refs
    tokens, cols = q_ref.shape[1:]
    half = tokens // 2
    band = lax.axis_index(BANDS)
    left = band > 0
    right = band < bands - 1
    head_of = iota((1, cols), 1) // HD
    k = k_ref[0]
    v = v_ref[0]
    row = iota((tokens, 1), 0)
    there = jnp.where(row < half, left.astype(jnp.int32), right.astype(jnp.int32)) > 0
    k_halo = jnp.where(there, k_halo_ref[0], k)
    v_halo = v_halo_ref[0]
    one = there.astype(jnp.bfloat16)
    v_halo = v_halo * one
    block = half
    for part in range(tokens // block):
        q = q_ref[0, part * block : (part + 1) * block, :]
        gathered = jnp.zeros((block, cols), jnp.float32)
        for head in range(cols // HD):
            mine = head_of == head
            q_head = jnp.where(mine, q, jnp.zeros_like(q))
            own = dot_t(q_head, k)
            far = dot_t(q_head, k_halo)
            top = jnp.maximum(
                jnp.max(own, -1, keepdims=True), jnp.max(far, -1, keepdims=True)
            )
            own = jnp.exp2(own - top).astype(jnp.bfloat16)
            far = jnp.exp2(far - top).astype(jnp.bfloat16)
            v_own = jnp.where(mine, v, jnp.ones_like(v))
            v_far = jnp.where(mine, v_halo, jnp.broadcast_to(one, v.shape))
            acc = dot(own, v_own) + dot(far, v_far)
            total = pltpu.roll(acc, cols // 2, 1)
            gathered = jnp.where(mine, acc / total, gathered)
        held_ref[part * block : (part + 1) * block] = gathered.astype(jnp.bfloat16)
    ranks = len(out_refs)
    quarter = tokens // ranks
    rank = lax.axis_index("tp")
    for distance, out_ref in enumerate(out_refs):
        first = pl.multiple_of(lax.rem(rank + distance, ranks) * quarter, quarter)
        out_ref[...] = held_ref[pl.ds(first, quarter), :]


def attend(q, k, v, k_halo, v_halo, ranks, bands):
    forwards, tokens, cols = q.shape
    spec = pl.BlockSpec((1, tokens, cols), lambda i: (i, 0, 0))
    quarter = tokens // ranks
    return pl.pallas_call(
        functools.partial(attend_kernel, bands=bands),
        out_shape=[jax.ShapeDtypeStruct((forwards * quarter, cols), jnp.bfloat16)] * ranks,
        grid=(forwards,),
        in_specs=[spec] * 5,
        out_specs=[pl.BlockSpec((quarter, cols), lambda i: (i, 0))] * ranks,
        scratch_shapes=[pltpu.VMEM((tokens, cols), jnp.bfloat16)],
        compiler_params=pltpu.CompilerParams(vmem_limit_bytes=14 * MIB),
        name="attend",
    )(q, k, v, k_halo, v_halo)


def cells_row(x):
    cols, rows = x.shape
    cells = cols * rows
    spread = (iota((rows, cells), 1) % rows == iota((rows, cells), 0)).astype(jnp.float32)
    wide = dot(x.astype(jnp.float32).astype(jnp.bfloat16), spread.astype(jnp.bfloat16))
    mine = iota((cols, cells), 1) // rows == iota((cols, cells), 0)
    return jnp.sum(jnp.where(mine, wide, 0.0), 0, keepdims=True)


def names_kernel(band_ref, tok_ref, out_ref):
    names = cells_row(band_ref[...]) * 128.0 + cells_row(tok_ref[...])
    out_ref[...] = names.astype(jnp.int32)


def make_names(band, tok):
    return pl.pallas_call(
        names_kernel,
        out_shape=jax.ShapeDtypeStruct((1, band.size), jnp.int32),
        in_specs=[ON_CHIP] * 2,
        out_specs=ON_CHIP,
        compiler_params=pltpu.CompilerParams(vmem_limit_bytes=2 * MIB),
        name="names",
    )(band, tok)


def pass_on(rows, distance):
    count = lax.axis_size(BANDS)
    came = lax.ppermute(rows, BANDS, [(i, (i + distance) % count) for i in range(count)])
    return jnp.concatenate([rows, came])


def pick_kernel(names_ref, pick_ref):
    bands, cells = names_ref.shape
    rows, wide = pick_ref.shape
    me = lax.axis_index(BANDS)
    names = names_ref[...]
    match = lax.shift_right_arithmetic(names, jnp.full_like(names, 7)) == me
    match = match.astype(jnp.float32)
    token = lax.bitwise_and(names, 127).astype(jnp.float32)
    before = (iota((cells, cells), 0) < iota((cells, cells), 1)).astype(jnp.float32)
    slot = dot(match.astype(jnp.bfloat16), before.astype(jnp.bfloat16))
    lanes = iota((bands, cells), 1)
    asked = jnp.zeros((bands, cells), jnp.float32)
    for s in range(4):
        hit = jnp.where(slot == s, match, 0.0)
        token_s = jnp.sum(hit * (token + 1.0), -1, keepdims=True) - 1.0
        asked = jnp.where(lanes == s, token_s, asked)
    r = iota((rows, 1), 0)
    row_of = lax.rem(me + bands - r // 16, bands)
    spread = (iota((rows, bands), 1) == row_of).astype(jnp.float32).astype(jnp.bfloat16)
    per_row = dot(spread, asked.astype(jnp.bfloat16))
    mine = iota((rows, cells), 1) == (r // 4) % 4
    token_r = jnp.sum(jnp.where(mine, per_row, 0.0), -1, keepdims=True).astype(jnp.int32)
    target = jnp.where(token_r >= 0, (r % 4) * cells + token_r, -1)
    pick_ref[...] = (iota((rows, wide), 1) == target).astype(jnp.float32).astype(jnp.bfloat16)


def make_pick(names):
    bands, cells = names.shape
    return pl.pallas_call(
        pick_kernel,
        out_shape=jax.ShapeDtypeStruct((bands * 16, 4 * cells), jnp.bfloat16),
        in_specs=[ON_CHIP],
        out_specs=ON_CHIP,
        compiler_params=pltpu.CompilerParams(vmem_limit_bytes=6 * MIB),
        name="pick",
    )(names)


def fetch_kernel(conv_hbm_ref, taps_ref, sem):
    copy = pltpu.make_async_copy(conv_hbm_ref.at[pl.ds(0, 3)], taps_ref, sem)
    copy.start()
    copy.wait()


def fetch_taps(conv_w):
    return pl.pallas_call(
        fetch_kernel,
        out_shape=jax.ShapeDtypeStruct((3, *conv_w.shape[1:]), conv_w.dtype),
        in_specs=[pl.BlockSpec(memory_space=pltpu.HBM)],
        out_specs=ON_CHIP,
        scratch_shapes=[pltpu.SemaphoreType.DMA(())],
        compiler_params=pltpu.CompilerParams(vmem_limit_bytes=2 * MIB),
        name="fetch",
    )(conv_w)


def combine_kernel(code_ref, att0_ref, att1_ref, att2_ref, att3_ref, w0_ref, w1_ref, w3_ref, top_ref, low_ref, x_ref, w_bound_ref, pick_ref, out_ref, send_ref, table_ref, own_ref, held_ref, bound_ref, sems):
    cols = att0_ref.shape[1]
    half = cols // 2
    features = x_ref.shape[1]
    quarter = out_ref.shape[1]
    rank = lax.axis_index("tp")
    rows = pl.ds(pl.multiple_of(rank * quarter, quarter), quarter)
    pairs = [
        (w0_ref, held_ref.at[pl.ds(0, cols)]),
        (w1_ref, held_ref.at[pl.ds(cols, cols)]),
        (w3_ref, held_ref.at[pl.ds(2 * cols, cols)]),
        (top_ref, held_ref.at[pl.ds(3 * cols, half)]),
        (low_ref, held_ref.at[pl.ds(3 * cols + half, half)]),
        (x_ref.at[rows], own_ref),
        (w_bound_ref, bound_ref),
    ]
    copies = [pltpu.make_async_copy(a, b, sems.at[i]) for i, (a, b) in enumerate(pairs)]
    for copy in copies:
        copy.start()
    code = jnp.full((1, 1), code_ref[0], jnp.int32)
    p = wiggle(code, rank * quarter, quarter, features)
    copies[0].wait()
    total = dot(att0_ref[...], held_ref[:cols])
    copies[1].wait()
    total = total + dot(att1_ref[...], held_ref[cols : 2 * cols])
    copies[2].wait()
    total = total + dot(att3_ref[...], held_ref[2 * cols : 3 * cols])
    copies[3].wait()
    copies[4].wait()
    total = total + dot(att2_ref[...], held_ref[3 * cols :])
    copies[5].wait()
    x = own_ref[...].astype(jnp.float32)
    made = []
    for s, sign in enumerate(SIGNS):
        part = x if sign == 0.0 else (x + p if sign > 0 else x - p)
        part = (part + total[s * quarter : (s + 1) * quarter]).astype(jnp.bfloat16)
        out_ref[s] = part
        made.append(part)
    copies[6].wait()
    forced = dot(jnp.concatenate(made, 0), bound_ref[...]).astype(jnp.bfloat16)
    for part in range(forced.shape[1] // 128):
        for s in range(3):
            table_ref[part * quarter : (part + 1) * quarter, s * 128 : (s + 1) * 128] = forced[
                s * quarter : (s + 1) * quarter, part * 128 : (part + 1) * 128
            ]
    picked = dot(pick_ref[...], table_ref[...])
    send_ref[...] = picked.astype(jnp.bfloat16).reshape(send_ref.shape)


def combine(code, att, w_outs, x, w_bound, pick):
    quarter = att[0].shape[0] // 3
    shape = (3, quarter, x.shape[1])
    table = (quarter * w_bound.shape[1] // 128, 384)
    sent = (pick.shape[0] // 16, 16, 384)
    far = [in_hbm(a) for a in (*w_outs, x, w_bound)]
    return pl.pallas_call(
        combine_kernel,
        out_shape=[jax.ShapeDtypeStruct(s, jnp.bfloat16) for s in (shape, sent)],
        in_specs=[SCALARS]
        + [pl.BlockSpec(a.shape, lambda: (0, 0)) for a in att]
        + [pl.BlockSpec(memory_space=pltpu.HBM)] * len(far)
        + [ON_CHIP],
        out_specs=[pl.BlockSpec(s, lambda: (0, 0, 0)) for s in (shape, sent)],
        scratch_shapes=[
            pltpu.VMEM(table, jnp.bfloat16),
            pltpu.VMEM((quarter, x.shape[1]), jnp.bfloat16),
            pltpu.VMEM((len(att) * att[0].shape[1], x.shape[1]), jnp.bfloat16),
            pltpu.VMEM(w_bound.shape, jnp.bfloat16),
            pltpu.SemaphoreType.DMA((len(far),)),
        ],
        compiler_params=pltpu.CompilerParams(vmem_limit_bytes=16 * MIB),
        name="combine",
    )(code, *att, *far, pick)


def inputs_kernel(arrived_ref, band_ref, reg_ref, out_ref, first_ref, last_ref):
    cols, rows, channels = reg_ref.shape
    cells = cols * rows
    slots = arrived_ref.shape[0] * arrived_ref.shape[1]
    table = arrived_ref[...].reshape(slots, 384)
    band_row = cells_row(band_ref[...])
    r, c = iota((cells, cells), 0), iota((cells, cells), 1)
    band_col = jnp.sum(jnp.where(r == c, band_row, 0.0), -1, keepdims=True)
    earlier = (band_col == band_row) & (c < r)
    slot = jnp.sum(jnp.where(earlier, 1.0, 0.0), -1, keepdims=True)
    target = (band_col * 16.0 + slot * 4.0).astype(jnp.int32)
    lane = iota((cells, slots), 1) - target
    for part in range(channels // 128):
        take = jnp.where(lane == part, 1.0, 0.0).astype(jnp.bfloat16)
        taken = dot(take, table)
        lanes = slice(part * 128, (part + 1) * 128)
        reg = reg_ref[:, :, lanes].astype(jnp.float32)
        for s in range(3):
            forced = taken[:, s * 128 : (s + 1) * 128]
            made = (reg + forced.reshape(cols, rows, 128)).astype(jnp.bfloat16)
            out_ref[:, s * rows : (s + 1) * rows, lanes] = made
            first_ref[s * rows : (s + 1) * rows, lanes] = made[0]
            last_ref[s * rows : (s + 1) * rows, lanes] = made[cols - 1]


def make_inputs(arrived, band, reg):
    cols, rows, channels = reg.shape
    shapes = [(cols, 3 * rows, channels), (3 * rows, channels), (3 * rows, channels)]
    return pl.pallas_call(
        inputs_kernel,
        out_shape=[jax.ShapeDtypeStruct(s, jnp.bfloat16) for s in shapes],
        in_specs=[ON_CHIP] * 3,
        out_specs=[ON_CHIP] * 3,
        compiler_params=pltpu.CompilerParams(vmem_limit_bytes=6 * MIB),
        name="inputs",
    )(arrived, band, reg)


def row_shifts(x, rows):
    wide = x.astype(jnp.float32)
    total = x.shape[0]
    row = iota((total, 1), 0) % rows
    low = jnp.where(row > 0, pltpu.roll(wide, 1, 0), 0.0).astype(jnp.bfloat16)
    high = jnp.where(row < rows - 1, pltpu.roll(wide, total - 1, 0), 0.0).astype(jnp.bfloat16)
    return low, x, high


def inner_kernel(x_ref, before_ref, conv_hbm_ref, sum_ref, after_ref, held_ref, sems):
    copies = [
        pltpu.make_async_copy(conv_hbm_ref.at[pl.ds(3, 3)], held_ref, sems.at[0]),
        pltpu.make_async_copy(conv_hbm_ref.at[pl.ds(6, 3)], after_ref, sems.at[1]),
    ]
    for copy in copies:
        copy.start()
    cols, slab, channels = x_ref.shape
    cells = cols * slab
    shifts = row_shifts(x_ref[...].reshape(cells, channels), slab // 3)

    def product(first, last, w_ref):
        total = None
        for b, x in enumerate(shifts):
            one = dot(x[first:last], w_ref[b])
            total = one if total is None else total + one
        return total

    before = product(0, cells - slab, before_ref)
    copies[0].wait()
    middle = product(0, cells, held_ref)
    copies[1].wait()
    after = product(slab, cells, after_ref)
    sum_ref[:slab] = middle[:slab] + after[:slab]
    sum_ref[slab : cells - slab] = middle[slab : cells - slab] + before[: cells - 2 * slab] + after[slab:]
    sum_ref[cells - slab :] = middle[cells - slab :] + before[cells - 2 * slab :]


def convolve_inner(x, taps, conv_w):
    cols, slab, channels = x.shape
    return pl.pallas_call(
        inner_kernel,
        out_shape=[
            jax.ShapeDtypeStruct((cols * slab, channels), jnp.float32),
            jax.ShapeDtypeStruct(taps.shape, taps.dtype),
        ],
        in_specs=[ON_CHIP] * 2 + [pl.BlockSpec(memory_space=pltpu.HBM)],
        out_specs=[ON_CHIP] * 2,
        scratch_shapes=[
            pltpu.VMEM((3, channels, channels), jnp.bfloat16),
            pltpu.SemaphoreType.DMA((2,)),
        ],
        compiler_params=pltpu.CompilerParams(vmem_limit_bytes=16 * MIB),
        name="convolve_inner",
    )(x, taps, conv_w)


def finish_kernel(x_ref, before_ref, after_ref, w_before_ref, w_after_ref, sum_ref, out_ref):
    cols, slab, channels = x_ref.shape
    rows = slab // 3
    sides = []
    for ref, w_ref in ((before_ref, w_before_ref), (after_ref, w_after_ref)):
        total = None
        for b, x in enumerate(row_shifts(ref[...], rows)):
            one = dot(x, w_ref[b])
            total = one if total is None else total + one
        sides.append(total)
    for col in range(cols):
        conv = sum_ref[col * slab : (col + 1) * slab]
        if col == 0:
            conv = conv + sides[0]
        if col == cols - 1:
            conv = conv + sides[1]
        result = x_ref[col].astype(jnp.float32) + conv / (1.0 + jnp.exp(-conv))
        result = result.astype(jnp.bfloat16)
        for s in range(3):
            out_ref[s, col] = result[s * rows : (s + 1) * rows]


def convolve_finish(x, before, after, w_before, w_after, total):
    cols, slab, channels = x.shape
    shape = (3, cols, slab // 3, channels)
    return pl.pallas_call(
        finish_kernel,
        out_shape=jax.ShapeDtypeStruct(shape, jnp.bfloat16),
        in_specs=[ON_CHIP] * 6,
        out_specs=pl.BlockSpec(shape, lambda: (0, 0, 0, 0)),
        compiler_params=pltpu.CompilerParams(vmem_limit_bytes=8 * MIB),
        name="convolve_finish",
    )(x, before, after, w_before, w_after, total)


def neighbours(last, first, axis):
    count = lax.axis_size(axis)
    up = [(i, i + 1) for i in range(count - 1)]
    down = [(j, i) for i, j in up]
    return lax.ppermute(last, axis, up), lax.ppermute(first, axis, down)


def per_device(
    global_state,
    band_codes,
    norm_gain,
    w_query,
    w_key,
    w_value,
    w_out,
    reg_state,
    src_band,
    src_tok,
    w_bound,
    conv_w,
):
    ranks = lax.axis_size("tp")
    bands = lax.axis_size(BANDS)
    tokens, features = global_state.shape
    half = tokens // 2
    gain = in_hbm(norm_gain)
    cell_band = src_band.reshape(src_tok.shape)

    up = [(i, (i + 1) % ranks) for i in range(ranks)]
    down = [(j, i) for i, j in up]
    last, first, *weights = make_edges(
        band_codes, in_hbm(global_state), [in_hbm(w) for w in (w_query, w_key, w_value)]
    )
    before, after = neighbours(last, first, BANDS)
    w1, w3 = lax.ppermute(w_out, "tp", up), lax.ppermute(w_out, "tp", down)
    q, k, v = project(band_codes, [first, last], gain, weights, False)
    names = pass_on(make_names(cell_band, src_tok), 1)
    q, names = lax.optimization_barrier((q, names))
    names = pass_on(pass_on(names, 2), 4)
    q, w1, w3 = lax.optimization_barrier((q, w1, w3))
    middle = w_out.shape[0] // 2
    top, low = lax.ppermute(w1[:middle], "tp", up), lax.ppermute(w3[middle:], "tp", down)
    q, before, after, names = lax.optimization_barrier((q, before, after, names))
    k_halo, v_halo = project(band_codes, [before, after], gain, weights[1:], True)
    k_halo, names = lax.optimization_barrier((k_halo, names))
    names = pass_on(names, 8)
    attended = attend(q, k, v, k_halo, v_halo, ranks, bands)
    attended, names, top, low = lax.optimization_barrier((attended, names, top, low))
    attended = [attended[0]] + [
        lax.ppermute(attended[d], "tp", [(i, (i + d) % ranks) for i in range(ranks)])
        for d in range(1, ranks)
    ]
    for distance in (16, 32):
        names = pass_on(names, distance)
    global_out, send = combine(
        band_codes, attended, [w_out, w1, w3, top, low], global_state, w_bound, make_pick(names)
    )
    conv_w, send = lax.optimization_barrier((conv_w, send))
    conv_w = in_hbm(conv_w)
    taps = fetch_taps(conv_w)
    arrived = lax.all_to_all(send, BANDS, 0, 0, tiled=True)
    taps, arrived = lax.optimization_barrier((taps, arrived))
    inputs, first, last = make_inputs(arrived, cell_band, reg_state)
    before, after = neighbours(last, first, CELLS)
    total, late = convolve_inner(inputs, taps, conv_w)
    return global_out, convolve_finish(inputs, before, after, taps, late, total)


def solution(mesh):
    placed = (
        P(("sec", "tile"), None),
        P(("sec", "tile")),
        P(),
        P(None, "tp"),
        P(None, "tp"),
        P(None, "tp"),
        P("tp", None),
        P(("sec", "tile", "tp"), None, None),
        P(("sec", "tile", "tp"), None, None),
        P(("sec", "tile", "tp"), None),
        P(),
        P(),
    )
    return jax.shard_map(
        per_device,
        mesh=mesh,
        in_specs=placed,
        out_specs=(
            P(None, ("sec", "tile", "tp"), None),
            P(None, ("sec", "tile", "tp"), None, None),
        ),
        check_vma=False,
    )
```

```python
import functools

import jax
import jax.numpy as jnp
from jax import lax
from jax.experimental import pallas as pl
from jax.experimental.pallas import tpu as pltpu
from jax.sharding import PartitionSpec as P

HD = 64
SIGNS = (0.0, 1.0, -1.0)
BANDS = ("sec", "tile")
CELLS = ("sec", "tile", "tp")
LOG2E = 1.4426950408889634
FETCHED = 5
MIB = 1024 * 1024
ON_CHIP = pl.BlockSpec(memory_space=pltpu.VMEM)
SCALARS = pl.BlockSpec(memory_space=pltpu.SMEM)

mix_band = 73856093
mix_token = 19349663
mix_feature = 83492791
mix_again = 668265261


def iota(shape, dim):
    return lax.broadcasted_iota(jnp.int32, shape, dim)


def in_hbm(x):
    return pltpu.with_memory_space_constraint(x, pltpu.HBM)


def dot(a, b):
    return jnp.dot(a, b, preferred_element_type=jnp.float32)


def dot_t(a, b):
    return lax.dot_general(a, b, (((1,), (1,)), ((), ())), preferred_element_type=jnp.float32)


def wiggle(code, first_token, rows, features):
    by_row = code * mix_band + (first_token + iota((rows, 1), 0)) * mix_token
    mixed = by_row + iota((1, features), 1) * mix_feature
    mixed = lax.bitwise_xor(mixed, lax.shift_right_arithmetic(mixed, jnp.full_like(mixed, 15)))
    mixed = mixed * mix_again
    mixed = lax.bitwise_xor(mixed, lax.shift_right_arithmetic(mixed, jnp.full_like(mixed, 13)))
    level = lax.bitwise_and(mixed, 1023).astype(jnp.float32)
    return (level - 511.5) * (0.5 / 295.6)


def edges_kernel(code_ref, x_ref, *refs):
    *refs, sems = refs
    count = (len(refs) - 2) // 2
    weights, (last_ref, first_ref, *held) = refs[:count], refs[count:]
    half = x_ref.shape[0] // 2
    pairs = [
        (x_ref.at[pl.ds(half, half)], last_ref.at[pl.ds(0, half)]),
        (x_ref.at[pl.ds(0, half)], first_ref.at[pl.ds(0, half)]),
        *zip(weights, held),
    ]
    copies = [pltpu.make_async_copy(a, b, sems.at[i]) for i, (a, b) in enumerate(pairs)]
    for copy in copies:
        copy.start()
    code = jnp.full((16, x_ref.shape[1]), code_ref[0], jnp.int32)
    lane = iota(code.shape, 1)
    shift = jnp.where(lane == 0, 16, jnp.where(lane == 1, 8, 0))
    digit = lax.bitwise_and(lax.shift_right_arithmetic(code, shift), 255)
    digit = digit.astype(jnp.float32).astype(jnp.bfloat16)
    last_ref[half:] = digit
    first_ref[half:] = digit
    for copy in copies:
        copy.wait()


def make_edges(code, x, weights):
    tokens, features = x.shape
    shapes = [(tokens // 2 + 16, features)] * 2 + [w.shape for w in weights]
    return pl.pallas_call(
        edges_kernel,
        out_shape=[jax.ShapeDtypeStruct(s, jnp.bfloat16) for s in shapes],
        in_specs=[SCALARS] + [pl.BlockSpec(memory_space=pltpu.HBM)] * (1 + len(weights)),
        out_specs=[ON_CHIP] * len(shapes),
        scratch_shapes=[pltpu.SemaphoreType.DMA((2 + len(weights),))],
        compiler_params=pltpu.CompilerParams(vmem_limit_bytes=2 * MIB),
        name="edges",
    )(code, x, *weights)


def project_kernel(code_ref, early_ref, late_ref, gain_ref, *refs, halo):
    *refs, both_ref, inv_ref = refs
    step = pl.program_id(0)
    rows = early_ref.shape[0] - 16
    if halo:
        first = (1 - step) * rows
        digits = jnp.where(
            step == 0, early_ref[rows : rows + 16, 0:128], late_ref[rows : rows + 16, 0:128]
        ).astype(jnp.float32)[0:1]
        lane = iota((1, 128), 1)
        place = jnp.where(lane == 0, 65536.0, jnp.where(lane == 1, 256.0, 1.0))
        code = jnp.sum(jnp.where(lane < 3, digits * place, 0.0), -1, keepdims=True)
        code = code.astype(jnp.int32)
    else:
        first = step * rows
        code = jnp.full((1, 1), code_ref[0], jnp.int32)
    weights, outs = refs[: len(refs) // 2], refs[len(refs) // 2 :]
    features = both_ref.shape[1]
    gain = gain_ref[...].astype(jnp.float32).reshape(1, features)
    chunk, block = 16, 128
    for at in range(0, rows, block):
        for r in range(at, at + block, chunk):
            x = jnp.where(step == 0, early_ref[r : r + chunk], late_ref[r : r + chunk])
            x = x.astype(jnp.float32)
            p = wiggle(code, first + r, chunk, features)
            place = 2 * at + (r - at)
            both_ref[place : place + chunk] = (x * gain).astype(jnp.bfloat16)
            both_ref[place + block : place + block + chunk] = (p * gain).astype(jnp.bfloat16)
            for s, sign in enumerate(SIGNS):
                state = x if sign == 0.0 else (x + p if sign > 0 else x - p)
                mean = jnp.sum(state * state, -1, keepdims=True) * (1.0 / features)
                inv_ref[s, r : r + chunk] = lax.rsqrt(mean + 1e-06)
        here = slice(at, at + block)
        for index, (w_ref, out_ref) in enumerate(zip(weights, outs)):
            scale = HD**-0.5 * LOG2E if (index == 0 and not halo) else 1.0
            made = dot(both_ref[2 * at : 2 * at + 2 * block], w_ref[...])
            base, diff = made[:block], made[block:]
            for s, sign in enumerate(SIGNS):
                full = base if sign == 0.0 else (base + diff if sign > 0 else base - diff)
                out_ref[s, here] = (full * (inv_ref[s, here] * scale)).astype(jnp.bfloat16)


def project(code, arrays, gain, weights, halo):
    features = gain.shape[0]
    cols = weights[0].shape[1]
    tokens = 2 * (arrays[0].shape[0] - 16)
    specs = [ON_CHIP for a in arrays]
    rows = tokens // 2
    return pl.pallas_call(
        functools.partial(project_kernel, halo=halo),
        out_shape=[jax.ShapeDtypeStruct((3, tokens, cols), jnp.bfloat16) for _ in weights],
        grid=(2,),
        in_specs=[SCALARS]
        + specs
        + [pl.BlockSpec(gain.shape, lambda i: (0,))]
        + [ON_CHIP for w in weights],
        out_specs=[pl.BlockSpec((3, rows, cols), lambda i: (0, i, 0)) for _ in weights],
        scratch_shapes=[
            pltpu.VMEM((2 * rows, features), jnp.bfloat16),
            pltpu.VMEM((3, rows, 1), jnp.float32),
        ],
        compiler_params=pltpu.CompilerParams(vmem_limit_bytes=12 * MIB),
        name="project_halo" if halo else "project_own",
    )(code, *arrays, gain, *weights)


def attend_kernel(q_ref, k_ref, v_ref, k_halo_ref, v_halo_ref, *refs, bands):
    *out_refs, held_ref = refs
    tokens, cols = q_ref.shape[1:]
    half = tokens // 2
    band = lax.axis_index(BANDS)
    left = band > 0
    right = band < bands - 1
    k = k_ref[0]
    v = v_ref[0]
    row = iota((tokens, 1), 0)
    there = jnp.where(row < half, left.astype(jnp.int32), right.astype(jnp.int32)) > 0
    k_halo = jnp.where(there, k_halo_ref[0], k)
    one = there.astype(jnp.bfloat16)
    v_halo = v_halo_ref[0] * one
    block, pair = half, 2 * HD
    which = iota((1, pair), 1) // HD
    work = [(head, part) for head in range(cols // HD) for part in range(tokens // block)]

    def lanes(head):
        return slice(head // 2 * pair, (head // 2 + 1) * pair)

    def scores(head, part):
        q = q_ref[0, part * block : (part + 1) * block, lanes(head)]
        q = jnp.where(which == head % 2, q, jnp.zeros_like(q))
        return dot_t(q, k[:, lanes(head)]), dot_t(q, k_halo[:, lanes(head)])

    first = {}
    own, far = scores(*work[0])
    for index, (head, part) in enumerate(work):
        later = scores(*work[index + 1]) if index + 1 < len(work) else (None, None)
        mine = which == head % 2
        top = jnp.maximum(jnp.max(own, -1, keepdims=True), jnp.max(far, -1, keepdims=True))
        own = jnp.exp2(own - top).astype(jnp.bfloat16)
        far = jnp.exp2(far - top).astype(jnp.bfloat16)
        v_own, v_far = v[:, lanes(head)], v_halo[:, lanes(head)]
        v_own = jnp.where(mine, v_own, jnp.ones_like(v_own))
        v_far = jnp.where(mine, v_far, jnp.broadcast_to(one, v_far.shape))
        acc = dot(own, v_own) + dot(far, v_far)
        made = acc / pltpu.roll(acc, HD, 1)
        if head % 2 == 0:
            first[part] = made
        else:
            both = jnp.where(mine, made, first[part]).astype(jnp.bfloat16)
            held_ref[part * block : (part + 1) * block, lanes(head)] = both
        own, far = later
    ranks = len(out_refs)
    quarter = tokens // ranks
    rank = lax.axis_index("tp")
    for distance, out_ref in enumerate(out_refs):
        first = pl.multiple_of(lax.rem(rank + distance, ranks) * quarter, quarter)
        out_ref[...] = held_ref[pl.ds(first, quarter), :]


def attend(q, k, v, k_halo, v_halo, ranks, bands):
    forwards, tokens, cols = q.shape
    spec = pl.BlockSpec((1, tokens, cols), lambda i: (i, 0, 0))
    quarter = tokens // ranks
    return pl.pallas_call(
        functools.partial(attend_kernel, bands=bands),
        out_shape=[jax.ShapeDtypeStruct((forwards * quarter, cols), jnp.bfloat16)] * ranks,
        grid=(forwards,),
        in_specs=[spec] * 5,
        out_specs=[pl.BlockSpec((quarter, cols), lambda i: (i, 0))] * ranks,
        scratch_shapes=[pltpu.VMEM((tokens, cols), jnp.bfloat16)],
        compiler_params=pltpu.CompilerParams(vmem_limit_bytes=14 * MIB),
        name="attend",
    )(q, k, v, k_halo, v_halo)


def cells_row(x):
    cols, rows = x.shape
    cells = cols * rows
    spread = (iota((rows, cells), 1) % rows == iota((rows, cells), 0)).astype(jnp.float32)
    wide = dot(x.astype(jnp.float32).astype(jnp.bfloat16), spread.astype(jnp.bfloat16))
    mine = iota((cols, cells), 1) // rows == iota((cols, cells), 0)
    return jnp.sum(jnp.where(mine, wide, 0.0), 0, keepdims=True)


def ask_kernel(band_ref, tok_ref, ask_ref):
    bands = ask_ref.shape[0]
    named = cells_row(band_ref[...])
    token = cells_row(tok_ref[...])
    cells = named.shape[1]
    match = (named.astype(jnp.int32) == iota((bands, cells), 0)).astype(jnp.float32)
    before = (iota((cells, cells), 0) < iota((cells, cells), 1)).astype(jnp.float32)
    slot = dot(match.astype(jnp.bfloat16), before.astype(jnp.bfloat16))
    lanes = iota((bands, cells), 1)
    asked = jnp.zeros((bands, cells), jnp.float32)
    for s in range(4):
        hit = jnp.where(slot == s, match, 0.0)
        token_s = jnp.sum(hit * (token + 1.0), -1, keepdims=True) - 1.0
        asked = jnp.where(lanes == s, token_s, asked)
    ask_ref[...] = asked[:, :4].astype(jnp.int32)


def ask(band, tok, bands):
    return pl.pallas_call(
        ask_kernel,
        out_shape=jax.ShapeDtypeStruct((bands, 4), jnp.int32),
        in_specs=[ON_CHIP] * 2,
        out_specs=ON_CHIP,
        compiler_params=pltpu.CompilerParams(vmem_limit_bytes=4 * MIB),
        name="ask",
    )(band, tok)


def fetch_kernel(conv_hbm_ref, taps_ref, sem):
    copy = pltpu.make_async_copy(conv_hbm_ref.at[pl.ds(0, FETCHED)], taps_ref, sem)
    copy.start()
    copy.wait()


def fetch_taps(conv_w):
    return pl.pallas_call(
        fetch_kernel,
        out_shape=jax.ShapeDtypeStruct((FETCHED, *conv_w.shape[1:]), conv_w.dtype),
        in_specs=[pl.BlockSpec(memory_space=pltpu.HBM)],
        out_specs=ON_CHIP,
        scratch_shapes=[pltpu.SemaphoreType.DMA(())],
        compiler_params=pltpu.CompilerParams(vmem_limit_bytes=2 * MIB),
        name="fetch",
    )(conv_w)


def pick_rows(asked, rows, cells):
    bands = asked.shape[0]
    spread = (iota((rows, bands), 0) // 16 == iota((rows, bands), 1)).astype(jnp.float32)
    per_row = dot(spread.astype(jnp.bfloat16), asked.astype(jnp.float32).astype(jnp.bfloat16))
    r = iota((rows, 1), 0)
    mine = iota((rows, 4), 1) == (r // 4) % 4
    token_r = jnp.sum(jnp.where(mine, per_row, 0.0), -1, keepdims=True).astype(jnp.int32)
    target = jnp.where(token_r >= 0, (r % 4) * cells + token_r, -1)
    return (iota((rows, 4 * cells), 1) == target).astype(jnp.float32).astype(jnp.bfloat16)


def combine_kernel(code_ref, att0_ref, att1_ref, att2_ref, att3_ref, w0_ref, w1_ref, w3_ref, top_ref, low_ref, x_ref, w_bound_ref, out_ref, table_ref, own_ref, held_ref, bound_ref, sems):
    cols = att0_ref.shape[1]
    half = cols // 2
    features = x_ref.shape[1]
    quarter = out_ref.shape[1]
    rank = lax.axis_index("tp")
    rows = pl.ds(pl.multiple_of(rank * quarter, quarter), quarter)
    pairs = [
        (w0_ref, held_ref.at[pl.ds(0, cols)]),
        (w1_ref, held_ref.at[pl.ds(cols, cols)]),
        (w3_ref, held_ref.at[pl.ds(2 * cols, cols)]),
        (top_ref, held_ref.at[pl.ds(3 * cols, half)]),
        (low_ref, held_ref.at[pl.ds(3 * cols + half, half)]),
        (x_ref.at[rows], own_ref),
        (w_bound_ref, bound_ref),
    ]
    copies = [pltpu.make_async_copy(a, b, sems.at[i]) for i, (a, b) in enumerate(pairs)]
    for copy in copies:
        copy.start()
    code = jnp.full((1, 1), code_ref[0], jnp.int32)
    p = wiggle(code, rank * quarter, quarter, features)
    copies[0].wait()
    total = dot(att0_ref[...], held_ref[:cols])
    copies[1].wait()
    total = total + dot(att1_ref[...], held_ref[cols : 2 * cols])
    copies[2].wait()
    total = total + dot(att3_ref[...], held_ref[2 * cols : 3 * cols])
    copies[3].wait()
    copies[4].wait()
    total = total + dot(att2_ref[...], held_ref[3 * cols :])
    copies[5].wait()
    x = own_ref[...].astype(jnp.float32)
    made = []
    for s, sign in enumerate(SIGNS):
        part = x if sign == 0.0 else (x + p if sign > 0 else x - p)
        part = (part + total[s * quarter : (s + 1) * quarter]).astype(jnp.bfloat16)
        out_ref[s] = part
        made.append(part)
    copies[6].wait()
    forced = dot(jnp.concatenate(made, 0), bound_ref[...]).astype(jnp.bfloat16)
    for part in range(forced.shape[1] // 128):
        for s in range(3):
            table_ref[part * quarter : (part + 1) * quarter, s * 128 : (s + 1) * 128] = forced[
                s * quarter : (s + 1) * quarter, part * 128 : (part + 1) * 128
            ]


def combine(code, att, w_outs, x, w_bound):
    quarter = att[0].shape[0] // 3
    shape = (3, quarter, x.shape[1])
    table = (quarter * w_bound.shape[1] // 128, 384)
    far = [in_hbm(a) for a in (*w_outs, x, w_bound)]
    return pl.pallas_call(
        combine_kernel,
        out_shape=[jax.ShapeDtypeStruct(s, jnp.bfloat16) for s in (shape, table)],
        in_specs=[SCALARS]
        + [pl.BlockSpec(a.shape, lambda: (0, 0)) for a in att]
        + [pl.BlockSpec(memory_space=pltpu.HBM)] * len(far),
        out_specs=[pl.BlockSpec(shape, lambda: (0, 0, 0)), ON_CHIP],
        scratch_shapes=[
            pltpu.VMEM((quarter, x.shape[1]), jnp.bfloat16),
            pltpu.VMEM((len(att) * att[0].shape[1], x.shape[1]), jnp.bfloat16),
            pltpu.VMEM(w_bound.shape, jnp.bfloat16),
            pltpu.SemaphoreType.DMA((len(far),)),
        ],
        compiler_params=pltpu.CompilerParams(vmem_limit_bytes=16 * MIB),
        name="combine",
    )(code, *att, *far)


def serve_kernel(asked_ref, table_ref, send_ref):
    pick = pick_rows(asked_ref[...], send_ref.shape[0] * 16, table_ref.shape[0] // 4)
    send_ref[...] = dot(pick, table_ref[...]).astype(jnp.bfloat16).reshape(send_ref.shape)


def serve(asked, table):
    shape = (asked.shape[0], 16, table.shape[1])
    return pl.pallas_call(
        serve_kernel,
        out_shape=jax.ShapeDtypeStruct(shape, jnp.bfloat16),
        in_specs=[ON_CHIP] * 2,
        out_specs=pl.BlockSpec(shape, lambda: (0, 0, 0)),
        compiler_params=pltpu.CompilerParams(vmem_limit_bytes=8 * MIB),
        name="serve",
    )(asked, table)


def inputs_kernel(arrived_ref, band_ref, reg_ref, out_ref, first_ref, last_ref):
    cols, rows, channels = reg_ref.shape
    cells = cols * rows
    slots = arrived_ref.shape[0] * arrived_ref.shape[1]
    table = arrived_ref[...].reshape(slots, 384)
    band_row = cells_row(band_ref[...])
    r, c = iota((cells, cells), 0), iota((cells, cells), 1)
    band_col = jnp.sum(jnp.where(r == c, band_row, 0.0), -1, keepdims=True)
    earlier = (band_col == band_row) & (c < r)
    slot = jnp.sum(jnp.where(earlier, 1.0, 0.0), -1, keepdims=True)
    target = (band_col * 16.0 + slot * 4.0).astype(jnp.int32)
    lane = iota((cells, slots), 1) - target
    for part in range(channels // 128):
        take = jnp.where(lane == part, 1.0, 0.0).astype(jnp.bfloat16)
        taken = dot(take, table)
        lanes = slice(part * 128, (part + 1) * 128)
        reg = reg_ref[:, :, lanes].astype(jnp.float32)
        for s in range(3):
            forced = taken[:, s * 128 : (s + 1) * 128]
            made = (reg + forced.reshape(cols, rows, 128)).astype(jnp.bfloat16)
            out_ref[:, s * rows : (s + 1) * rows, lanes] = made
            first_ref[s * rows : (s + 1) * rows, lanes] = made[0]
            last_ref[s * rows : (s + 1) * rows, lanes] = made[cols - 1]


def make_inputs(arrived, band, reg):
    cols, rows, channels = reg.shape
    shapes = [(cols, 3 * rows, channels), (3 * rows, channels), (3 * rows, channels)]
    return pl.pallas_call(
        inputs_kernel,
        out_shape=[jax.ShapeDtypeStruct(s, jnp.bfloat16) for s in shapes],
        in_specs=[ON_CHIP] * 3,
        out_specs=[ON_CHIP] * 3,
        compiler_params=pltpu.CompilerParams(vmem_limit_bytes=6 * MIB),
        name="inputs",
    )(arrived, band, reg)


def row_shifts(x, rows):
    wide = x.astype(jnp.float32)
    total = x.shape[0]
    row = iota((total, 1), 0) % rows
    low = jnp.where(row > 0, pltpu.roll(wide, 1, 0), 0.0).astype(jnp.bfloat16)
    high = jnp.where(row < rows - 1, pltpu.roll(wide, total - 1, 0), 0.0).astype(jnp.bfloat16)
    return low, x, high


def inner_kernel(x_ref, taps_ref, conv_hbm_ref, sum_ref, after_ref, held_ref, sems):
    copies = [
        pltpu.make_async_copy(
            conv_hbm_ref.at[pl.ds(FETCHED, 6 - FETCHED)], held_ref, sems.at[0]
        ),
        pltpu.make_async_copy(conv_hbm_ref.at[pl.ds(6, 3)], after_ref, sems.at[1]),
    ]
    for copy in copies:
        copy.start()
    cols, slab, channels = x_ref.shape
    cells = cols * slab
    shifts = row_shifts(x_ref[...].reshape(cells, channels), slab // 3)
    sums = [None] * 3
    for tap in range(9):
        if tap == FETCHED:
            copies[0].wait()
        if tap == 6:
            copies[1].wait()
        if tap < FETCHED:
            w = taps_ref[tap]
        elif tap < 6:
            w = held_ref[tap - FETCHED]
        else:
            w = after_ref[tap - 6]
        x = shifts[tap % 3]
        x = (x[: cells - slab], x, x[slab:])[tap // 3]
        one = dot(x, w)
        sums[tap // 3] = one if sums[tap // 3] is None else sums[tap // 3] + one
    before, middle, after = sums
    sum_ref[:slab] = middle[:slab] + after[:slab]
    sum_ref[slab : cells - slab] = middle[slab : cells - slab] + before[: cells - 2 * slab] + after[slab:]
    sum_ref[cells - slab :] = middle[cells - slab :] + before[cells - 2 * slab :]


def convolve_inner(x, taps, conv_w):
    cols, slab, channels = x.shape
    return pl.pallas_call(
        inner_kernel,
        out_shape=[
            jax.ShapeDtypeStruct((cols * slab, channels), jnp.float32),
            jax.ShapeDtypeStruct((3, channels, channels), taps.dtype),
        ],
        in_specs=[ON_CHIP] * 2 + [pl.BlockSpec(memory_space=pltpu.HBM)],
        out_specs=[ON_CHIP] * 2,
        scratch_shapes=[
            pltpu.VMEM((6 - FETCHED, channels, channels), jnp.bfloat16),
            pltpu.SemaphoreType.DMA((2,)),
        ],
        compiler_params=pltpu.CompilerParams(vmem_limit_bytes=16 * MIB),
        name="convolve_inner",
    )(x, taps, conv_w)


def finish_kernel(x_ref, before_ref, after_ref, w_before_ref, w_after_ref, sum_ref, out_ref):
    cols, slab, channels = x_ref.shape
    rows = slab // 3
    sides = []
    for ref, w_ref in ((before_ref, w_before_ref), (after_ref, w_after_ref)):
        total = None
        for b, x in enumerate(row_shifts(ref[...], rows)):
            one = dot(x, w_ref[b])
            total = one if total is None else total + one
        sides.append(total)
    for col in range(cols):
        conv = sum_ref[col * slab : (col + 1) * slab]
        if col == 0:
            conv = conv + sides[0]
        if col == cols - 1:
            conv = conv + sides[1]
        result = x_ref[col].astype(jnp.float32) + conv / (1.0 + jnp.exp(-conv))
        result = result.astype(jnp.bfloat16)
        for s in range(3):
            out_ref[s, col] = result[s * rows : (s + 1) * rows]


def convolve_finish(x, before, after, w_before, w_after, total):
    cols, slab, channels = x.shape
    shape = (3, cols, slab // 3, channels)
    return pl.pallas_call(
        finish_kernel,
        out_shape=jax.ShapeDtypeStruct(shape, jnp.bfloat16),
        in_specs=[ON_CHIP] * 6,
        out_specs=pl.BlockSpec(shape, lambda: (0, 0, 0, 0)),
        compiler_params=pltpu.CompilerParams(vmem_limit_bytes=8 * MIB),
        name="convolve_finish",
    )(x, before, after, w_before, w_after, total)


def neighbours(last, first, axis):
    count = lax.axis_size(axis)
    up = [(i, i + 1) for i in range(count - 1)]
    down = [(j, i) for i, j in up]
    return lax.ppermute(last, axis, up), lax.ppermute(first, axis, down)


def per_device(
    global_state,
    band_codes,
    norm_gain,
    w_query,
    w_key,
    w_value,
    w_out,
    reg_state,
    src_band,
    src_tok,
    w_bound,
    conv_w,
):
    ranks = lax.axis_size("tp")
    bands = lax.axis_size(BANDS)
    tokens, features = global_state.shape
    half = tokens // 2
    gain = in_hbm(norm_gain)
    cell_band = src_band.reshape(src_tok.shape)

    up = [(i, (i + 1) % ranks) for i in range(ranks)]
    down = [(j, i) for i, j in up]
    last, first, *weights = make_edges(
        band_codes, in_hbm(global_state), [in_hbm(w) for w in (w_query, w_key, w_value)]
    )
    before, after = neighbours(last, first, BANDS)
    w1, w3 = lax.ppermute(w_out, "tp", up), lax.ppermute(w_out, "tp", down)
    q, k, v = project(band_codes, [first, last], gain, weights, False)
    asked = ask(cell_band, src_tok, bands)
    q, w1, w3 = lax.optimization_barrier((q, w1, w3))
    middle = w_out.shape[0] // 2
    top, low = lax.ppermute(w1[:middle], "tp", up), lax.ppermute(w3[middle:], "tp", down)
    q, before, after = lax.optimization_barrier((q, before, after))
    k_halo, v_halo = project(band_codes, [before, after], gain, weights[1:], True)
    attended = attend(q, k, v, k_halo, v_halo, ranks, bands)
    attended, asked, top, low = lax.optimization_barrier((attended, asked, top, low))
    attended = [attended[0]] + [
        lax.ppermute(attended[d], "tp", [(i, (i + d) % ranks) for i in range(ranks)])
        for d in range(1, ranks)
    ]
    asked = lax.all_to_all(asked[:, None, :], BANDS, 0, 0, tiled=True)[:, 0, :]
    global_out, table = combine(band_codes, attended, [w_out, w1, w3, top, low], global_state, w_bound)
    send = serve(asked, table)
    conv_w, send = lax.optimization_barrier((conv_w, send))
    conv_w = in_hbm(conv_w)
    taps = fetch_taps(conv_w)
    arrived = lax.all_to_all(send, BANDS, 0, 0, tiled=True)
    taps, arrived = lax.optimization_barrier((taps, arrived))
    inputs, first, last = make_inputs(arrived, cell_band, reg_state)
    before, after = neighbours(last, first, CELLS)
    total, late = convolve_inner(inputs, taps, conv_w)
    return global_out, convolve_finish(inputs, before, after, taps, late, total)


def solution(mesh):
    placed = (
        P(("sec", "tile"), None),
        P(("sec", "tile")),
        P(),
        P(None, "tp"),
        P(None, "tp"),
        P(None, "tp"),
        P("tp", None),
        P(("sec", "tile", "tp"), None, None),
        P(("sec", "tile", "tp"), None, None),
        P(("sec", "tile", "tp"), None),
        P(),
        P(),
    )
    return jax.shard_map(
        per_device,
        mesh=mesh,
        in_specs=placed,
        out_specs=(
            P(None, ("sec", "tile", "tp"), None),
            P(None, ("sec", "tile", "tp"), None, None),
        ),
        check_vma=False,
    )
```

```python
import functools

import jax
import jax.numpy as jnp
from jax import lax
from jax.experimental import pallas as pl
from jax.experimental.pallas import tpu as pltpu
from jax.sharding import PartitionSpec as P

HD = 64
SIGNS = (0.0, 1.0, -1.0)
BANDS = ("sec", "tile")
CELLS = ("sec", "tile", "tp")
LOG2E = 1.4426950408889634
FETCHED = 5
MIB = 1024 * 1024
ON_CHIP = pl.BlockSpec(memory_space=pltpu.VMEM)
SCALARS = pl.BlockSpec(memory_space=pltpu.SMEM)

mix_band = 73856093
mix_token = 19349663
mix_feature = 83492791
mix_again = 668265261


def iota(shape, dim):
    return lax.broadcasted_iota(jnp.int32, shape, dim)


def in_hbm(x):
    return pltpu.with_memory_space_constraint(x, pltpu.HBM)


def dot(a, b):
    return jnp.dot(a, b, preferred_element_type=jnp.float32)


def dot_t(a, b):
    return lax.dot_general(a, b, (((1,), (1,)), ((), ())), preferred_element_type=jnp.float32)


def wiggle(code, first_token, rows, features):
    by_row = code * mix_band + (first_token + iota((rows, 1), 0)) * mix_token
    mixed = by_row + iota((1, features), 1) * mix_feature
    mixed = lax.bitwise_xor(mixed, lax.shift_right_arithmetic(mixed, jnp.full_like(mixed, 15)))
    mixed = mixed * mix_again
    mixed = lax.bitwise_xor(mixed, lax.shift_right_arithmetic(mixed, jnp.full_like(mixed, 13)))
    level = lax.bitwise_and(mixed, 1023).astype(jnp.float32)
    return (level - 511.5) * (0.5 / 295.6)


def edges_kernel(code_ref, x_ref, *refs):
    *refs, flat_ref, sems = refs
    gain_ref, *refs, row_ref = refs
    count = (len(refs) - 2) // 2
    weights, (last_ref, first_ref, *held) = refs[:count], refs[count:]
    half = x_ref.shape[0] // 2
    pairs = [
        (x_ref.at[pl.ds(half, half)], last_ref.at[pl.ds(0, half)]),
        (x_ref.at[pl.ds(0, half)], first_ref.at[pl.ds(0, half)]),
        *zip(weights, held),
        (gain_ref, flat_ref),
    ]
    copies = [pltpu.make_async_copy(a, b, sems.at[i]) for i, (a, b) in enumerate(pairs)]
    for copy in copies:
        copy.start()
    code = jnp.full((16, x_ref.shape[1]), code_ref[0], jnp.int32)
    lane = iota(code.shape, 1)
    shift = jnp.where(lane == 0, 16, jnp.where(lane == 1, 8, 0))
    digit = lax.bitwise_and(lax.shift_right_arithmetic(code, shift), 255)
    digit = digit.astype(jnp.float32).astype(jnp.bfloat16)
    last_ref[half:] = digit
    first_ref[half:] = digit
    for copy in copies:
        copy.wait()
    row_ref[...] = flat_ref[...].astype(jnp.float32).reshape(row_ref.shape)


def make_edges(code, x, gain, weights):
    tokens, features = x.shape
    shapes = [(tokens // 2 + 16, features)] * 2 + [w.shape for w in weights]
    shapes = [jax.ShapeDtypeStruct(s, jnp.bfloat16) for s in shapes]
    shapes.append(jax.ShapeDtypeStruct((1, features), jnp.float32))
    return pl.pallas_call(
        edges_kernel,
        out_shape=shapes,
        in_specs=[SCALARS] + [pl.BlockSpec(memory_space=pltpu.HBM)] * (2 + len(weights)),
        out_specs=[ON_CHIP] * len(shapes),
        scratch_shapes=[
            pltpu.VMEM(gain.shape, gain.dtype),
            pltpu.SemaphoreType.DMA((3 + len(weights),)),
        ],
        compiler_params=pltpu.CompilerParams(vmem_limit_bytes=2 * MIB),
        name="edges",
    )(code, x, gain, *weights)


def project_kernel(code_ref, early_ref, late_ref, gain_ref, *refs, halo):
    *refs, both_ref, inv_ref = refs
    step = pl.program_id(0)
    rows = early_ref.shape[0] - 16
    if halo:
        first = (1 - step) * rows
        digits = jnp.where(
            step == 0, early_ref[rows : rows + 16, 0:128], late_ref[rows : rows + 16, 0:128]
        ).astype(jnp.float32)[0:1]
        lane = iota((1, 128), 1)
        place = jnp.where(lane == 0, 65536.0, jnp.where(lane == 1, 256.0, 1.0))
        code = jnp.sum(jnp.where(lane < 3, digits * place, 0.0), -1, keepdims=True)
        code = code.astype(jnp.int32)
    else:
        first = step * rows
        code = jnp.full((1, 1), code_ref[0], jnp.int32)
    weights, outs = refs[: len(refs) // 2], refs[len(refs) // 2 :]
    features = both_ref.shape[1]
    gain = gain_ref[...]
    chunk, block = 16, 128
    for at in range(0, rows, block):
        for r in range(at, at + block, chunk):
            x = jnp.where(step == 0, early_ref[r : r + chunk], late_ref[r : r + chunk])
            x = x.astype(jnp.float32)
            p = wiggle(code, first + r, chunk, features)
            place = 2 * at + (r - at)
            both_ref[place : place + chunk] = (x * gain).astype(jnp.bfloat16)
            both_ref[place + block : place + block + chunk] = (p * gain).astype(jnp.bfloat16)
            for s, sign in enumerate(SIGNS):
                state = x if sign == 0.0 else (x + p if sign > 0 else x - p)
                mean = jnp.sum(state * state, -1, keepdims=True) * (1.0 / features)
                inv_ref[s, r : r + chunk] = lax.rsqrt(mean + 1e-06)
        here = slice(at, at + block)
        there = pl.ds(pl.multiple_of(step * rows + at, block), block)
        for index, (w_ref, out_ref) in enumerate(zip(weights, outs)):
            scale = HD**-0.5 * LOG2E if (index == 0 and not halo) else 1.0
            made = dot(both_ref[2 * at : 2 * at + 2 * block], w_ref[...])
            base, diff = made[:block], made[block:]
            for s, sign in enumerate(SIGNS):
                full = base if sign == 0.0 else (base + diff if sign > 0 else base - diff)
                out_ref[s, there] = (full * (inv_ref[s, here] * scale)).astype(jnp.bfloat16)


def project(code, arrays, gain, weights, halo):
    features = gain.shape[1]
    cols = weights[0].shape[1]
    tokens = 2 * (arrays[0].shape[0] - 16)
    specs = [ON_CHIP for a in arrays]
    rows = tokens // 2
    return pl.pallas_call(
        functools.partial(project_kernel, halo=halo),
        out_shape=[jax.ShapeDtypeStruct((3, tokens, cols), jnp.bfloat16) for _ in weights],
        grid=(2,),
        in_specs=[SCALARS]
        + specs
        + [ON_CHIP]
        + [ON_CHIP for w in weights],
        out_specs=[ON_CHIP for _ in weights],
        scratch_shapes=[
            pltpu.VMEM((2 * rows, features), jnp.bfloat16),
            pltpu.VMEM((3, rows, 1), jnp.float32),
        ],
        compiler_params=pltpu.CompilerParams(vmem_limit_bytes=12 * MIB),
        name="project_halo" if halo else "project_own",
    )(code, *arrays, gain, *weights)


def attend_kernel(q_ref, k_ref, v_ref, k_halo_ref, v_halo_ref, *refs, bands):
    *out_refs, held_ref = refs
    tokens, cols = q_ref.shape[1:]
    step = pl.program_id(0)
    half = tokens // 2
    band = lax.axis_index(BANDS)
    left = band > 0
    right = band < bands - 1
    k = k_ref[step]
    v = v_ref[step]
    row = iota((tokens, 1), 0)
    there = jnp.where(row < half, left.astype(jnp.int32), right.astype(jnp.int32)) > 0
    k_halo = jnp.where(there, k_halo_ref[step], k)
    one = there.astype(jnp.bfloat16)
    v_halo = v_halo_ref[step] * one
    block, pair = half, 2 * HD
    which = iota((1, pair), 1) // HD
    work = [(head, part) for head in range(cols // HD) for part in range(tokens // block)]

    def lanes(head):
        return slice(head // 2 * pair, (head // 2 + 1) * pair)

    def scores(head, part):
        q = q_ref[step, part * block : (part + 1) * block, lanes(head)]
        q = jnp.where(which == head % 2, q, jnp.zeros_like(q))
        return dot_t(q, k[:, lanes(head)]), dot_t(q, k_halo[:, lanes(head)])

    first = {}
    own, far = scores(*work[0])
    for index, (head, part) in enumerate(work):
        later = scores(*work[index + 1]) if index + 1 < len(work) else (None, None)
        mine = which == head % 2
        top = jnp.maximum(jnp.max(own, -1, keepdims=True), jnp.max(far, -1, keepdims=True))
        own = jnp.exp2(own - top).astype(jnp.bfloat16)
        far = jnp.exp2(far - top).astype(jnp.bfloat16)
        v_own, v_far = v[:, lanes(head)], v_halo[:, lanes(head)]
        v_own = jnp.where(mine, v_own, jnp.ones_like(v_own))
        v_far = jnp.where(mine, v_far, jnp.broadcast_to(one, v_far.shape))
        acc = dot(own, v_own) + dot(far, v_far)
        made = acc / pltpu.roll(acc, HD, 1)
        if head % 2 == 0:
            first[part] = made
        else:
            both = jnp.where(mine, made, first[part]).astype(jnp.bfloat16)
            held_ref[part * block : (part + 1) * block, lanes(head)] = both
        own, far = later
    ranks = len(out_refs)
    quarter = tokens // ranks
    rank = lax.axis_index("tp")
    for distance, out_ref in enumerate(out_refs):
        first = pl.multiple_of(lax.rem(rank + distance, ranks) * quarter, quarter)
        mine = pl.ds(pl.multiple_of(step * quarter, quarter), quarter)
        out_ref[mine, :] = held_ref[pl.ds(first, quarter), :]


def attend(q, k, v, k_halo, v_halo, ranks, bands):
    forwards, tokens, cols = q.shape
    quarter = tokens // ranks
    return pl.pallas_call(
        functools.partial(attend_kernel, bands=bands),
        out_shape=[jax.ShapeDtypeStruct((forwards * quarter, cols), jnp.bfloat16)] * ranks,
        grid=(forwards,),
        in_specs=[ON_CHIP] * 5,
        out_specs=[ON_CHIP] * ranks,
        scratch_shapes=[pltpu.VMEM((tokens, cols), jnp.bfloat16)],
        compiler_params=pltpu.CompilerParams(vmem_limit_bytes=14 * MIB),
        name="attend",
    )(q, k, v, k_halo, v_halo)


def cells_row(x):
    cols, rows = x.shape
    cells = cols * rows
    spread = (iota((rows, cells), 1) % rows == iota((rows, cells), 0)).astype(jnp.float32)
    wide = dot(x.astype(jnp.float32).astype(jnp.bfloat16), spread.astype(jnp.bfloat16))
    mine = iota((cols, cells), 1) // rows == iota((cols, cells), 0)
    return jnp.sum(jnp.where(mine, wide, 0.0), 0, keepdims=True)


def ask_kernel(band_ref, tok_ref, ask_ref):
    bands = ask_ref.shape[0]
    named = cells_row(band_ref[...])
    token = cells_row(tok_ref[...])
    cells = named.shape[1]
    match = (named.astype(jnp.int32) == iota((bands, cells), 0)).astype(jnp.float32)
    before = (iota((cells, cells), 0) < iota((cells, cells), 1)).astype(jnp.float32)
    slot = dot(match.astype(jnp.bfloat16), before.astype(jnp.bfloat16))
    lanes = iota((bands, cells), 1)
    asked = jnp.zeros((bands, cells), jnp.float32)
    for s in range(4):
        hit = jnp.where(slot == s, match, 0.0)
        token_s = jnp.sum(hit * (token + 1.0), -1, keepdims=True) - 1.0
        asked = jnp.where(lanes == s, token_s, asked)
    ask_ref[...] = asked[:, :4].astype(jnp.int32)


def ask(band, tok, bands):
    return pl.pallas_call(
        ask_kernel,
        out_shape=jax.ShapeDtypeStruct((bands, 4), jnp.int32),
        in_specs=[ON_CHIP] * 2,
        out_specs=ON_CHIP,
        compiler_params=pltpu.CompilerParams(vmem_limit_bytes=4 * MIB),
        name="ask",
    )(band, tok)


def fetch_kernel(conv_hbm_ref, taps_ref, sem):
    copy = pltpu.make_async_copy(conv_hbm_ref.at[pl.ds(0, FETCHED)], taps_ref, sem)
    copy.start()
    copy.wait()


def fetch_taps(conv_w):
    return pl.pallas_call(
        fetch_kernel,
        out_shape=jax.ShapeDtypeStruct((FETCHED, *conv_w.shape[1:]), conv_w.dtype),
        in_specs=[pl.BlockSpec(memory_space=pltpu.HBM)],
        out_specs=ON_CHIP,
        scratch_shapes=[pltpu.SemaphoreType.DMA(())],
        compiler_params=pltpu.CompilerParams(vmem_limit_bytes=2 * MIB),
        name="fetch",
    )(conv_w)


def pick_rows(asked, rows, cells):
    bands = asked.shape[0]
    spread = (iota((rows, bands), 0) // 16 == iota((rows, bands), 1)).astype(jnp.float32)
    per_row = dot(spread.astype(jnp.bfloat16), asked.astype(jnp.float32).astype(jnp.bfloat16))
    r = iota((rows, 1), 0)
    mine = iota((rows, 4), 1) == (r // 4) % 4
    token_r = jnp.sum(jnp.where(mine, per_row, 0.0), -1, keepdims=True).astype(jnp.int32)
    target = jnp.where(token_r >= 0, (r % 4) * cells + token_r, -1)
    return (iota((rows, 4 * cells), 1) == target).astype(jnp.float32).astype(jnp.bfloat16)


def combine_kernel(code_ref, att0_ref, att1_ref, att2_ref, att3_ref, w0_ref, w1_ref, w3_ref, top_ref, low_ref, x_ref, w_bound_ref, out_ref, table_ref, own_ref, held_ref, bound_ref, sems):
    cols = att0_ref.shape[1]
    half = cols // 2
    features = x_ref.shape[1]
    quarter = out_ref.shape[1]
    rank = lax.axis_index("tp")
    rows = pl.ds(pl.multiple_of(rank * quarter, quarter), quarter)
    pairs = [
        (w0_ref, held_ref.at[pl.ds(0, cols)]),
        (w1_ref, held_ref.at[pl.ds(cols, cols)]),
        (w3_ref, held_ref.at[pl.ds(2 * cols, cols)]),
        (top_ref, held_ref.at[pl.ds(3 * cols, half)]),
        (low_ref, held_ref.at[pl.ds(3 * cols + half, half)]),
        (x_ref.at[rows], own_ref),
        (w_bound_ref, bound_ref),
    ]
    copies = [pltpu.make_async_copy(a, b, sems.at[i]) for i, (a, b) in enumerate(pairs)]
    for copy in copies:
        copy.start()
    code = jnp.full((1, 1), code_ref[0], jnp.int32)
    p = wiggle(code, rank * quarter, quarter, features)
    copies[0].wait()
    total = dot(att0_ref[...], held_ref[:cols])
    copies[1].wait()
    total = total + dot(att1_ref[...], held_ref[cols : 2 * cols])
    copies[2].wait()
    total = total + dot(att3_ref[...], held_ref[2 * cols : 3 * cols])
    copies[3].wait()
    copies[4].wait()
    total = total + dot(att2_ref[...], held_ref[3 * cols :])
    copies[5].wait()
    x = own_ref[...].astype(jnp.float32)
    made = []
    for s, sign in enumerate(SIGNS):
        part = x if sign == 0.0 else (x + p if sign > 0 else x - p)
        part = (part + total[s * quarter : (s + 1) * quarter]).astype(jnp.bfloat16)
        out_ref[s] = part
        made.append(part)
    copies[6].wait()
    forced = dot(jnp.concatenate(made, 0), bound_ref[...]).astype(jnp.bfloat16)
    for part in range(forced.shape[1] // 128):
        for s in range(3):
            table_ref[part * quarter : (part + 1) * quarter, s * 128 : (s + 1) * 128] = forced[
                s * quarter : (s + 1) * quarter, part * 128 : (part + 1) * 128
            ]


def combine(code, att, w_outs, x, w_bound):
    quarter = att[0].shape[0] // 3
    shape = (3, quarter, x.shape[1])
    table = (quarter * w_bound.shape[1] // 128, 384)
    far = [in_hbm(a) for a in (*w_outs, x, w_bound)]
    return pl.pallas_call(
        combine_kernel,
        out_shape=[jax.ShapeDtypeStruct(s, jnp.bfloat16) for s in (shape, table)],
        in_specs=[SCALARS]
        + [ON_CHIP for a in att]
        + [pl.BlockSpec(memory_space=pltpu.HBM)] * len(far),
        out_specs=[pl.BlockSpec(shape, lambda: (0, 0, 0)), ON_CHIP],
        scratch_shapes=[
            pltpu.VMEM((quarter, x.shape[1]), jnp.bfloat16),
            pltpu.VMEM((len(att) * att[0].shape[1], x.shape[1]), jnp.bfloat16),
            pltpu.VMEM(w_bound.shape, jnp.bfloat16),
            pltpu.SemaphoreType.DMA((len(far),)),
        ],
        compiler_params=pltpu.CompilerParams(vmem_limit_bytes=16 * MIB),
        name="combine",
    )(code, *att, *far)


def serve_kernel(asked_ref, table_ref, send_ref):
    pick = pick_rows(asked_ref[...], send_ref.shape[0] * 16, table_ref.shape[0] // 4)
    send_ref[...] = dot(pick, table_ref[...]).astype(jnp.bfloat16).reshape(send_ref.shape)


def serve(asked, table):
    shape = (asked.shape[0], 16, table.shape[1])
    return pl.pallas_call(
        serve_kernel,
        out_shape=jax.ShapeDtypeStruct(shape, jnp.bfloat16),
        in_specs=[ON_CHIP] * 2,
        out_specs=pl.BlockSpec(shape, lambda: (0, 0, 0)),
        compiler_params=pltpu.CompilerParams(vmem_limit_bytes=8 * MIB),
        name="serve",
    )(asked, table)


def inputs_kernel(arrived_ref, band_ref, reg_ref, out_ref, first_ref, last_ref):
    cols, rows, channels = reg_ref.shape
    cells = cols * rows
    slots = arrived_ref.shape[0] * arrived_ref.shape[1]
    table = arrived_ref[...].reshape(slots, 384)
    band_row = cells_row(band_ref[...])
    r, c = iota((cells, cells), 0), iota((cells, cells), 1)
    band_col = jnp.sum(jnp.where(r == c, band_row, 0.0), -1, keepdims=True)
    earlier = (band_col == band_row) & (c < r)
    slot = jnp.sum(jnp.where(earlier, 1.0, 0.0), -1, keepdims=True)
    target = (band_col * 16.0 + slot * 4.0).astype(jnp.int32)
    lane = iota((cells, slots), 1) - target
    for part in range(channels // 128):
        take = jnp.where(lane == part, 1.0, 0.0).astype(jnp.bfloat16)
        taken = dot(take, table)
        lanes = slice(part * 128, (part + 1) * 128)
        reg = reg_ref[:, :, lanes].astype(jnp.float32)
        for s in range(3):
            forced = taken[:, s * 128 : (s + 1) * 128]
            made = (reg + forced.reshape(cols, rows, 128)).astype(jnp.bfloat16)
            out_ref[:, s * rows : (s + 1) * rows, lanes] = made
            first_ref[s * rows : (s + 1) * rows, lanes] = made[0]
            last_ref[s * rows : (s + 1) * rows, lanes] = made[cols - 1]


def make_inputs(arrived, band, reg):
    cols, rows, channels = reg.shape
    shapes = [(cols, 3 * rows, channels), (3 * rows, channels), (3 * rows, channels)]
    return pl.pallas_call(
        inputs_kernel,
        out_shape=[jax.ShapeDtypeStruct(s, jnp.bfloat16) for s in shapes],
        in_specs=[ON_CHIP] * 3,
        out_specs=[ON_CHIP] * 3,
        compiler_params=pltpu.CompilerParams(vmem_limit_bytes=6 * MIB),
        name="inputs",
    )(arrived, band, reg)


def row_shifts(x, rows):
    wide = x.astype(jnp.float32)
    total = x.shape[0]
    row = iota((total, 1), 0) % rows
    low = jnp.where(row > 0, pltpu.roll(wide, 1, 0), 0.0).astype(jnp.bfloat16)
    high = jnp.where(row < rows - 1, pltpu.roll(wide, total - 1, 0), 0.0).astype(jnp.bfloat16)
    return low, x, high


def inner_kernel(x_ref, taps_ref, conv_hbm_ref, sum_ref, after_ref, held_ref, sems):
    copies = [
        pltpu.make_async_copy(
            conv_hbm_ref.at[pl.ds(FETCHED, 6 - FETCHED)], held_ref, sems.at[0]
        ),
        pltpu.make_async_copy(conv_hbm_ref.at[pl.ds(6, 3)], after_ref, sems.at[1]),
    ]
    for copy in copies:
        copy.start()
    cols, slab, channels = x_ref.shape
    cells = cols * slab
    shifts = row_shifts(x_ref[...].reshape(cells, channels), slab // 3)
    sums = [None] * 3
    for tap in range(9):
        if tap == FETCHED:
            copies[0].wait()
        if tap == 6:
            copies[1].wait()
        if tap < FETCHED:
            w = taps_ref[tap]
        elif tap < 6:
            w = held_ref[tap - FETCHED]
        else:
            w = after_ref[tap - 6]
        x = shifts[tap % 3]
        x = (x[: cells - slab], x, x[slab:])[tap // 3]
        one = dot(x, w)
        sums[tap // 3] = one if sums[tap // 3] is None else sums[tap // 3] + one
    before, middle, after = sums
    sum_ref[:slab] = middle[:slab] + after[:slab]
    sum_ref[slab : cells - slab] = middle[slab : cells - slab] + before[: cells - 2 * slab] + after[slab:]
    sum_ref[cells - slab :] = middle[cells - slab :] + before[cells - 2 * slab :]


def convolve_inner(x, taps, conv_w):
    cols, slab, channels = x.shape
    return pl.pallas_call(
        inner_kernel,
        out_shape=[
            jax.ShapeDtypeStruct((cols * slab, channels), jnp.float32),
            jax.ShapeDtypeStruct((3, channels, channels), taps.dtype),
        ],
        in_specs=[ON_CHIP] * 2 + [pl.BlockSpec(memory_space=pltpu.HBM)],
        out_specs=[ON_CHIP] * 2,
        scratch_shapes=[
            pltpu.VMEM((6 - FETCHED, channels, channels), jnp.bfloat16),
            pltpu.SemaphoreType.DMA((2,)),
        ],
        compiler_params=pltpu.CompilerParams(vmem_limit_bytes=16 * MIB),
        name="convolve_inner",
    )(x, taps, conv_w)


def finish_kernel(x_ref, before_ref, after_ref, w_before_ref, w_after_ref, sum_ref, out_ref):
    cols, slab, channels = x_ref.shape
    rows = slab // 3
    sides = []
    for ref, w_ref in ((before_ref, w_before_ref), (after_ref, w_after_ref)):
        total = None
        for b, x in enumerate(row_shifts(ref[...], rows)):
            one = dot(x, w_ref[b])
            total = one if total is None else total + one
        sides.append(total)
    for col in range(cols):
        conv = sum_ref[col * slab : (col + 1) * slab]
        if col == 0:
            conv = conv + sides[0]
        if col == cols - 1:
            conv = conv + sides[1]
        result = x_ref[col].astype(jnp.float32) + conv / (1.0 + jnp.exp(-conv))
        result = result.astype(jnp.bfloat16)
        for s in range(3):
            out_ref[s, col] = result[s * rows : (s + 1) * rows]


def convolve_finish(x, before, after, w_before, w_after, total):
    cols, slab, channels = x.shape
    shape = (3, cols, slab // 3, channels)
    return pl.pallas_call(
        finish_kernel,
        out_shape=jax.ShapeDtypeStruct(shape, jnp.bfloat16),
        in_specs=[ON_CHIP] * 6,
        out_specs=pl.BlockSpec(shape, lambda: (0, 0, 0, 0)),
        compiler_params=pltpu.CompilerParams(vmem_limit_bytes=8 * MIB),
        name="convolve_finish",
    )(x, before, after, w_before, w_after, total)


def neighbours(last, first, axis):
    count = lax.axis_size(axis)
    up = [(i, i + 1) for i in range(count - 1)]
    down = [(j, i) for i, j in up]
    return lax.ppermute(last, axis, up), lax.ppermute(first, axis, down)


def per_device(
    global_state,
    band_codes,
    norm_gain,
    w_query,
    w_key,
    w_value,
    w_out,
    reg_state,
    src_band,
    src_tok,
    w_bound,
    conv_w,
):
    ranks = lax.axis_size("tp")
    bands = lax.axis_size(BANDS)
    tokens, features = global_state.shape
    half = tokens // 2
    cell_band = src_band.reshape(src_tok.shape)

    up = [(i, (i + 1) % ranks) for i in range(ranks)]
    down = [(j, i) for i, j in up]
    last, first, *weights, gain = make_edges(
        band_codes, in_hbm(global_state), in_hbm(norm_gain), [in_hbm(w) for w in (w_query, w_key, w_value)]
    )
    before, after = neighbours(last, first, BANDS)
    w1, w3 = lax.ppermute(w_out, "tp", up), lax.ppermute(w_out, "tp", down)
    q, k, v = project(band_codes, [first, last], gain, weights, False)
    asked = ask(cell_band, src_tok, bands)
    q, w1, w3 = lax.optimization_barrier((q, w1, w3))
    middle = w_out.shape[0] // 2
    top, low = lax.ppermute(w1[:middle], "tp", up), lax.ppermute(w3[middle:], "tp", down)
    q, before, after = lax.optimization_barrier((q, before, after))
    k_halo, v_halo = project(band_codes, [before, after], gain, weights[1:], True)
    attended = attend(q, k, v, k_halo, v_halo, ranks, bands)
    attended, asked, top, low = lax.optimization_barrier((attended, asked, top, low))
    attended = [attended[0]] + [
        lax.ppermute(attended[d], "tp", [(i, (i + d) % ranks) for i in range(ranks)])
        for d in range(1, ranks)
    ]
    asked = lax.all_to_all(asked[:, None, :], BANDS, 0, 0, tiled=True)[:, 0, :]
    global_out, table = combine(band_codes, attended, [w_out, w1, w3, top, low], global_state, w_bound)
    send = serve(asked, table)
    conv_w, send = lax.optimization_barrier((conv_w, send))
    conv_w = in_hbm(conv_w)
    taps = fetch_taps(conv_w)
    arrived = lax.all_to_all(send, BANDS, 0, 0, tiled=True)
    taps, arrived = lax.optimization_barrier((taps, arrived))
    inputs, first, last = make_inputs(arrived, cell_band, reg_state)
    before, after = neighbours(last, first, CELLS)
    total, late = convolve_inner(inputs, taps, conv_w)
    return global_out, convolve_finish(inputs, before, after, taps, late, total)


def solution(mesh):
    placed = (
        P(("sec", "tile"), None),
        P(("sec", "tile")),
        P(),
        P(None, "tp"),
        P(None, "tp"),
        P(None, "tp"),
        P("tp", None),
        P(("sec", "tile", "tp"), None, None),
        P(("sec", "tile", "tp"), None, None),
        P(("sec", "tile", "tp"), None),
        P(),
        P(),
    )
    return jax.shard_map(
        per_device,
        mesh=mesh,
        in_specs=placed,
        out_specs=(
            P(None, ("sec", "tile", "tp"), None),
            P(None, ("sec", "tile", "tp"), None, None),
        ),
        check_vma=False,
    )
```

```python
import functools

import jax
import jax.numpy as jnp
from jax import lax
from jax.experimental import pallas as pl
from jax.experimental.pallas import tpu as pltpu
from jax.sharding import PartitionSpec as P

HD = 64
SIGNS = (0.0, 1.0, -1.0)
BANDS = ("sec", "tile")
CELLS = ("sec", "tile", "tp")
LOG2E = 1.4426950408889634
FETCHED = 5
MIB = 1024 * 1024
ON_CHIP = pl.BlockSpec(memory_space=pltpu.VMEM)
SCALARS = pl.BlockSpec(memory_space=pltpu.SMEM)

mix_band = 73856093
mix_token = 19349663
mix_feature = 83492791
mix_again = 668265261


def iota(shape, dim):
    return lax.broadcasted_iota(jnp.int32, shape, dim)


def in_hbm(x):
    return pltpu.with_memory_space_constraint(x, pltpu.HBM)


def dot(a, b):
    return jnp.dot(a, b, preferred_element_type=jnp.float32)


def dot_t(a, b):
    return lax.dot_general(a, b, (((1,), (1,)), ((), ())), preferred_element_type=jnp.float32)


def wiggle(code, first_token, rows, features):
    by_row = code * mix_band + (first_token + iota((rows, 1), 0)) * mix_token
    mixed = by_row + iota((1, features), 1) * mix_feature
    mixed = lax.bitwise_xor(mixed, lax.shift_right_arithmetic(mixed, jnp.full_like(mixed, 15)))
    mixed = mixed * mix_again
    mixed = lax.bitwise_xor(mixed, lax.shift_right_arithmetic(mixed, jnp.full_like(mixed, 13)))
    level = lax.bitwise_and(mixed, 1023).astype(jnp.float32)
    return (level - 511.5) * (0.5 / 295.6)


def edges_kernel(code_ref, x_ref, last_ref, first_ref, sems):
    half = x_ref.shape[0] // 2
    copies = [
        pltpu.make_async_copy(x_ref.at[pl.ds(half, half)], last_ref.at[pl.ds(0, half)], sems.at[0]),
        pltpu.make_async_copy(x_ref.at[pl.ds(0, half)], first_ref.at[pl.ds(0, half)], sems.at[1]),
    ]
    for copy in copies:
        copy.start()
    code = jnp.full((16, x_ref.shape[1]), code_ref[0], jnp.int32)
    lane = iota(code.shape, 1)
    shift = jnp.where(lane == 0, 16, jnp.where(lane == 1, 8, 0))
    digit = lax.bitwise_and(lax.shift_right_arithmetic(code, shift), 255)
    digit = digit.astype(jnp.float32).astype(jnp.bfloat16)
    last_ref[half:] = digit
    first_ref[half:] = digit
    for copy in copies:
        copy.wait()


def make_edges(code, x):
    tokens, features = x.shape
    shape = jax.ShapeDtypeStruct((tokens // 2 + 16, features), jnp.bfloat16)
    return pl.pallas_call(
        edges_kernel,
        out_shape=[shape, shape],
        in_specs=[SCALARS, pl.BlockSpec(memory_space=pltpu.HBM)],
        out_specs=[ON_CHIP] * 2,
        scratch_shapes=[pltpu.SemaphoreType.DMA((2,))],
        compiler_params=pltpu.CompilerParams(vmem_limit_bytes=2 * MIB),
        name="edges",
    )(code, x)


def load_kernel(gain_ref, *refs):
    *refs, row_ref, flat_ref, sems = refs
    count = len(refs) // 2
    pairs = [*zip(refs[:count], refs[count:]), (gain_ref, flat_ref)]
    copies = [pltpu.make_async_copy(a, b, sems.at[i]) for i, (a, b) in enumerate(pairs)]
    for copy in copies:
        copy.start()
    for copy in copies:
        copy.wait()
    row_ref[...] = flat_ref[...].astype(jnp.float32).reshape(row_ref.shape)


def load(gain, weights):
    shapes = [jax.ShapeDtypeStruct(w.shape, w.dtype) for w in weights]
    shapes.append(jax.ShapeDtypeStruct((1, gain.shape[0]), jnp.float32))
    count = len(weights) + 1
    return pl.pallas_call(
        load_kernel,
        out_shape=shapes,
        in_specs=[pl.BlockSpec(memory_space=pltpu.HBM)] * count,
        out_specs=[ON_CHIP] * count,
        scratch_shapes=[pltpu.VMEM(gain.shape, gain.dtype), pltpu.SemaphoreType.DMA((count,))],
        compiler_params=pltpu.CompilerParams(vmem_limit_bytes=2 * MIB),
        name="load",
    )(gain, *weights)


def project_kernel(code_ref, early_ref, late_ref, gain_ref, *refs, halo):
    *refs, both_ref, inv_ref = refs
    step = pl.program_id(0)
    rows = early_ref.shape[0] - 16
    if halo:
        first = (1 - step) * rows
        digits = jnp.where(
            step == 0, early_ref[rows : rows + 16, 0:128], late_ref[rows : rows + 16, 0:128]
        ).astype(jnp.float32)[0:1]
        lane = iota((1, 128), 1)
        place = jnp.where(lane == 0, 65536.0, jnp.where(lane == 1, 256.0, 1.0))
        code = jnp.sum(jnp.where(lane < 3, digits * place, 0.0), -1, keepdims=True)
        code = code.astype(jnp.int32)
    else:
        first = step * rows
        code = jnp.full((1, 1), code_ref[0], jnp.int32)
    weights, outs = refs[: len(refs) // 2], refs[len(refs) // 2 :]
    features = both_ref.shape[1]
    gain = gain_ref[...]
    chunk, block = 16, 128
    for at in range(0, rows, block):
        for r in range(at, at + block, chunk):
            x = jnp.where(step == 0, early_ref[r : r + chunk], late_ref[r : r + chunk])
            x = x.astype(jnp.float32)
            p = wiggle(code, first + r, chunk, features)
            place = 2 * at + (r - at)
            both_ref[place : place + chunk] = (x * gain).astype(jnp.bfloat16)
            both_ref[place + block : place + block + chunk] = (p * gain).astype(jnp.bfloat16)
            for s, sign in enumerate(SIGNS):
                state = x if sign == 0.0 else (x + p if sign > 0 else x - p)
                mean = jnp.sum(state * state, -1, keepdims=True) * (1.0 / features)
                inv_ref[s, r : r + chunk] = lax.rsqrt(mean + 1e-06)
        here = slice(at, at + block)
        there = pl.ds(pl.multiple_of(step * rows + at, block), block)
        for index, (w_ref, out_ref) in enumerate(zip(weights, outs)):
            scale = HD**-0.5 * LOG2E if (index == 0 and not halo) else 1.0
            made = dot(both_ref[2 * at : 2 * at + 2 * block], w_ref[...])
            base, diff = made[:block], made[block:]
            for s, sign in enumerate(SIGNS):
                full = base if sign == 0.0 else (base + diff if sign > 0 else base - diff)
                out_ref[s, there] = (full * (inv_ref[s, here] * scale)).astype(jnp.bfloat16)


def project(code, arrays, gain, weights, halo):
    features = gain.shape[1]
    cols = weights[0].shape[1]
    tokens = 2 * (arrays[0].shape[0] - 16)
    specs = [ON_CHIP for a in arrays]
    rows = tokens // 2
    return pl.pallas_call(
        functools.partial(project_kernel, halo=halo),
        out_shape=[jax.ShapeDtypeStruct((3, tokens, cols), jnp.bfloat16) for _ in weights],
        grid=(2,),
        in_specs=[SCALARS]
        + specs
        + [ON_CHIP]
        + [ON_CHIP for w in weights],
        out_specs=[ON_CHIP for _ in weights],
        scratch_shapes=[
            pltpu.VMEM((2 * rows, features), jnp.bfloat16),
            pltpu.VMEM((3, rows, 1), jnp.float32),
        ],
        compiler_params=pltpu.CompilerParams(vmem_limit_bytes=12 * MIB),
        name="project_halo" if halo else "project_own",
    )(code, *arrays, gain, *weights)


def attend_kernel(q_ref, k_ref, v_ref, k_halo_ref, v_halo_ref, *refs, bands):
    *out_refs, held_ref = refs
    tokens, cols = q_ref.shape[1:]
    step = pl.program_id(0)
    half = tokens // 2
    band = lax.axis_index(BANDS)
    left = band > 0
    right = band < bands - 1
    k = k_ref[step]
    v = v_ref[step]
    row = iota((tokens, 1), 0)
    there = jnp.where(row < half, left.astype(jnp.int32), right.astype(jnp.int32)) > 0
    k_halo = jnp.where(there, k_halo_ref[step], k)
    one = there.astype(jnp.bfloat16)
    v_halo = v_halo_ref[step] * one
    block, pair = half, 2 * HD
    which = iota((1, pair), 1) // HD
    work = [(head, part) for head in range(cols // HD) for part in range(tokens // block)]

    def lanes(head):
        return slice(head // 2 * pair, (head // 2 + 1) * pair)

    def scores(head, part):
        q = q_ref[step, part * block : (part + 1) * block, lanes(head)]
        q = jnp.where(which == head % 2, q, jnp.zeros_like(q))
        return dot_t(q, k[:, lanes(head)]), dot_t(q, k_halo[:, lanes(head)])

    first = {}
    own, far = scores(*work[0])
    for index, (head, part) in enumerate(work):
        later = scores(*work[index + 1]) if index + 1 < len(work) else (None, None)
        mine = which == head % 2
        top = jnp.maximum(jnp.max(own, -1, keepdims=True), jnp.max(far, -1, keepdims=True))
        own = jnp.exp2(own - top).astype(jnp.bfloat16)
        far = jnp.exp2(far - top).astype(jnp.bfloat16)
        v_own, v_far = v[:, lanes(head)], v_halo[:, lanes(head)]
        v_own = jnp.where(mine, v_own, jnp.ones_like(v_own))
        v_far = jnp.where(mine, v_far, jnp.broadcast_to(one, v_far.shape))
        acc = dot(own, v_own) + dot(far, v_far)
        made = acc / pltpu.roll(acc, HD, 1)
        if head % 2 == 0:
            first[part] = made
        else:
            both = jnp.where(mine, made, first[part]).astype(jnp.bfloat16)
            held_ref[part * block : (part + 1) * block, lanes(head)] = both
        own, far = later
    ranks = len(out_refs)
    quarter = tokens // ranks
    rank = lax.axis_index("tp")
    for distance, out_ref in enumerate(out_refs):
        first = pl.multiple_of(lax.rem(rank + distance, ranks) * quarter, quarter)
        mine = pl.ds(pl.multiple_of(step * quarter, quarter), quarter)
        out_ref[mine, :] = held_ref[pl.ds(first, quarter), :]


def attend(q, k, v, k_halo, v_halo, ranks, bands):
    forwards, tokens, cols = q.shape
    quarter = tokens // ranks
    return pl.pallas_call(
        functools.partial(attend_kernel, bands=bands),
        out_shape=[jax.ShapeDtypeStruct((forwards * quarter, cols), jnp.bfloat16)] * ranks,
        grid=(forwards,),
        in_specs=[ON_CHIP] * 5,
        out_specs=[ON_CHIP] * ranks,
        scratch_shapes=[pltpu.VMEM((tokens, cols), jnp.bfloat16)],
        compiler_params=pltpu.CompilerParams(vmem_limit_bytes=14 * MIB),
        name="attend",
    )(q, k, v, k_halo, v_halo)


def cells_row(x):
    cols, rows = x.shape
    cells = cols * rows
    spread = (iota((rows, cells), 1) % rows == iota((rows, cells), 0)).astype(jnp.float32)
    wide = dot(x.astype(jnp.float32).astype(jnp.bfloat16), spread.astype(jnp.bfloat16))
    mine = iota((cols, cells), 1) // rows == iota((cols, cells), 0)
    return jnp.sum(jnp.where(mine, wide, 0.0), 0, keepdims=True)


def ask_kernel(band_ref, tok_ref, ask_ref):
    bands = ask_ref.shape[0]
    named = cells_row(band_ref[...])
    token = cells_row(tok_ref[...])
    cells = named.shape[1]
    match = (named.astype(jnp.int32) == iota((bands, cells), 0)).astype(jnp.float32)
    before = (iota((cells, cells), 0) < iota((cells, cells), 1)).astype(jnp.float32)
    slot = dot(match.astype(jnp.bfloat16), before.astype(jnp.bfloat16))
    lanes = iota((bands, cells), 1)
    asked = jnp.zeros((bands, cells), jnp.float32)
    for s in range(4):
        hit = jnp.where(slot == s, match, 0.0)
        token_s = jnp.sum(hit * (token + 1.0), -1, keepdims=True) - 1.0
        asked = jnp.where(lanes == s, token_s, asked)
    ask_ref[...] = asked[:, :4].astype(jnp.int32)


def ask(band, tok, bands):
    return pl.pallas_call(
        ask_kernel,
        out_shape=jax.ShapeDtypeStruct((bands, 4), jnp.int32),
        in_specs=[ON_CHIP] * 2,
        out_specs=ON_CHIP,
        compiler_params=pltpu.CompilerParams(vmem_limit_bytes=4 * MIB),
        name="ask",
    )(band, tok)


def fetch_kernel(conv_hbm_ref, taps_ref, sem):
    copy = pltpu.make_async_copy(conv_hbm_ref.at[pl.ds(0, FETCHED)], taps_ref, sem)
    copy.start()
    copy.wait()


def fetch_taps(conv_w):
    return pl.pallas_call(
        fetch_kernel,
        out_shape=jax.ShapeDtypeStruct((FETCHED, *conv_w.shape[1:]), conv_w.dtype),
        in_specs=[pl.BlockSpec(memory_space=pltpu.HBM)],
        out_specs=ON_CHIP,
        scratch_shapes=[pltpu.SemaphoreType.DMA(())],
        compiler_params=pltpu.CompilerParams(vmem_limit_bytes=2 * MIB),
        name="fetch",
    )(conv_w)


def pick_rows(asked, rows, cells):
    bands = asked.shape[0]
    spread = (iota((rows, bands), 0) // 16 == iota((rows, bands), 1)).astype(jnp.float32)
    per_row = dot(spread.astype(jnp.bfloat16), asked.astype(jnp.float32).astype(jnp.bfloat16))
    r = iota((rows, 1), 0)
    mine = iota((rows, 4), 1) == (r // 4) % 4
    token_r = jnp.sum(jnp.where(mine, per_row, 0.0), -1, keepdims=True).astype(jnp.int32)
    target = jnp.where(token_r >= 0, (r % 4) * cells + token_r, -1)
    return (iota((rows, 4 * cells), 1) == target).astype(jnp.float32).astype(jnp.bfloat16)


def combine_kernel(code_ref, att0_ref, att1_ref, att2_ref, att3_ref, w0_ref, w1_ref, w3_ref, top_ref, low_ref, x_ref, w_bound_ref, out_ref, table_ref, own_ref, held_ref, bound_ref, sems):
    cols = att0_ref.shape[1]
    half = cols // 2
    features = x_ref.shape[1]
    quarter = out_ref.shape[1]
    rank = lax.axis_index("tp")
    rows = pl.ds(pl.multiple_of(rank * quarter, quarter), quarter)
    pairs = [
        (w0_ref, held_ref.at[pl.ds(0, cols)]),
        (w1_ref, held_ref.at[pl.ds(cols, cols)]),
        (w3_ref, held_ref.at[pl.ds(2 * cols, cols)]),
        (top_ref, held_ref.at[pl.ds(3 * cols, half)]),
        (low_ref, held_ref.at[pl.ds(3 * cols + half, half)]),
        (x_ref.at[rows], own_ref),
        (w_bound_ref, bound_ref),
    ]
    copies = [pltpu.make_async_copy(a, b, sems.at[i]) for i, (a, b) in enumerate(pairs)]
    for copy in copies:
        copy.start()
    code = jnp.full((1, 1), code_ref[0], jnp.int32)
    p = wiggle(code, rank * quarter, quarter, features)
    copies[0].wait()
    total = dot(att0_ref[...], held_ref[:cols])
    copies[1].wait()
    total = total + dot(att1_ref[...], held_ref[cols : 2 * cols])
    copies[2].wait()
    total = total + dot(att3_ref[...], held_ref[2 * cols : 3 * cols])
    copies[3].wait()
    copies[4].wait()
    total = total + dot(att2_ref[...], held_ref[3 * cols :])
    copies[5].wait()
    x = own_ref[...].astype(jnp.float32)
    made = []
    for s, sign in enumerate(SIGNS):
        part = x if sign == 0.0 else (x + p if sign > 0 else x - p)
        part = (part + total[s * quarter : (s + 1) * quarter]).astype(jnp.bfloat16)
        out_ref[s] = part
        made.append(part)
    copies[6].wait()
    forced = dot(jnp.concatenate(made, 0), bound_ref[...]).astype(jnp.bfloat16)
    for part in range(forced.shape[1] // 128):
        for s in range(3):
            table_ref[part * quarter : (part + 1) * quarter, s * 128 : (s + 1) * 128] = forced[
                s * quarter : (s + 1) * quarter, part * 128 : (part + 1) * 128
            ]


def combine(code, att, w_outs, x, w_bound):
    quarter = att[0].shape[0] // 3
    shape = (3, quarter, x.shape[1])
    table = (quarter * w_bound.shape[1] // 128, 384)
    far = [in_hbm(a) for a in (*w_outs, x, w_bound)]
    return pl.pallas_call(
        combine_kernel,
        out_shape=[jax.ShapeDtypeStruct(s, jnp.bfloat16) for s in (shape, table)],
        in_specs=[SCALARS]
        + [ON_CHIP for a in att]
        + [pl.BlockSpec(memory_space=pltpu.HBM)] * len(far),
        out_specs=[pl.BlockSpec(shape, lambda: (0, 0, 0)), ON_CHIP],
        scratch_shapes=[
            pltpu.VMEM((quarter, x.shape[1]), jnp.bfloat16),
            pltpu.VMEM((len(att) * att[0].shape[1], x.shape[1]), jnp.bfloat16),
            pltpu.VMEM(w_bound.shape, jnp.bfloat16),
            pltpu.SemaphoreType.DMA((len(far),)),
        ],
        compiler_params=pltpu.CompilerParams(vmem_limit_bytes=16 * MIB),
        name="combine",
    )(code, *att, *far)


def serve_kernel(asked_ref, table_ref, send_ref):
    pick = pick_rows(asked_ref[...], send_ref.shape[0] * 16, table_ref.shape[0] // 4)
    send_ref[...] = dot(pick, table_ref[...]).astype(jnp.bfloat16).reshape(send_ref.shape)


def serve(asked, table):
    shape = (asked.shape[0], 16, table.shape[1])
    return pl.pallas_call(
        serve_kernel,
        out_shape=jax.ShapeDtypeStruct(shape, jnp.bfloat16),
        in_specs=[ON_CHIP] * 2,
        out_specs=pl.BlockSpec(shape, lambda: (0, 0, 0)),
        compiler_params=pltpu.CompilerParams(vmem_limit_bytes=8 * MIB),
        name="serve",
    )(asked, table)


def inputs_kernel(arrived_ref, band_ref, reg_ref, out_ref, first_ref, last_ref):
    cols, rows, channels = reg_ref.shape
    cells = cols * rows
    slots = arrived_ref.shape[0] * arrived_ref.shape[1]
    table = arrived_ref[...].reshape(slots, 384)
    band_row = cells_row(band_ref[...])
    r, c = iota((cells, cells), 0), iota((cells, cells), 1)
    band_col = jnp.sum(jnp.where(r == c, band_row, 0.0), -1, keepdims=True)
    earlier = (band_col == band_row) & (c < r)
    slot = jnp.sum(jnp.where(earlier, 1.0, 0.0), -1, keepdims=True)
    target = (band_col * 16.0 + slot * 4.0).astype(jnp.int32)
    lane = iota((cells, slots), 1) - target
    for part in range(channels // 128):
        take = jnp.where(lane == part, 1.0, 0.0).astype(jnp.bfloat16)
        taken = dot(take, table)
        lanes = slice(part * 128, (part + 1) * 128)
        reg = reg_ref[:, :, lanes].astype(jnp.float32)
        for s in range(3):
            forced = taken[:, s * 128 : (s + 1) * 128]
            made = (reg + forced.reshape(cols, rows, 128)).astype(jnp.bfloat16)
            out_ref[:, s * rows : (s + 1) * rows, lanes] = made
            first_ref[s * rows : (s + 1) * rows, lanes] = made[0]
            last_ref[s * rows : (s + 1) * rows, lanes] = made[cols - 1]


def make_inputs(arrived, band, reg):
    cols, rows, channels = reg.shape
    shapes = [(cols, 3 * rows, channels), (3 * rows, channels), (3 * rows, channels)]
    return pl.pallas_call(
        inputs_kernel,
        out_shape=[jax.ShapeDtypeStruct(s, jnp.bfloat16) for s in shapes],
        in_specs=[ON_CHIP] * 3,
        out_specs=[ON_CHIP] * 3,
        compiler_params=pltpu.CompilerParams(vmem_limit_bytes=6 * MIB),
        name="inputs",
    )(arrived, band, reg)


def row_shifts(x, rows):
    wide = x.astype(jnp.float32)
    total = x.shape[0]
    row = iota((total, 1), 0) % rows
    low = jnp.where(row > 0, pltpu.roll(wide, 1, 0), 0.0).astype(jnp.bfloat16)
    high = jnp.where(row < rows - 1, pltpu.roll(wide, total - 1, 0), 0.0).astype(jnp.bfloat16)
    return low, x, high


def inner_kernel(x_ref, taps_ref, conv_hbm_ref, sum_ref, after_ref, held_ref, sems):
    copies = [
        pltpu.make_async_copy(
            conv_hbm_ref.at[pl.ds(FETCHED, 6 - FETCHED)], held_ref, sems.at[0]
        ),
        pltpu.make_async_copy(conv_hbm_ref.at[pl.ds(6, 3)], after_ref, sems.at[1]),
    ]
    for copy in copies:
        copy.start()
    cols, slab, channels = x_ref.shape
    cells = cols * slab
    shifts = row_shifts(x_ref[...].reshape(cells, channels), slab // 3)
    sums = [None] * 3
    for tap in range(9):
        if tap == FETCHED:
            copies[0].wait()
        if tap == 6:
            copies[1].wait()
        if tap < FETCHED:
            w = taps_ref[tap]
        elif tap < 6:
            w = held_ref[tap - FETCHED]
        else:
            w = after_ref[tap - 6]
        x = shifts[tap % 3]
        x = (x[: cells - slab], x, x[slab:])[tap // 3]
        one = dot(x, w)
        sums[tap // 3] = one if sums[tap // 3] is None else sums[tap // 3] + one
    before, middle, after = sums
    sum_ref[:slab] = middle[:slab] + after[:slab]
    sum_ref[slab : cells - slab] = middle[slab : cells - slab] + before[: cells - 2 * slab] + after[slab:]
    sum_ref[cells - slab :] = middle[cells - slab :] + before[cells - 2 * slab :]


def convolve_inner(x, taps, conv_w):
    cols, slab, channels = x.shape
    return pl.pallas_call(
        inner_kernel,
        out_shape=[
            jax.ShapeDtypeStruct((cols * slab, channels), jnp.float32),
            jax.ShapeDtypeStruct((3, channels, channels), taps.dtype),
        ],
        in_specs=[ON_CHIP] * 2 + [pl.BlockSpec(memory_space=pltpu.HBM)],
        out_specs=[ON_CHIP] * 2,
        scratch_shapes=[
            pltpu.VMEM((6 - FETCHED, channels, channels), jnp.bfloat16),
            pltpu.SemaphoreType.DMA((2,)),
        ],
        compiler_params=pltpu.CompilerParams(vmem_limit_bytes=16 * MIB),
        name="convolve_inner",
    )(x, taps, conv_w)


def finish_kernel(x_ref, before_ref, after_ref, w_before_ref, w_after_ref, sum_ref, out_ref):
    cols, slab, channels = x_ref.shape
    rows = slab // 3
    sides = []
    for ref, w_ref in ((before_ref, w_before_ref), (after_ref, w_after_ref)):
        total = None
        for b, x in enumerate(row_shifts(ref[...], rows)):
            one = dot(x, w_ref[b])
            total = one if total is None else total + one
        sides.append(total)
    for col in range(cols):
        conv = sum_ref[col * slab : (col + 1) * slab]
        if col == 0:
            conv = conv + sides[0]
        if col == cols - 1:
            conv = conv + sides[1]
        result = x_ref[col].astype(jnp.float32) + conv / (1.0 + jnp.exp(-conv))
        result = result.astype(jnp.bfloat16)
        for s in range(3):
            out_ref[s, col] = result[s * rows : (s + 1) * rows]


def convolve_finish(x, before, after, w_before, w_after, total):
    cols, slab, channels = x.shape
    shape = (3, cols, slab // 3, channels)
    return pl.pallas_call(
        finish_kernel,
        out_shape=jax.ShapeDtypeStruct(shape, jnp.bfloat16),
        in_specs=[ON_CHIP] * 6,
        out_specs=pl.BlockSpec(shape, lambda: (0, 0, 0, 0)),
        compiler_params=pltpu.CompilerParams(vmem_limit_bytes=8 * MIB),
        name="convolve_finish",
    )(x, before, after, w_before, w_after, total)


def neighbours(last, first, axis):
    count = lax.axis_size(axis)
    up = [(i, i + 1) for i in range(count - 1)]
    down = [(j, i) for i, j in up]
    return lax.ppermute(last, axis, up), lax.ppermute(first, axis, down)


def per_device(
    global_state,
    band_codes,
    norm_gain,
    w_query,
    w_key,
    w_value,
    w_out,
    reg_state,
    src_band,
    src_tok,
    w_bound,
    conv_w,
):
    ranks = lax.axis_size("tp")
    bands = lax.axis_size(BANDS)
    tokens, features = global_state.shape
    half = tokens // 2
    cell_band = src_band.reshape(src_tok.shape)

    up = [(i, (i + 1) % ranks) for i in range(ranks)]
    down = [(j, i) for i, j in up]
    last, first = make_edges(band_codes, in_hbm(global_state))
    before, after = neighbours(last, first, BANDS)
    last, w_query, w_key, w_value = lax.optimization_barrier((last, w_query, w_key, w_value))
    *weights, gain = load(in_hbm(norm_gain), [in_hbm(w) for w in (w_query, w_key, w_value)])
    w1, w3 = lax.ppermute(w_out, "tp", up), lax.ppermute(w_out, "tp", down)
    q, k, v = project(band_codes, [first, last], gain, weights, False)
    asked = ask(cell_band, src_tok, bands)
    q, w1, w3 = lax.optimization_barrier((q, w1, w3))
    middle = w_out.shape[0] // 2
    top, low = lax.ppermute(w1[:middle], "tp", up), lax.ppermute(w3[middle:], "tp", down)
    q, before, after = lax.optimization_barrier((q, before, after))
    k_halo, v_halo = project(band_codes, [before, after], gain, weights[1:], True)
    attended = attend(q, k, v, k_halo, v_halo, ranks, bands)
    attended, asked, top, low = lax.optimization_barrier((attended, asked, top, low))
    attended = [attended[0]] + [
        lax.ppermute(attended[d], "tp", [(i, (i + d) % ranks) for i in range(ranks)])
        for d in range(1, ranks)
    ]
    asked = lax.all_to_all(asked[:, None, :], BANDS, 0, 0, tiled=True)[:, 0, :]
    global_out, table = combine(band_codes, attended, [w_out, w1, w3, top, low], global_state, w_bound)
    send = serve(asked, table)
    conv_w, send = lax.optimization_barrier((conv_w, send))
    conv_w = in_hbm(conv_w)
    taps = fetch_taps(conv_w)
    arrived = lax.all_to_all(send, BANDS, 0, 0, tiled=True)
    taps, arrived = lax.optimization_barrier((taps, arrived))
    inputs, first, last = make_inputs(arrived, cell_band, reg_state)
    before, after = neighbours(last, first, CELLS)
    total, late = convolve_inner(inputs, taps, conv_w)
    return global_out, convolve_finish(inputs, before, after, taps, late, total)


def solution(mesh):
    placed = (
        P(("sec", "tile"), None),
        P(("sec", "tile")),
        P(),
        P(None, "tp"),
        P(None, "tp"),
        P(None, "tp"),
        P("tp", None),
        P(("sec", "tile", "tp"), None, None),
        P(("sec", "tile", "tp"), None, None),
        P(("sec", "tile", "tp"), None),
        P(),
        P(),
    )
    return jax.shard_map(
        per_device,
        mesh=mesh,
        in_specs=placed,
        out_specs=(
            P(None, ("sec", "tile", "tp"), None),
            P(None, ("sec", "tile", "tp"), None, None),
        ),
        check_vma=False,
    )
```

```python
import functools

import jax
import jax.numpy as jnp
from jax import lax
from jax.experimental import pallas as pl
from jax.experimental.pallas import tpu as pltpu
from jax.sharding import PartitionSpec as P

HD = 64
SIGNS = (0.0, 1.0, -1.0)
BANDS = ("sec", "tile")
CELLS = ("sec", "tile", "tp")
LOG2E = 1.4426950408889634
FETCHED = 5
MIB = 1024 * 1024
ON_CHIP = pl.BlockSpec(memory_space=pltpu.VMEM)
SCALARS = pl.BlockSpec(memory_space=pltpu.SMEM)

mix_band = 73856093
mix_token = 19349663
mix_feature = 83492791
mix_again = 668265261


def iota(shape, dim):
    return lax.broadcasted_iota(jnp.int32, shape, dim)


def in_hbm(x):
    return pltpu.with_memory_space_constraint(x, pltpu.HBM)


def dot(a, b):
    return jnp.dot(a, b, preferred_element_type=jnp.float32)


def dot_t(a, b):
    return lax.dot_general(a, b, (((1,), (1,)), ((), ())), preferred_element_type=jnp.float32)


def wiggle(code, first_token, rows, features):
    by_row = code * mix_band + (first_token + iota((rows, 1), 0)) * mix_token
    mixed = by_row + iota((1, features), 1) * mix_feature
    mixed = lax.bitwise_xor(mixed, lax.shift_right_arithmetic(mixed, jnp.full_like(mixed, 15)))
    mixed = mixed * mix_again
    mixed = lax.bitwise_xor(mixed, lax.shift_right_arithmetic(mixed, jnp.full_like(mixed, 13)))
    level = lax.bitwise_and(mixed, 1023).astype(jnp.float32)
    return (level - 511.5) * (0.5 / 295.6)


def edges_kernel(code_ref, x_ref, last_ref, first_ref, sems):
    half = x_ref.shape[0] // 2
    copies = [
        pltpu.make_async_copy(x_ref.at[pl.ds(half, half)], last_ref.at[pl.ds(0, half)], sems.at[0]),
        pltpu.make_async_copy(x_ref.at[pl.ds(0, half)], first_ref.at[pl.ds(0, half)], sems.at[1]),
    ]
    for copy in copies:
        copy.start()
    code = jnp.full((16, x_ref.shape[1]), code_ref[0], jnp.int32)
    lane = iota(code.shape, 1)
    shift = jnp.where(lane == 0, 16, jnp.where(lane == 1, 8, 0))
    digit = lax.bitwise_and(lax.shift_right_arithmetic(code, shift), 255)
    digit = digit.astype(jnp.float32).astype(jnp.bfloat16)
    last_ref[half:] = digit
    first_ref[half:] = digit
    for copy in copies:
        copy.wait()


def make_edges(code, x):
    tokens, features = x.shape
    shape = jax.ShapeDtypeStruct((tokens // 2 + 16, features), jnp.bfloat16)
    return pl.pallas_call(
        edges_kernel,
        out_shape=[shape, shape],
        in_specs=[SCALARS, pl.BlockSpec(memory_space=pltpu.HBM)],
        out_specs=[ON_CHIP] * 2,
        scratch_shapes=[pltpu.SemaphoreType.DMA((2,))],
        compiler_params=pltpu.CompilerParams(vmem_limit_bytes=2 * MIB),
        name="edges",
    )(code, x)


def load_kernel(gain_ref, *refs):
    *refs, row_ref, flat_ref, sems = refs
    count = len(refs) // 2
    pairs = [*zip(refs[:count], refs[count:]), (gain_ref, flat_ref)]
    copies = [pltpu.make_async_copy(a, b, sems.at[i]) for i, (a, b) in enumerate(pairs)]
    for copy in copies:
        copy.start()
    for copy in copies:
        copy.wait()
    row_ref[...] = flat_ref[...].astype(jnp.float32).reshape(row_ref.shape)


def load(gain, weights):
    shapes = [jax.ShapeDtypeStruct(w.shape, w.dtype) for w in weights]
    shapes.append(jax.ShapeDtypeStruct((1, gain.shape[0]), jnp.float32))
    count = len(weights) + 1
    return pl.pallas_call(
        load_kernel,
        out_shape=shapes,
        in_specs=[pl.BlockSpec(memory_space=pltpu.HBM)] * count,
        out_specs=[ON_CHIP] * count,
        scratch_shapes=[pltpu.VMEM(gain.shape, gain.dtype), pltpu.SemaphoreType.DMA((count,))],
        compiler_params=pltpu.CompilerParams(vmem_limit_bytes=2 * MIB),
        name="load",
    )(gain, *weights)


def project_kernel(code_ref, early_ref, late_ref, gain_ref, *refs, halo):
    *refs, both_ref, inv_ref = refs
    step = pl.program_id(0)
    rows = early_ref.shape[0] - 16
    if halo:
        first = (1 - step) * rows
        digits = jnp.where(
            step == 0, early_ref[rows : rows + 16, 0:128], late_ref[rows : rows + 16, 0:128]
        ).astype(jnp.float32)[0:1]
        lane = iota((1, 128), 1)
        place = jnp.where(lane == 0, 65536.0, jnp.where(lane == 1, 256.0, 1.0))
        code = jnp.sum(jnp.where(lane < 3, digits * place, 0.0), -1, keepdims=True)
        code = code.astype(jnp.int32)
    else:
        first = step * rows
        code = jnp.full((1, 1), code_ref[0], jnp.int32)
    weights, outs = refs[: len(refs) // 2], refs[len(refs) // 2 :]
    features = both_ref.shape[1]
    gain = gain_ref[...]
    chunk, block = 16, 128
    for at in range(0, rows, block):
        for r in range(at, at + block, chunk):
            x = jnp.where(step == 0, early_ref[r : r + chunk], late_ref[r : r + chunk])
            x = x.astype(jnp.float32)
            p = wiggle(code, first + r, chunk, features)
            place = 2 * at + (r - at)
            both_ref[place : place + chunk] = (x * gain).astype(jnp.bfloat16)
            both_ref[place + block : place + block + chunk] = (p * gain).astype(jnp.bfloat16)
            for s, sign in enumerate(SIGNS):
                state = x if sign == 0.0 else (x + p if sign > 0 else x - p)
                mean = jnp.sum(state * state, -1, keepdims=True) * (1.0 / features)
                inv_ref[s, r : r + chunk] = lax.rsqrt(mean + 1e-06)
        here = slice(at, at + block)
        there = pl.ds(pl.multiple_of(step * rows + at, block), block)
        for index, (w_ref, out_ref) in enumerate(zip(weights, outs)):
            scale = HD**-0.5 * LOG2E if (index == 0 and not halo) else 1.0
            made = dot(both_ref[2 * at : 2 * at + 2 * block], w_ref[...])
            base, diff = made[:block], made[block:]
            for s, sign in enumerate(SIGNS):
                full = base if sign == 0.0 else (base + diff if sign > 0 else base - diff)
                out_ref[s, there] = (full * (inv_ref[s, here] * scale)).astype(jnp.bfloat16)


def project(code, arrays, gain, weights, halo):
    features = gain.shape[1]
    cols = weights[0].shape[1]
    tokens = 2 * (arrays[0].shape[0] - 16)
    specs = [ON_CHIP for a in arrays]
    rows = tokens // 2
    return pl.pallas_call(
        functools.partial(project_kernel, halo=halo),
        out_shape=[jax.ShapeDtypeStruct((3, tokens, cols), jnp.bfloat16) for _ in weights],
        grid=(2,),
        in_specs=[SCALARS]
        + specs
        + [ON_CHIP]
        + [ON_CHIP for w in weights],
        out_specs=[ON_CHIP for _ in weights],
        scratch_shapes=[
            pltpu.VMEM((2 * rows, features), jnp.bfloat16),
            pltpu.VMEM((3, rows, 1), jnp.float32),
        ],
        compiler_params=pltpu.CompilerParams(vmem_limit_bytes=12 * MIB),
        name="project_halo" if halo else "project_own",
    )(code, *arrays, gain, *weights)


def attend_kernel(q_ref, k_ref, v_ref, k_halo_ref, v_halo_ref, *refs, bands):
    *out_refs, held_ref = refs
    tokens, cols = q_ref.shape[1:]
    step = pl.program_id(0)
    half = tokens // 2
    band = lax.axis_index(BANDS)
    left = band > 0
    right = band < bands - 1
    k = k_ref[step]
    v = v_ref[step]
    row = iota((tokens, 1), 0)
    there = jnp.where(row < half, left.astype(jnp.int32), right.astype(jnp.int32)) > 0
    k_halo = jnp.where(there, k_halo_ref[step], k)
    one = there.astype(jnp.bfloat16)
    v_halo = v_halo_ref[step] * one
    block, pair = half, 2 * HD
    which = iota((1, pair), 1) // HD
    work = [(head, part) for head in range(cols // HD) for part in range(tokens // block)]

    def lanes(head):
        return slice(head // 2 * pair, (head // 2 + 1) * pair)

    def scores(head, part):
        q = q_ref[step, part * block : (part + 1) * block, lanes(head)]
        q = jnp.where(which == head % 2, q, jnp.zeros_like(q))
        return dot_t(q, k[:, lanes(head)]), dot_t(q, k_halo[:, lanes(head)])

    first = {}
    own, far = scores(*work[0])
    for index, (head, part) in enumerate(work):
        later = scores(*work[index + 1]) if index + 1 < len(work) else (None, None)
        mine = which == head % 2
        top = jnp.maximum(jnp.max(own, -1, keepdims=True), jnp.max(far, -1, keepdims=True))
        own = jnp.exp2(own - top).astype(jnp.bfloat16)
        far = jnp.exp2(far - top).astype(jnp.bfloat16)
        v_own, v_far = v[:, lanes(head)], v_halo[:, lanes(head)]
        v_own = jnp.where(mine, v_own, jnp.ones_like(v_own))
        v_far = jnp.where(mine, v_far, jnp.broadcast_to(one, v_far.shape))
        acc = dot(own, v_own) + dot(far, v_far)
        made = acc / pltpu.roll(acc, HD, 1)
        if head % 2 == 0:
            first[part] = made
        else:
            both = jnp.where(mine, made, first[part]).astype(jnp.bfloat16)
            held_ref[part * block : (part + 1) * block, lanes(head)] = both
        own, far = later
    ranks = len(out_refs)
    quarter = tokens // ranks
    rank = lax.axis_index("tp")
    for distance, out_ref in enumerate(out_refs):
        first = pl.multiple_of(lax.rem(rank + distance, ranks) * quarter, quarter)
        mine = pl.ds(pl.multiple_of(step * quarter, quarter), quarter)
        out_ref[mine, :] = held_ref[pl.ds(first, quarter), :]


def attend(q, k, v, k_halo, v_halo, ranks, bands):
    forwards, tokens, cols = q.shape
    quarter = tokens // ranks
    return pl.pallas_call(
        functools.partial(attend_kernel, bands=bands),
        out_shape=[jax.ShapeDtypeStruct((forwards * quarter, cols), jnp.bfloat16)] * ranks,
        grid=(forwards,),
        in_specs=[ON_CHIP] * 5,
        out_specs=[ON_CHIP] * ranks,
        scratch_shapes=[pltpu.VMEM((tokens, cols), jnp.bfloat16)],
        compiler_params=pltpu.CompilerParams(vmem_limit_bytes=14 * MIB),
        name="attend",
    )(q, k, v, k_halo, v_halo)


def cells_row(x):
    cols, rows = x.shape
    cells = cols * rows
    spread = (iota((rows, cells), 1) % rows == iota((rows, cells), 0)).astype(jnp.float32)
    wide = dot(x.astype(jnp.float32).astype(jnp.bfloat16), spread.astype(jnp.bfloat16))
    mine = iota((cols, cells), 1) // rows == iota((cols, cells), 0)
    return jnp.sum(jnp.where(mine, wide, 0.0), 0, keepdims=True)


def ask_kernel(band_ref, tok_ref, ask_ref):
    bands = ask_ref.shape[0]
    named = cells_row(band_ref[...])
    token = cells_row(tok_ref[...])
    cells = named.shape[1]
    match = (named.astype(jnp.int32) == iota((bands, cells), 0)).astype(jnp.float32)
    before = (iota((cells, cells), 0) < iota((cells, cells), 1)).astype(jnp.float32)
    slot = dot(match.astype(jnp.bfloat16), before.astype(jnp.bfloat16))
    lanes = iota((bands, cells), 1)
    asked = jnp.zeros((bands, cells), jnp.float32)
    for s in range(4):
        hit = jnp.where(slot == s, match, 0.0)
        token_s = jnp.sum(hit * (token + 1.0), -1, keepdims=True) - 1.0
        asked = jnp.where(lanes == s, token_s, asked)
    ask_ref[...] = asked[:, :4].astype(jnp.int32)


def ask(band, tok, bands):
    return pl.pallas_call(
        ask_kernel,
        out_shape=jax.ShapeDtypeStruct((bands, 4), jnp.int32),
        in_specs=[ON_CHIP] * 2,
        out_specs=ON_CHIP,
        compiler_params=pltpu.CompilerParams(vmem_limit_bytes=4 * MIB),
        name="ask",
    )(band, tok)


def fetch_kernel(conv_hbm_ref, taps_ref, sem):
    copy = pltpu.make_async_copy(conv_hbm_ref.at[pl.ds(0, FETCHED)], taps_ref, sem)
    copy.start()
    copy.wait()


def fetch_taps(conv_w):
    return pl.pallas_call(
        fetch_kernel,
        out_shape=jax.ShapeDtypeStruct((FETCHED, *conv_w.shape[1:]), conv_w.dtype),
        in_specs=[pl.BlockSpec(memory_space=pltpu.HBM)],
        out_specs=ON_CHIP,
        scratch_shapes=[pltpu.SemaphoreType.DMA(())],
        compiler_params=pltpu.CompilerParams(vmem_limit_bytes=2 * MIB),
        name="fetch",
    )(conv_w)


def pick_rows(asked, rows, cells):
    bands = asked.shape[0]
    spread = (iota((rows, bands), 0) // 16 == iota((rows, bands), 1)).astype(jnp.float32)
    per_row = dot(spread.astype(jnp.bfloat16), asked.astype(jnp.float32).astype(jnp.bfloat16))
    r = iota((rows, 1), 0)
    mine = iota((rows, 4), 1) == (r // 4) % 4
    token_r = jnp.sum(jnp.where(mine, per_row, 0.0), -1, keepdims=True).astype(jnp.int32)
    target = jnp.where(token_r >= 0, (r % 4) * cells + token_r, -1)
    return (iota((rows, 4 * cells), 1) == target).astype(jnp.float32).astype(jnp.bfloat16)


def combine_kernel(code_ref, att0_ref, att1_ref, att2_ref, att3_ref, w0_ref, w1_ref, w3_ref, top_ref, low_ref, x_ref, w_bound_ref, out_ref, table_ref, own_ref, held_ref, bound_ref, sems):
    cols = att0_ref.shape[1]
    half = cols // 2
    features = x_ref.shape[1]
    quarter = out_ref.shape[1]
    rank = lax.axis_index("tp")
    rows = pl.ds(pl.multiple_of(rank * quarter, quarter), quarter)
    pairs = [
        (w0_ref, held_ref.at[pl.ds(0, cols)]),
        (w1_ref, held_ref.at[pl.ds(cols, cols)]),
        (w3_ref, held_ref.at[pl.ds(2 * cols, cols)]),
        (top_ref, held_ref.at[pl.ds(3 * cols, half)]),
        (low_ref, held_ref.at[pl.ds(3 * cols + half, half)]),
        (x_ref.at[rows], own_ref),
        (w_bound_ref, bound_ref),
    ]
    copies = [pltpu.make_async_copy(a, b, sems.at[i]) for i, (a, b) in enumerate(pairs)]
    for copy in copies:
        copy.start()
    code = jnp.full((1, 1), code_ref[0], jnp.int32)
    p = wiggle(code, rank * quarter, quarter, features)
    copies[0].wait()
    total = dot(att0_ref[...], held_ref[:cols])
    copies[1].wait()
    total = total + dot(att1_ref[...], held_ref[cols : 2 * cols])
    copies[2].wait()
    total = total + dot(att3_ref[...], held_ref[2 * cols : 3 * cols])
    copies[3].wait()
    copies[4].wait()
    total = total + dot(att2_ref[...], held_ref[3 * cols :])
    copies[5].wait()
    x = own_ref[...].astype(jnp.float32)
    made = []
    for s, sign in enumerate(SIGNS):
        part = x if sign == 0.0 else (x + p if sign > 0 else x - p)
        part = (part + total[s * quarter : (s + 1) * quarter]).astype(jnp.bfloat16)
        out_ref[s] = part
        made.append(part)
    copies[6].wait()
    forced = dot(jnp.concatenate(made, 0), bound_ref[...]).astype(jnp.bfloat16)
    for part in range(forced.shape[1] // 128):
        for s in range(3):
            table_ref[part * quarter : (part + 1) * quarter, s * 128 : (s + 1) * 128] = forced[
                s * quarter : (s + 1) * quarter, part * 128 : (part + 1) * 128
            ]


def combine(code, att, w_outs, x, w_bound):
    quarter = att[0].shape[0] // 3
    shape = (3, quarter, x.shape[1])
    table = (quarter * w_bound.shape[1] // 128, 384)
    far = [in_hbm(a) for a in (*w_outs, x, w_bound)]
    return pl.pallas_call(
        combine_kernel,
        out_shape=[jax.ShapeDtypeStruct(s, jnp.bfloat16) for s in (shape, table)],
        in_specs=[SCALARS]
        + [ON_CHIP for a in att]
        + [pl.BlockSpec(memory_space=pltpu.HBM)] * len(far),
        out_specs=[pl.BlockSpec(shape, lambda: (0, 0, 0)), ON_CHIP],
        scratch_shapes=[
            pltpu.VMEM((quarter, x.shape[1]), jnp.bfloat16),
            pltpu.VMEM((len(att) * att[0].shape[1], x.shape[1]), jnp.bfloat16),
            pltpu.VMEM(w_bound.shape, jnp.bfloat16),
            pltpu.SemaphoreType.DMA((len(far),)),
        ],
        compiler_params=pltpu.CompilerParams(vmem_limit_bytes=16 * MIB),
        name="combine",
    )(code, *att, *far)


def serve_kernel(asked_ref, table_ref, send_ref):
    pick = pick_rows(asked_ref[...], send_ref.shape[0] * 16, table_ref.shape[0] // 4)
    send_ref[...] = dot(pick, table_ref[...]).astype(jnp.bfloat16).reshape(send_ref.shape)


def serve(asked, table):
    shape = (asked.shape[0], 16, table.shape[1])
    return pl.pallas_call(
        serve_kernel,
        out_shape=jax.ShapeDtypeStruct(shape, jnp.bfloat16),
        in_specs=[ON_CHIP] * 2,
        out_specs=pl.BlockSpec(shape, lambda: (0, 0, 0)),
        compiler_params=pltpu.CompilerParams(vmem_limit_bytes=8 * MIB),
        name="serve",
    )(asked, table)


def inputs_kernel(arrived_ref, band_ref, reg_ref, out_ref, first_ref, last_ref):
    cols, rows, channels = reg_ref.shape
    cells = cols * rows
    slots = arrived_ref.shape[0] * arrived_ref.shape[1]
    table = arrived_ref[...].reshape(slots, 384)
    band_row = cells_row(band_ref[...])
    r, c = iota((cells, cells), 0), iota((cells, cells), 1)
    band_col = jnp.sum(jnp.where(r == c, band_row, 0.0), -1, keepdims=True)
    earlier = (band_col == band_row) & (c < r)
    slot = jnp.sum(jnp.where(earlier, 1.0, 0.0), -1, keepdims=True)
    target = (band_col * 16.0 + slot * 4.0).astype(jnp.int32)
    lane = iota((cells, slots), 1) - target
    for part in range(channels // 128):
        take = jnp.where(lane == part, 1.0, 0.0).astype(jnp.bfloat16)
        taken = dot(take, table)
        lanes = slice(part * 128, (part + 1) * 128)
        reg = reg_ref[:, :, lanes].astype(jnp.float32)
        for s in range(3):
            forced = taken[:, s * 128 : (s + 1) * 128]
            made = (reg + forced.reshape(cols, rows, 128)).astype(jnp.bfloat16)
            out_ref[:, s * rows : (s + 1) * rows, lanes] = made
            first_ref[s * rows : (s + 1) * rows, lanes] = made[0]
            last_ref[s * rows : (s + 1) * rows, lanes] = made[cols - 1]


def make_inputs(arrived, band, reg):
    cols, rows, channels = reg.shape
    shapes = [(cols, 3 * rows, channels), (3 * rows, channels), (3 * rows, channels)]
    return pl.pallas_call(
        inputs_kernel,
        out_shape=[jax.ShapeDtypeStruct(s, jnp.bfloat16) for s in shapes],
        in_specs=[ON_CHIP] * 3,
        out_specs=[ON_CHIP] * 3,
        compiler_params=pltpu.CompilerParams(vmem_limit_bytes=6 * MIB),
        name="inputs",
    )(arrived, band, reg)


def row_shifts(x, rows):
    wide = x.astype(jnp.float32)
    total = x.shape[0]
    row = iota((total, 1), 0) % rows
    low = jnp.where(row > 0, pltpu.roll(wide, 1, 0), 0.0).astype(jnp.bfloat16)
    high = jnp.where(row < rows - 1, pltpu.roll(wide, total - 1, 0), 0.0).astype(jnp.bfloat16)
    return low, x, high


def inner_kernel(x_ref, taps_ref, conv_hbm_ref, sum_ref, after_ref, held_ref, sems):
    copies = [
        pltpu.make_async_copy(
            conv_hbm_ref.at[pl.ds(FETCHED, 6 - FETCHED)], held_ref, sems.at[0]
        ),
        pltpu.make_async_copy(conv_hbm_ref.at[pl.ds(6, 3)], after_ref, sems.at[1]),
    ]
    for copy in copies:
        copy.start()
    cols, slab, channels = x_ref.shape
    cells = cols * slab
    shifts = row_shifts(x_ref[...].reshape(cells, channels), slab // 3)
    sums = [None] * 3
    for tap in range(9):
        if tap == FETCHED:
            copies[0].wait()
        if tap == 6:
            copies[1].wait()
        if tap < FETCHED:
            w = taps_ref[tap]
        elif tap < 6:
            w = held_ref[tap - FETCHED]
        else:
            w = after_ref[tap - 6]
        x = shifts[tap % 3]
        x = (x[: cells - slab], x, x[slab:])[tap // 3]
        one = dot(x, w)
        sums[tap // 3] = one if sums[tap // 3] is None else sums[tap // 3] + one
    before, middle, after = sums
    sum_ref[:slab] = middle[:slab] + after[:slab]
    sum_ref[slab : cells - slab] = middle[slab : cells - slab] + before[: cells - 2 * slab] + after[slab:]
    sum_ref[cells - slab :] = middle[cells - slab :] + before[cells - 2 * slab :]


def convolve_inner(x, taps, conv_w):
    cols, slab, channels = x.shape
    return pl.pallas_call(
        inner_kernel,
        out_shape=[
            jax.ShapeDtypeStruct((cols * slab, channels), jnp.float32),
            jax.ShapeDtypeStruct((3, channels, channels), taps.dtype),
        ],
        in_specs=[ON_CHIP] * 2 + [pl.BlockSpec(memory_space=pltpu.HBM)],
        out_specs=[ON_CHIP] * 2,
        scratch_shapes=[
            pltpu.VMEM((6 - FETCHED, channels, channels), jnp.bfloat16),
            pltpu.SemaphoreType.DMA((2,)),
        ],
        compiler_params=pltpu.CompilerParams(vmem_limit_bytes=16 * MIB),
        name="convolve_inner",
    )(x, taps, conv_w)


def finish_kernel(x_ref, before_ref, after_ref, w_before_ref, w_after_ref, sum_ref, out_ref):
    cols, slab, channels = x_ref.shape
    rows = slab // 3
    sides = []
    for ref, w_ref in ((before_ref, w_before_ref), (after_ref, w_after_ref)):
        total = None
        for b, x in enumerate(row_shifts(ref[...], rows)):
            one = dot(x, w_ref[b])
            total = one if total is None else total + one
        sides.append(total)
    for col in range(cols):
        conv = sum_ref[col * slab : (col + 1) * slab]
        if col == 0:
            conv = conv + sides[0]
        if col == cols - 1:
            conv = conv + sides[1]
        result = x_ref[col].astype(jnp.float32) + conv / (1.0 + jnp.exp(-conv))
        result = result.astype(jnp.bfloat16)
        for s in range(3):
            out_ref[s, col] = result[s * rows : (s + 1) * rows]


def convolve_finish(x, before, after, w_before, w_after, total):
    cols, slab, channels = x.shape
    shape = (3, cols, slab // 3, channels)
    return pl.pallas_call(
        finish_kernel,
        out_shape=jax.ShapeDtypeStruct(shape, jnp.bfloat16),
        in_specs=[ON_CHIP] * 6,
        out_specs=pl.BlockSpec(shape, lambda: (0, 0, 0, 0)),
        compiler_params=pltpu.CompilerParams(vmem_limit_bytes=8 * MIB),
        name="convolve_finish",
    )(x, before, after, w_before, w_after, total)


def neighbours(last, first, axis):
    count = lax.axis_size(axis)
    up = [(i, i + 1) for i in range(count - 1)]
    down = [(j, i) for i, j in up]
    return lax.ppermute(last, axis, up), lax.ppermute(first, axis, down)


def per_device(
    global_state,
    band_codes,
    norm_gain,
    w_query,
    w_key,
    w_value,
    w_out,
    reg_state,
    src_band,
    src_tok,
    w_bound,
    conv_w,
):
    ranks = lax.axis_size("tp")
    bands = lax.axis_size(BANDS)
    tokens, features = global_state.shape
    half = tokens // 2
    cell_band = src_band.reshape(src_tok.shape)

    up = [(i, (i + 1) % ranks) for i in range(ranks)]
    down = [(j, i) for i, j in up]
    last, first = make_edges(band_codes, in_hbm(global_state))
    before, after = neighbours(last, first, BANDS)
    last, w_query, w_key, w_value = lax.optimization_barrier((last, w_query, w_key, w_value))
    *weights, gain = load(in_hbm(norm_gain), [in_hbm(w) for w in (w_query, w_key, w_value)])
    gain, w_out = lax.optimization_barrier((gain, w_out))
    w1, w3 = lax.ppermute(w_out, "tp", up), lax.ppermute(w_out, "tp", down)
    q, k, v = project(band_codes, [first, last], gain, weights, False)
    asked = ask(cell_band, src_tok, bands)
    q, before, after, asked = lax.optimization_barrier((q, before, after, asked))
    k_halo, v_halo = project(band_codes, [before, after], gain, weights[1:], True)
    k_halo, w1, w3 = lax.optimization_barrier((k_halo, w1, w3))
    middle = w_out.shape[0] // 2
    top, low = lax.ppermute(w1[:middle], "tp", up), lax.ppermute(w3[middle:], "tp", down)
    attended = attend(q, k, v, k_halo, v_halo, ranks, bands)
    attended, asked, top, low = lax.optimization_barrier((attended, asked, top, low))
    attended = [attended[0]] + [
        lax.ppermute(attended[d], "tp", [(i, (i + d) % ranks) for i in range(ranks)])
        for d in range(1, ranks)
    ]
    asked = lax.all_to_all(asked[:, None, :], BANDS, 0, 0, tiled=True)[:, 0, :]
    global_out, table = combine(band_codes, attended, [w_out, w1, w3, top, low], global_state, w_bound)
    send = serve(asked, table)
    conv_w, send = lax.optimization_barrier((conv_w, send))
    conv_w = in_hbm(conv_w)
    taps = fetch_taps(conv_w)
    arrived = lax.all_to_all(send, BANDS, 0, 0, tiled=True)
    taps, arrived = lax.optimization_barrier((taps, arrived))
    inputs, first, last = make_inputs(arrived, cell_band, reg_state)
    before, after = neighbours(last, first, CELLS)
    total, late = convolve_inner(inputs, taps, conv_w)
    return global_out, convolve_finish(inputs, before, after, taps, late, total)


def solution(mesh):
    placed = (
        P(("sec", "tile"), None),
        P(("sec", "tile")),
        P(),
        P(None, "tp"),
        P(None, "tp"),
        P(None, "tp"),
        P("tp", None),
        P(("sec", "tile", "tp"), None, None),
        P(("sec", "tile", "tp"), None, None),
        P(("sec", "tile", "tp"), None),
        P(),
        P(),
    )
    return jax.shard_map(
        per_device,
        mesh=mesh,
        in_specs=placed,
        out_specs=(
            P(None, ("sec", "tile", "tp"), None),
            P(None, ("sec", "tile", "tp"), None, None),
        ),
        check_vma=False,
    )
```

```python
import functools

import jax
import jax.numpy as jnp
from jax import lax
from jax.experimental import pallas as pl
from jax.experimental.pallas import tpu as pltpu
from jax.sharding import PartitionSpec as P

HD = 64
SIGNS = (0.0, 1.0, -1.0)
BANDS = ("sec", "tile")
CELLS = ("sec", "tile", "tp")
LOG2E = 1.4426950408889634
FETCHED = 5
MIB = 1024 * 1024
ON_CHIP = pl.BlockSpec(memory_space=pltpu.VMEM)
SCALARS = pl.BlockSpec(memory_space=pltpu.SMEM)

mix_band = 73856093
mix_token = 19349663
mix_feature = 83492791
mix_again = 668265261


def iota(shape, dim):
    return lax.broadcasted_iota(jnp.int32, shape, dim)


def in_hbm(x):
    return pltpu.with_memory_space_constraint(x, pltpu.HBM)


def dot(a, b):
    return jnp.dot(a, b, preferred_element_type=jnp.float32)


def dot_t(a, b):
    return lax.dot_general(a, b, (((1,), (1,)), ((), ())), preferred_element_type=jnp.float32)


def wiggle(code, first_token, rows, features):
    by_row = code * mix_band + (first_token + iota((rows, 1), 0)) * mix_token
    mixed = by_row + iota((1, features), 1) * mix_feature
    mixed = lax.bitwise_xor(mixed, lax.shift_right_arithmetic(mixed, jnp.full_like(mixed, 15)))
    mixed = mixed * mix_again
    mixed = lax.bitwise_xor(mixed, lax.shift_right_arithmetic(mixed, jnp.full_like(mixed, 13)))
    level = lax.bitwise_and(mixed, 1023).astype(jnp.float32)
    return (level - 511.5) * (0.5 / 295.6)


def edges_kernel(code_ref, x_ref, last_ref, first_ref, sems):
    half = x_ref.shape[0] // 2
    copies = [
        pltpu.make_async_copy(x_ref.at[pl.ds(half, half)], last_ref.at[pl.ds(0, half)], sems.at[0]),
        pltpu.make_async_copy(x_ref.at[pl.ds(0, half)], first_ref.at[pl.ds(0, half)], sems.at[1]),
    ]
    for copy in copies:
        copy.start()
    code = jnp.full((16, x_ref.shape[1]), code_ref[0], jnp.int32)
    lane = iota(code.shape, 1)
    shift = jnp.where(lane == 0, 16, jnp.where(lane == 1, 8, 0))
    digit = lax.bitwise_and(lax.shift_right_arithmetic(code, shift), 255)
    digit = digit.astype(jnp.float32).astype(jnp.bfloat16)
    last_ref[half:] = digit
    first_ref[half:] = digit
    for copy in copies:
        copy.wait()


def make_edges(code, x):
    tokens, features = x.shape
    shape = jax.ShapeDtypeStruct((tokens // 2 + 16, features), jnp.bfloat16)
    return pl.pallas_call(
        edges_kernel,
        out_shape=[shape, shape],
        in_specs=[SCALARS, pl.BlockSpec(memory_space=pltpu.HBM)],
        out_specs=[ON_CHIP] * 2,
        scratch_shapes=[pltpu.SemaphoreType.DMA((2,))],
        compiler_params=pltpu.CompilerParams(vmem_limit_bytes=2 * MIB),
        name="edges",
    )(code, x)


def load_kernel(gain_ref, *refs):
    *refs, row_ref, flat_ref, sems = refs
    count = len(refs) // 2
    pairs = [*zip(refs[:count], refs[count:]), (gain_ref, flat_ref)]
    copies = [pltpu.make_async_copy(a, b, sems.at[i]) for i, (a, b) in enumerate(pairs)]
    for copy in copies:
        copy.start()
    for copy in copies:
        copy.wait()
    row_ref[...] = flat_ref[...].astype(jnp.float32).reshape(row_ref.shape)


def load(gain, weights):
    shapes = [jax.ShapeDtypeStruct(w.shape, w.dtype) for w in weights]
    shapes.append(jax.ShapeDtypeStruct((1, gain.shape[0]), jnp.float32))
    count = len(weights) + 1
    return pl.pallas_call(
        load_kernel,
        out_shape=shapes,
        in_specs=[pl.BlockSpec(memory_space=pltpu.HBM)] * count,
        out_specs=[ON_CHIP] * count,
        scratch_shapes=[pltpu.VMEM(gain.shape, gain.dtype), pltpu.SemaphoreType.DMA((count,))],
        compiler_params=pltpu.CompilerParams(vmem_limit_bytes=2 * MIB),
        name="load",
    )(gain, *weights)


def project_kernel(code_ref, early_ref, late_ref, gain_ref, *refs, halo):
    *refs, both_ref, inv_ref = refs
    step = pl.program_id(0)
    rows = early_ref.shape[0] - 16
    if halo:
        first = (1 - step) * rows
        digits = jnp.where(
            step == 0, early_ref[rows : rows + 16, 0:128], late_ref[rows : rows + 16, 0:128]
        ).astype(jnp.float32)[0:1]
        lane = iota((1, 128), 1)
        place = jnp.where(lane == 0, 65536.0, jnp.where(lane == 1, 256.0, 1.0))
        code = jnp.sum(jnp.where(lane < 3, digits * place, 0.0), -1, keepdims=True)
        code = code.astype(jnp.int32)
    else:
        first = step * rows
        code = jnp.full((1, 1), code_ref[0], jnp.int32)
    weights, outs = refs[: len(refs) // 2], refs[len(refs) // 2 :]
    features = both_ref.shape[1]
    gain = gain_ref[...]
    chunk, block = 16, 128
    for at in range(0, rows, block):
        for r in range(at, at + block, chunk):
            x = jnp.where(step == 0, early_ref[r : r + chunk], late_ref[r : r + chunk])
            x = x.astype(jnp.float32)
            p = wiggle(code, first + r, chunk, features)
            place = 2 * at + (r - at)
            both_ref[place : place + chunk] = (x * gain).astype(jnp.bfloat16)
            both_ref[place + block : place + block + chunk] = (p * gain).astype(jnp.bfloat16)
            for s, sign in enumerate(SIGNS):
                state = x if sign == 0.0 else (x + p if sign > 0 else x - p)
                mean = jnp.sum(state * state, -1, keepdims=True) * (1.0 / features)
                inv_ref[s, r : r + chunk] = lax.rsqrt(mean + 1e-06)
        here = slice(at, at + block)
        there = pl.ds(pl.multiple_of(step * rows + at, block), block)
        for index, (w_ref, out_ref) in enumerate(zip(weights, outs)):
            scale = HD**-0.5 * LOG2E if (index == 0 and not halo) else 1.0
            made = dot(both_ref[2 * at : 2 * at + 2 * block], w_ref[...])
            base, diff = made[:block], made[block:]
            for s, sign in enumerate(SIGNS):
                full = base if sign == 0.0 else (base + diff if sign > 0 else base - diff)
                out_ref[s, there] = (full * (inv_ref[s, here] * scale)).astype(jnp.bfloat16)


def project(code, arrays, gain, weights, halo):
    features = gain.shape[1]
    cols = weights[0].shape[1]
    tokens = 2 * (arrays[0].shape[0] - 16)
    specs = [ON_CHIP for a in arrays]
    rows = tokens // 2
    return pl.pallas_call(
        functools.partial(project_kernel, halo=halo),
        out_shape=[jax.ShapeDtypeStruct((3, tokens, cols), jnp.bfloat16) for _ in weights],
        grid=(2,),
        in_specs=[SCALARS]
        + specs
        + [ON_CHIP]
        + [ON_CHIP for w in weights],
        out_specs=[ON_CHIP for _ in weights],
        scratch_shapes=[
            pltpu.VMEM((2 * rows, features), jnp.bfloat16),
            pltpu.VMEM((3, rows, 1), jnp.float32),
        ],
        compiler_params=pltpu.CompilerParams(vmem_limit_bytes=12 * MIB),
        name="project_halo" if halo else "project_own",
    )(code, *arrays, gain, *weights)


def attend_kernel(q_ref, k_ref, v_ref, k_halo_ref, v_halo_ref, *refs, bands):
    *out_refs, held_ref = refs
    tokens, cols = q_ref.shape[1:]
    step = pl.program_id(0)
    half = tokens // 2
    band = lax.axis_index(BANDS)
    left = band > 0
    right = band < bands - 1
    k = k_ref[step]
    v = v_ref[step]
    row = iota((tokens, 1), 0)
    there = jnp.where(row < half, left.astype(jnp.int32), right.astype(jnp.int32)) > 0
    k_halo = jnp.where(there, k_halo_ref[step], k)
    one = there.astype(jnp.bfloat16)
    v_halo = v_halo_ref[step] * one
    block, pair = half, 2 * HD
    which = iota((1, pair), 1) // HD
    work = [(head, part) for head in range(cols // HD) for part in range(tokens // block)]

    def lanes(head):
        return slice(head // 2 * pair, (head // 2 + 1) * pair)

    def scores(head, part):
        q = q_ref[step, part * block : (part + 1) * block, lanes(head)]
        q = jnp.where(which == head % 2, q, jnp.zeros_like(q))
        return dot_t(q, k[:, lanes(head)]), dot_t(q, k_halo[:, lanes(head)])

    first = {}
    own, far = scores(*work[0])
    for index, (head, part) in enumerate(work):
        later = scores(*work[index + 1]) if index + 1 < len(work) else (None, None)
        mine = which == head % 2
        top = jnp.maximum(jnp.max(own, -1, keepdims=True), jnp.max(far, -1, keepdims=True))
        own = jnp.exp2(own - top).astype(jnp.bfloat16)
        far = jnp.exp2(far - top).astype(jnp.bfloat16)
        v_own, v_far = v[:, lanes(head)], v_halo[:, lanes(head)]
        v_own = jnp.where(mine, v_own, jnp.ones_like(v_own))
        v_far = jnp.where(mine, v_far, jnp.broadcast_to(one, v_far.shape))
        acc = dot(own, v_own) + dot(far, v_far)
        made = acc / pltpu.roll(acc, HD, 1)
        if head % 2 == 0:
            first[part] = made
        else:
            both = jnp.where(mine, made, first[part]).astype(jnp.bfloat16)
            held_ref[part * block : (part + 1) * block, lanes(head)] = both
        own, far = later
    ranks = len(out_refs)
    quarter = tokens // ranks
    rank = lax.axis_index("tp")
    for distance, out_ref in enumerate(out_refs):
        first = pl.multiple_of(lax.rem(rank + distance, ranks) * quarter, quarter)
        mine = pl.ds(pl.multiple_of(step * quarter, quarter), quarter)
        out_ref[mine, :] = held_ref[pl.ds(first, quarter), :]


def attend(q, k, v, k_halo, v_halo, ranks, bands):
    forwards, tokens, cols = q.shape
    quarter = tokens // ranks
    return pl.pallas_call(
        functools.partial(attend_kernel, bands=bands),
        out_shape=[jax.ShapeDtypeStruct((forwards * quarter, cols), jnp.bfloat16)] * ranks,
        grid=(forwards,),
        in_specs=[ON_CHIP] * 5,
        out_specs=[ON_CHIP] * ranks,
        scratch_shapes=[pltpu.VMEM((tokens, cols), jnp.bfloat16)],
        compiler_params=pltpu.CompilerParams(vmem_limit_bytes=14 * MIB),
        name="attend",
    )(q, k, v, k_halo, v_halo)


def cells_row(x):
    cols, rows = x.shape
    cells = cols * rows
    spread = (iota((rows, cells), 1) % rows == iota((rows, cells), 0)).astype(jnp.float32)
    wide = dot(x.astype(jnp.float32).astype(jnp.bfloat16), spread.astype(jnp.bfloat16))
    mine = iota((cols, cells), 1) // rows == iota((cols, cells), 0)
    return jnp.sum(jnp.where(mine, wide, 0.0), 0, keepdims=True)


def ask_kernel(band_ref, tok_ref, ask_ref):
    bands = ask_ref.shape[0]
    named = cells_row(band_ref[...])
    token = cells_row(tok_ref[...])
    cells = named.shape[1]
    match = (named.astype(jnp.int32) == iota((bands, cells), 0)).astype(jnp.float32)
    before = (iota((cells, cells), 0) < iota((cells, cells), 1)).astype(jnp.float32)
    slot = dot(match.astype(jnp.bfloat16), before.astype(jnp.bfloat16))
    lanes = iota((bands, cells), 1)
    asked = jnp.zeros((bands, cells), jnp.float32)
    for s in range(4):
        hit = jnp.where(slot == s, match, 0.0)
        token_s = jnp.sum(hit * (token + 1.0), -1, keepdims=True) - 1.0
        asked = jnp.where(lanes == s, token_s, asked)
    ask_ref[...] = asked[:, :4].astype(jnp.int32)


def ask(band, tok, bands):
    return pl.pallas_call(
        ask_kernel,
        out_shape=jax.ShapeDtypeStruct((bands, 4), jnp.int32),
        in_specs=[ON_CHIP] * 2,
        out_specs=ON_CHIP,
        compiler_params=pltpu.CompilerParams(vmem_limit_bytes=4 * MIB),
        name="ask",
    )(band, tok)


def fetch_kernel(conv_hbm_ref, taps_ref, sem):
    copy = pltpu.make_async_copy(conv_hbm_ref.at[pl.ds(0, FETCHED)], taps_ref, sem)
    copy.start()
    copy.wait()


def fetch_taps(conv_w):
    return pl.pallas_call(
        fetch_kernel,
        out_shape=jax.ShapeDtypeStruct((FETCHED, *conv_w.shape[1:]), conv_w.dtype),
        in_specs=[pl.BlockSpec(memory_space=pltpu.HBM)],
        out_specs=ON_CHIP,
        scratch_shapes=[pltpu.SemaphoreType.DMA(())],
        compiler_params=pltpu.CompilerParams(vmem_limit_bytes=2 * MIB),
        name="fetch",
    )(conv_w)


def pick_rows(asked, rows, cells):
    bands = asked.shape[0]
    spread = (iota((rows, bands), 0) // 16 == iota((rows, bands), 1)).astype(jnp.float32)
    per_row = dot(spread.astype(jnp.bfloat16), asked.astype(jnp.float32).astype(jnp.bfloat16))
    r = iota((rows, 1), 0)
    mine = iota((rows, 4), 1) == (r // 4) % 4
    token_r = jnp.sum(jnp.where(mine, per_row, 0.0), -1, keepdims=True).astype(jnp.int32)
    target = jnp.where(token_r >= 0, (r % 4) * cells + token_r, -1)
    return (iota((rows, 4 * cells), 1) == target).astype(jnp.float32).astype(jnp.bfloat16)


def combine_kernel(code_ref, att0_ref, att1_ref, att2_ref, att3_ref, w0_ref, w1_ref, w3_ref, top_ref, low_ref, x_ref, w_bound_ref, out_ref, table_ref, own_ref, held_ref, bound_ref, sems):
    cols = att0_ref.shape[1]
    half = cols // 2
    features = x_ref.shape[1]
    quarter = out_ref.shape[1]
    rank = lax.axis_index("tp")
    rows = pl.ds(pl.multiple_of(rank * quarter, quarter), quarter)
    pairs = [
        (w0_ref, held_ref.at[pl.ds(0, cols)]),
        (w1_ref, held_ref.at[pl.ds(cols, cols)]),
        (w3_ref, held_ref.at[pl.ds(2 * cols, cols)]),
        (top_ref, held_ref.at[pl.ds(3 * cols, half)]),
        (low_ref, held_ref.at[pl.ds(3 * cols + half, half)]),
        (x_ref.at[rows], own_ref),
        (w_bound_ref, bound_ref),
    ]
    copies = [pltpu.make_async_copy(a, b, sems.at[i]) for i, (a, b) in enumerate(pairs)]
    for copy in copies:
        copy.start()
    code = jnp.full((1, 1), code_ref[0], jnp.int32)
    p = wiggle(code, rank * quarter, quarter, features)
    copies[0].wait()
    total = dot(att0_ref[...], held_ref[:cols])
    copies[1].wait()
    total = total + dot(att1_ref[...], held_ref[cols : 2 * cols])
    copies[2].wait()
    total = total + dot(att3_ref[...], held_ref[2 * cols : 3 * cols])
    copies[3].wait()
    copies[4].wait()
    total = total + dot(att2_ref[...], held_ref[3 * cols :])
    copies[5].wait()
    x = own_ref[...].astype(jnp.float32)
    made = []
    for s, sign in enumerate(SIGNS):
        part = x if sign == 0.0 else (x + p if sign > 0 else x - p)
        part = (part + total[s * quarter : (s + 1) * quarter]).astype(jnp.bfloat16)
        out_ref[s] = part
        made.append(part)
    copies[6].wait()
    forced = dot(jnp.concatenate(made, 0), bound_ref[...]).astype(jnp.bfloat16)
    for part in range(forced.shape[1] // 128):
        for s in range(3):
            table_ref[part * quarter : (part + 1) * quarter, s * 128 : (s + 1) * 128] = forced[
                s * quarter : (s + 1) * quarter, part * 128 : (part + 1) * 128
            ]


def combine(code, att, w_outs, x, w_bound):
    quarter = att[0].shape[0] // 3
    shape = (3, quarter, x.shape[1])
    table = (quarter * w_bound.shape[1] // 128, 384)
    far = [in_hbm(a) for a in (*w_outs, x, w_bound)]
    return pl.pallas_call(
        combine_kernel,
        out_shape=[jax.ShapeDtypeStruct(s, jnp.bfloat16) for s in (shape, table)],
        in_specs=[SCALARS]
        + [ON_CHIP for a in att]
        + [pl.BlockSpec(memory_space=pltpu.HBM)] * len(far),
        out_specs=[pl.BlockSpec(shape, lambda: (0, 0, 0)), ON_CHIP],
        scratch_shapes=[
            pltpu.VMEM((quarter, x.shape[1]), jnp.bfloat16),
            pltpu.VMEM((len(att) * att[0].shape[1], x.shape[1]), jnp.bfloat16),
            pltpu.VMEM(w_bound.shape, jnp.bfloat16),
            pltpu.SemaphoreType.DMA((len(far),)),
        ],
        compiler_params=pltpu.CompilerParams(vmem_limit_bytes=16 * MIB),
        name="combine",
    )(code, *att, *far)


def serve_kernel(asked_ref, table_ref, send_ref):
    pick = pick_rows(asked_ref[...], send_ref.shape[0] * 16, table_ref.shape[0] // 4)
    send_ref[...] = dot(pick, table_ref[...]).astype(jnp.bfloat16).reshape(send_ref.shape)


def serve(asked, table):
    shape = (asked.shape[0], 16, table.shape[1])
    return pl.pallas_call(
        serve_kernel,
        out_shape=jax.ShapeDtypeStruct(shape, jnp.bfloat16),
        in_specs=[ON_CHIP] * 2,
        out_specs=pl.BlockSpec(shape, lambda: (0, 0, 0)),
        compiler_params=pltpu.CompilerParams(vmem_limit_bytes=8 * MIB),
        name="serve",
    )(asked, table)


def inputs_kernel(arrived_ref, band_ref, reg_ref, out_ref, first_ref, last_ref):
    cols, rows, channels = reg_ref.shape
    cells = cols * rows
    slots = arrived_ref.shape[0] * arrived_ref.shape[1]
    table = arrived_ref[...].reshape(slots, 384)
    band_row = cells_row(band_ref[...])
    r, c = iota((cells, cells), 0), iota((cells, cells), 1)
    band_col = jnp.sum(jnp.where(r == c, band_row, 0.0), -1, keepdims=True)
    earlier = (band_col == band_row) & (c < r)
    slot = jnp.sum(jnp.where(earlier, 1.0, 0.0), -1, keepdims=True)
    target = (band_col * 16.0 + slot * 4.0).astype(jnp.int32)
    lane = iota((cells, slots), 1) - target
    for part in range(channels // 128):
        take = jnp.where(lane == part, 1.0, 0.0).astype(jnp.bfloat16)
        taken = dot(take, table)
        lanes = slice(part * 128, (part + 1) * 128)
        reg = reg_ref[:, :, lanes].astype(jnp.float32)
        for s in range(3):
            forced = taken[:, s * 128 : (s + 1) * 128]
            made = (reg + forced.reshape(cols, rows, 128)).astype(jnp.bfloat16)
            out_ref[:, s * rows : (s + 1) * rows, lanes] = made
            first_ref[s * rows : (s + 1) * rows, lanes] = made[0]
            last_ref[s * rows : (s + 1) * rows, lanes] = made[cols - 1]


def make_inputs(arrived, band, reg):
    cols, rows, channels = reg.shape
    shapes = [(cols, 3 * rows, channels), (3 * rows, channels), (3 * rows, channels)]
    return pl.pallas_call(
        inputs_kernel,
        out_shape=[jax.ShapeDtypeStruct(s, jnp.bfloat16) for s in shapes],
        in_specs=[ON_CHIP] * 3,
        out_specs=[ON_CHIP] * 3,
        compiler_params=pltpu.CompilerParams(vmem_limit_bytes=6 * MIB),
        name="inputs",
    )(arrived, band, reg)


def row_shifts(x, rows):
    wide = x.astype(jnp.float32)
    total = x.shape[0]
    row = iota((total, 1), 0) % rows
    low = jnp.where(row > 0, pltpu.roll(wide, 1, 0), 0.0).astype(jnp.bfloat16)
    high = jnp.where(row < rows - 1, pltpu.roll(wide, total - 1, 0), 0.0).astype(jnp.bfloat16)
    return low, x, high


def inner_kernel(x_ref, taps_ref, conv_hbm_ref, sum_ref, after_ref, held_ref, sems):
    copies = [
        pltpu.make_async_copy(
            conv_hbm_ref.at[pl.ds(FETCHED, 6 - FETCHED)], held_ref, sems.at[0]
        ),
        pltpu.make_async_copy(conv_hbm_ref.at[pl.ds(6, 3)], after_ref, sems.at[1]),
    ]
    for copy in copies:
        copy.start()
    cols, slab, channels = x_ref.shape
    cells = cols * slab
    shifts = row_shifts(x_ref[...].reshape(cells, channels), slab // 3)
    sums = [None] * 3
    for tap in range(9):
        if tap == FETCHED:
            copies[0].wait()
        if tap == 6:
            copies[1].wait()
        if tap < FETCHED:
            w = taps_ref[tap]
        elif tap < 6:
            w = held_ref[tap - FETCHED]
        else:
            w = after_ref[tap - 6]
        x = shifts[tap % 3]
        x = (x[: cells - slab], x, x[slab:])[tap // 3]
        one = dot(x, w)
        sums[tap // 3] = one if sums[tap // 3] is None else sums[tap // 3] + one
    before, middle, after = sums
    sum_ref[:slab] = middle[:slab] + after[:slab]
    sum_ref[slab : cells - slab] = middle[slab : cells - slab] + before[: cells - 2 * slab] + after[slab:]
    sum_ref[cells - slab :] = middle[cells - slab :] + before[cells - 2 * slab :]


def convolve_inner(x, taps, conv_w):
    cols, slab, channels = x.shape
    return pl.pallas_call(
        inner_kernel,
        out_shape=[
            jax.ShapeDtypeStruct((cols * slab, channels), jnp.float32),
            jax.ShapeDtypeStruct((3, channels, channels), taps.dtype),
        ],
        in_specs=[ON_CHIP] * 2 + [pl.BlockSpec(memory_space=pltpu.HBM)],
        out_specs=[ON_CHIP] * 2,
        scratch_shapes=[
            pltpu.VMEM((6 - FETCHED, channels, channels), jnp.bfloat16),
            pltpu.SemaphoreType.DMA((2,)),
        ],
        compiler_params=pltpu.CompilerParams(vmem_limit_bytes=16 * MIB),
        name="convolve_inner",
    )(x, taps, conv_w)


def finish_kernel(x_ref, before_ref, after_ref, w_before_ref, w_after_ref, sum_ref, out_ref):
    cols, slab, channels = x_ref.shape
    rows = slab // 3
    sides = []
    for ref, w_ref in ((before_ref, w_before_ref), (after_ref, w_after_ref)):
        total = None
        for b, x in enumerate(row_shifts(ref[...], rows)):
            one = dot(x, w_ref[b])
            total = one if total is None else total + one
        sides.append(total)
    for col in range(cols):
        conv = sum_ref[col * slab : (col + 1) * slab]
        if col == 0:
            conv = conv + sides[0]
        if col == cols - 1:
            conv = conv + sides[1]
        result = x_ref[col].astype(jnp.float32) + conv / (1.0 + jnp.exp(-conv))
        result = result.astype(jnp.bfloat16)
        for s in range(3):
            out_ref[s, col] = result[s * rows : (s + 1) * rows]


def convolve_finish(x, before, after, w_before, w_after, total):
    cols, slab, channels = x.shape
    shape = (3, cols, slab // 3, channels)
    return pl.pallas_call(
        finish_kernel,
        out_shape=jax.ShapeDtypeStruct(shape, jnp.bfloat16),
        in_specs=[ON_CHIP] * 6,
        out_specs=pl.BlockSpec(shape, lambda: (0, 0, 0, 0)),
        compiler_params=pltpu.CompilerParams(vmem_limit_bytes=8 * MIB),
        name="convolve_finish",
    )(x, before, after, w_before, w_after, total)


def neighbours(last, first, axis):
    count = lax.axis_size(axis)
    up = [(i, i + 1) for i in range(count - 1)]
    down = [(j, i) for i, j in up]
    return lax.ppermute(last, axis, up), lax.ppermute(first, axis, down)


def per_device(
    global_state,
    band_codes,
    norm_gain,
    w_query,
    w_key,
    w_value,
    w_out,
    reg_state,
    src_band,
    src_tok,
    w_bound,
    conv_w,
):
    ranks = lax.axis_size("tp")
    bands = lax.axis_size(BANDS)
    tokens, features = global_state.shape
    half = tokens // 2
    cell_band = src_band.reshape(src_tok.shape)

    up = [(i, (i + 1) % ranks) for i in range(ranks)]
    down = [(j, i) for i, j in up]
    last, first = make_edges(band_codes, in_hbm(global_state))
    before, after = neighbours(last, first, BANDS)
    last, w_query, w_key, w_value = lax.optimization_barrier((last, w_query, w_key, w_value))
    *weights, gain = load(in_hbm(norm_gain), [in_hbm(w) for w in (w_query, w_key, w_value)])
    w1, w3 = lax.ppermute(w_out, "tp", up), lax.ppermute(w_out, "tp", down)
    q, k, v = project(band_codes, [first, last], gain, weights, False)
    asked = ask(cell_band, src_tok, bands)
    q, w1, w3 = lax.optimization_barrier((q, w1, w3))
    middle = w_out.shape[0] // 2
    top, low = lax.ppermute(w1[:middle], "tp", up), lax.ppermute(w3[middle:], "tp", down)
    q, before, after = lax.optimization_barrier((q, before, after))
    k_halo, v_halo = project(band_codes, [before, after], gain, weights[1:], True)
    attended = attend(q, k, v, k_halo, v_halo, ranks, bands)
    attended, asked, top, low = lax.optimization_barrier((attended, asked, top, low))
    att2, att1, att3 = (
        lax.ppermute(attended[d], "tp", [(i, (i + d) % ranks) for i in range(ranks)])
        for d in (2, 1, 3)
    )
    attended = [attended[0], att1, att2, att3]
    asked = lax.all_to_all(asked[:, None, :], BANDS, 0, 0, tiled=True)[:, 0, :]
    global_out, table = combine(band_codes, attended, [w_out, w1, w3, top, low], global_state, w_bound)
    send = serve(asked, table)
    conv_w, send = lax.optimization_barrier((conv_w, send))
    conv_w = in_hbm(conv_w)
    taps = fetch_taps(conv_w)
    arrived = lax.all_to_all(send, BANDS, 0, 0, tiled=True)
    taps, arrived = lax.optimization_barrier((taps, arrived))
    inputs, first, last = make_inputs(arrived, cell_band, reg_state)
    before, after = neighbours(last, first, CELLS)
    total, late = convolve_inner(inputs, taps, conv_w)
    return global_out, convolve_finish(inputs, before, after, taps, late, total)


def solution(mesh):
    placed = (
        P(("sec", "tile"), None),
        P(("sec", "tile")),
        P(),
        P(None, "tp"),
        P(None, "tp"),
        P(None, "tp"),
        P("tp", None),
        P(("sec", "tile", "tp"), None, None),
        P(("sec", "tile", "tp"), None, None),
        P(("sec", "tile", "tp"), None),
        P(),
        P(),
    )
    return jax.shard_map(
        per_device,
        mesh=mesh,
        in_specs=placed,
        out_specs=(
            P(None, ("sec", "tile", "tp"), None),
            P(None, ("sec", "tile", "tp"), None, None),
        ),
        check_vma=False,
    )
```
